32 devices in a mesh: dp: 8 (over z, x), hid: 2 (over y), mp: 2 (over core).
Axes of the slice: x: 2, y: 2, z: 4, core: 2. Of those that a mesh axis runs over, the one named last changes fastest.
Arguments:
- tokens: bfloat16 [32768, 768], P(('dp', 'hid', 'mp')), may hold values from -6 to 6
- segment_ids: int32 [32768], P(('dp', 'hid', 'mp')), may hold values from 0 to 3, as said below
- cluster_ids: int32 [12, 32768], P(None, ('dp', 'hid', 'mp')), may hold values from 0 to 99, as said below
- cotangent: bfloat16 [32768, 768], P(('dp', 'hid', 'mp')), may hold values from -6 to 6
- first_gain: float32 [768], replicated, may hold values from 0.5 to 1.5
- first_shift: float32 [768], replicated, may hold values from -2 to 2
- w_query: float32 [768, 768], P(('dp', 'hid', 'mp')), may hold values from -0.875 to 0.875
- b_query: float32 [768], replicated, may hold values from -5 to 5
- w_key: float32 [768, 768], P(('dp', 'hid', 'mp')), may hold values from -0.21875 to 0.21875
- w_value: float32 [768, 768], P(('dp', 'hid', 'mp')), may hold values from -0.21875 to 0.21875
- b_value: float32 [768], replicated, may hold values from -0.6 to 0.6
- w_out: float32 [768, 768], P(('dp', 'hid', 'mp')), may hold values from -1.25 to 1.25
- b_out: float32 [768], replicated, may hold values from -2 to 2
- second_gain: float32 [768], replicated, may hold values from 0.5 to 1.5
- second_shift: float32 [768], replicated, may hold values from -2 to 2
- w_up: float32 [768, 3072], P('dp', ('hid', 'mp')), may hold values from -0.21875 to 0.21875
- b_up: float32 [3072], replicated, may hold values from -2 to 2
- w_down: float32 [3072, 768], P(('hid', 'mp'), 'dp'), may hold values from -0.109375 to 0.109375
- b_down: float32 [768], replicated, may hold values from -2 to 2
Outputs:
- output: bfloat16 [32768, 768], P(('dp', 'hid', 'mp'))
- tokens_grad: bfloat16 [32768, 768], P(('dp', 'hid', 'mp'))
- first_gain_grad: float32 [768], replicated
- first_shift_grad: float32 [768], replicated
- w_query_grad: float32 [768, 768], P(('dp', 'hid', 'mp'))
- b_query_grad: float32 [768], replicated
- w_key_grad: float32 [768, 768], P(('dp', 'hid', 'mp'))
- w_value_grad: float32 [768, 768], P(('dp', 'hid', 'mp'))
- b_value_grad: float32 [768], replicated
- w_out_grad: float32 [768, 768], P(('dp', 'hid', 'mp'))
- b_out_grad: float32 [768], replicated
- second_gain_grad: float32 [768], replicated
- second_shift_grad: float32 [768], replicated
- w_up_grad: float32 [768, 3072], P('dp', ('hid', 'mp'))
- b_up_grad: float32 [3072], replicated
- w_down_grad: float32 [3072, 768], P(('hid', 'mp'), 'dp')
- b_down_grad: float32 [768], replicated
The draws below stay inside these ranges and needn't reach their ends.
Inputs may be any that keep to these rules, and one draw needn't show every extreme that they name: `segment_ids`: within each sequence of 1024 tokens the ids never fall and take every value, so that a sequence holds 4 documents. `cluster_ids`: for each head and sequence every cluster holds one token or more, all of one document, and every document holds 25 of the head's clusters.
All inputs are finite; a program needn't handle non-finite values.
Results may differ from the reference program's by a relative error of at most 0.015.
The reference program's roundings to bfloat16 on the way count: a program that leaves them out, or rounds other values in their place, can miss the bound.
Values may be sent and summed in bfloat16 or wider, within the bound.
No kernel may reach another device: no remote copies, remote signals or barrier semaphores. Data moves between devices by JAX's collectives and lax.ppermute only.
A program may use at most 192 MiB of HBM per device.

```python
import jax
import jax.numpy as jnp
from jax import lax

D = 768
HEADS = 12
HEAD = 64
FF = 3072
CLUSTERS = 100
SEQ = 1024
DOCS = 4
TOKENS = 32768


def layout(key):
    row_total = TOKENS // SEQ
    reach = SEQ // (4 * DOCS)
    jitter = jax.random.randint(jax.random.fold_in(key, 11), (row_total, DOCS - 1), -reach, reach + 1)
    cuts = (jnp.arange(1, DOCS, dtype=jnp.int32) * (SEQ // DOCS))[None, :] + jitter
    places = jnp.arange(SEQ, dtype=jnp.int32)
    segments = jnp.sum((places[None, :, None] >= cuts[:, None, :]).astype(jnp.int32), axis=2)
    starts = jnp.concatenate([jnp.zeros((row_total, 1), jnp.int32), cuts], axis=1)
    begins = jnp.take_along_axis(starts, segments, axis=1)
    return (segments, places[None, :] - begins)


def draw_segment_ids(key, part):
    segments, inner = layout(key)
    return segments.reshape(TOKENS).astype(jnp.int32)


def draw_cluster_ids(key, part):
    segments, inner = layout(key)
    row_total = TOKENS // SEQ
    per_doc = CLUSTERS // DOCS
    subkeys = jax.random.split(jax.random.fold_in(key, 23), row_total * HEADS)
    orders = jax.vmap(lambda one_key: jax.random.permutation(one_key, CLUSTERS))(subkeys)
    orders = orders.reshape(row_total, HEADS, CLUSTERS).astype(jnp.int32)
    picks = jax.random.randint(jax.random.fold_in(key, 37), (row_total, HEADS, SEQ), 0, per_doc)
    local = jnp.where(inner[:, None, :] < per_doc, inner[:, None, :], picks)
    slots = (segments[:, None, :] * per_doc + local).astype(jnp.int32)
    chosen = jnp.take_along_axis(orders, slots, axis=2)
    return chosen.transpose(1, 0, 2).reshape(HEADS, TOKENS).astype(jnp.int32)


def strengthened(array, rng, source, target, shards_of, factor):
    def block_of(axis_at):
        return (jnp.arange(array.shape[axis_at]) // (array.shape[axis_at] // shards_of)).reshape((-1,) + (1,) * (array.ndim - 1 - axis_at))

    first = jax.random.permutation(rng, shards_of)[block_of(target)]
    second = (block_of(target) + shards_of // 2) % shards_of
    return jnp.where((block_of(source) == first) | (block_of(source) == second), factor * array, array)


def level_of(own_key, dims, shards, least, high):
    factor_of = 1.0
    for dim, shards_of in shards:
        heights = jax.random.uniform(jax.random.fold_in(jax.random.fold_in(own_key, 6), dim), (shards_of,), jnp.float32, least / len(shards), high / len(shards))
        factor_of = factor_of * jnp.repeat(jnp.exp(heights), dims[dim] // shards_of).reshape((-1,) + (1,) * (len(dims) - 1 - dim))
    return factor_of


def gaussian(own_key, shape, scale, most, shards=(), kind=jnp.bfloat16):
    loudness = level_of(own_key, shape, shards, -0.22, 0.18) if shards else 1.0
    values = jax.random.normal(own_key, shape, jnp.float32) * scale * loudness
    return jnp.minimum(jnp.maximum(values, -most), most).astype(kind)


def noise_with(rng, extent, scale, most, cuts, heavy, kind=jnp.bfloat16):
    values = scale * jax.random.normal(rng, extent, jnp.float32)
    if cuts:
        values = values * level_of(rng, extent, cuts, -0.22, 0.18)
    return jnp.clip(strengthened(values, jax.random.fold_in(rng, 3), *heavy), -most, most).astype(kind)


def setup_inputs(seed: int = 0) -> dict:
    arg_keys = jax.random.split(jax.random.key(seed), 20)
    tokens = noise_with(arg_keys[0], (TOKENS, D), 1.0, 6.0, ((0, 32),), (0, 1, 32, 2.75))
    segment_ids = draw_segment_ids(jax.random.fold_in(arg_keys[19], 71), 0)
    cluster_ids = draw_cluster_ids(jax.random.fold_in(arg_keys[19], 71), 0)
    cotangent = noise_with(arg_keys[3], (TOKENS, D), 1.0, 6.0, ((0, 32),), (0, 1, 32, 2.75))
    first_gain = jnp.clip(1.0 + 0.1 * jax.random.normal(arg_keys[4], (D,), jnp.float32), 0.5, 1.5)
    first_shift = gaussian(arg_keys[5], (D,), 0.3, 2.0, (), jnp.float32)
    w_query = gaussian(arg_keys[6], (D, D), (D // 16) ** -0.5, 0.875, ((0, 32),), jnp.float32)
    b_query = gaussian(arg_keys[7], (D,), 1.0, 5.0, (), jnp.float32)
    w_key = gaussian(arg_keys[8], (D, D), D ** -0.5, 0.21875, ((0, 32),), jnp.float32)
    w_value = gaussian(arg_keys[9], (D, D), D ** -0.5, 0.21875, ((0, 32),), jnp.float32)
    b_value = gaussian(arg_keys[10], (D,), 0.1, 0.6, (), jnp.float32)
    w_out = gaussian(arg_keys[11], (D, D), (D // 32) ** -0.5, 1.25, ((0, 32),), jnp.float32)
    b_out = gaussian(arg_keys[12], (D,), 0.3, 2.0, (), jnp.float32)
    second_gain = jnp.clip(1.0 + 0.1 * jax.random.normal(arg_keys[13], (D,), jnp.float32), 0.5, 1.5)
    second_shift = gaussian(arg_keys[14], (D,), 0.3, 2.0, (), jnp.float32)
    w_up = gaussian(arg_keys[15], (D, FF), D ** -0.5, 0.21875, ((0, 8), (1, 4)), jnp.float32)
    b_up = gaussian(arg_keys[16], (FF,), 0.3, 2.0, (), jnp.float32)
    w_down = gaussian(arg_keys[17], (FF, D), FF ** -0.5, 0.109375, ((0, 4), (1, 8)), jnp.float32)
    b_down = gaussian(arg_keys[18], (D,), 0.3, 2.0, (), jnp.float32)
    return dict(tokens=tokens, segment_ids=segment_ids, cluster_ids=cluster_ids, cotangent=cotangent, first_gain=first_gain, first_shift=first_shift, w_query=w_query, b_query=b_query, w_key=w_key, w_value=w_value, b_value=b_value, w_out=w_out, b_out=b_out, second_gain=second_gain, second_shift=second_shift, w_up=w_up, b_up=b_up, w_down=w_down, b_down=b_down)


precise = lax.Precision.HIGHEST

@jax.custom_vjp
def low(v):
    return lax.optimization_barrier(v.astype(jnp.bfloat16)).astype(jnp.float32)

@jax.custom_vjp
def low_back(v):
    return v

def low_keep(v):
    return (low(v), None)

def low_pass(kept, grad):
    return (grad,)

def back_keep(v):
    return (v, None)

def back_low(kept, grad):
    return (low(grad),)
low.defvjp(low_keep, low_pass)
low_back.defvjp(back_keep, back_low)

def normalize(values, gain, shift):
    middle = lax.optimization_barrier(jnp.mean(values, axis=-1, keepdims=True))
    centered = values - middle
    spread = lax.optimization_barrier(jnp.mean(centered * centered, axis=-1, keepdims=True))
    return centered * lax.rsqrt(spread + 1e-05) * gain + shift

def clustered(query, key_rows, value_rows, segments, clusters):
    query_heads = query.reshape(SEQ, HEADS, HEAD)
    key_heads = key_rows.reshape(SEQ, HEADS, HEAD)
    value_heads = value_rows.reshape(SEQ, HEADS, HEAD)
    members = clusters[:, None, :] == jnp.arange(CLUSTERS, dtype=jnp.int32)[None, :, None]
    one_hot = members.astype(query.dtype)
    counts = lax.optimization_barrier(jnp.sum(one_hot, axis=2))
    summed = jnp.einsum('hcl,lhd->hcd', one_hot, query_heads, precision=precise)
    centroid = low(summed / counts[:, :, None])
    owners = lax.optimization_barrier(jnp.max(jnp.where(members, segments[None, None, :], -1), axis=2))
    allowed = owners[:, :, None] == segments[None, None, :]
    scores = low_back(0.125 * jnp.einsum('hcd,lhd->hcl', centroid, key_heads, precision=precise))
    masked = jnp.where(allowed, scores, -1e+30)
    probability = low(jax.nn.softmax(masked, axis=-1))
    context = low_back(low(jnp.einsum('hcl,lhd->hcd', probability, value_heads, precision=precise)))
    mixed = jnp.einsum('hcl,hcd->lhd', one_hot, context, precision=precise)
    return mixed.reshape(SEQ, D)

def forward(inputs, params, segments, clusters, group):
    first_gain, first_shift, w_query, b_query, w_key, w_value, b_value, w_out, b_out, second_gain, second_shift, w_up, b_up, w_down, b_down = params
    normed_in = low(normalize(inputs, first_gain, first_shift))
    query = low_back(low(jnp.dot(normed_in, low(w_query), precision=precise) + b_query))
    key_rows = low_back(low(jnp.dot(normed_in, low(w_key), precision=precise)))
    value_rows = low_back(low(jnp.dot(normed_in, low(w_value), precision=precise) + b_value))
    shaped = lambda table: table.reshape(group, SEQ, D)
    mixed = jax.vmap(clustered)(shaped(query), shaped(key_rows), shaped(value_rows), segments.reshape(group, SEQ), clusters.reshape(HEADS, group, SEQ).transpose(1, 0, 2))
    mixed = low_back(mixed.reshape(group * SEQ, D))
    residual = inputs + low_back(jnp.dot(mixed, low(w_out), precision=precise) + b_out)
    normed_mid = low(normalize(residual, second_gain, second_shift))
    pre_act = low_back(jnp.dot(normed_mid, low(w_up), precision=precise) + b_up)
    hidden = low(jax.nn.gelu(pre_act, approximate=False))
    return residual + jnp.dot(hidden, low(w_down), precision=precise) + b_down

def reference(tokens, segment_ids, cluster_ids, cotangent, first_gain, first_shift, w_query, b_query, w_key, w_value, b_value, w_out, b_out, second_gain, second_shift, w_up, b_up, w_down, b_down):
    params = tuple((p.astype(jnp.float32) for p in (first_gain, first_shift, w_query, b_query, w_key, w_value, b_value, w_out, b_out, second_gain, second_shift, w_up, b_up, w_down, b_down)))
    row_total = TOKENS // SEQ
    group = 4 if row_total % 4 == 0 else 1
    steps_total = row_total // group
    span = group * SEQ
    inputs = tokens.astype(jnp.float32).reshape(steps_total, span, D)
    grads_in = cotangent.astype(jnp.float32).reshape(steps_total, span, D)
    segments = segment_ids.reshape(steps_total, span)
    clusters = cluster_ids.reshape(HEADS, steps_total, span).transpose(1, 0, 2)

    def advance(totals, item):
        block_in, block_grad, block_seg, block_clu = item

        def run(values, weights):
            return forward(values, weights, block_seg, block_clu, group)
        result, pull = jax.vjp(run, block_in, params)
        grad_inputs, grad_params = pull(block_grad)
        totals = jax.tree.map(jnp.add, totals, grad_params)
        return (totals, (result.astype(jnp.bfloat16), grad_inputs.astype(jnp.bfloat16)))
    zeros = jax.tree.map(jnp.zeros_like, params)
    totals, (results, grad_rows) = lax.scan(advance, zeros, (inputs, grads_in, segments, clusters))
    return (results.reshape(TOKENS, D), grad_rows.reshape(TOKENS, D), totals[0], totals[1], totals[2], totals[3], totals[4], totals[5], totals[6], totals[7], totals[8], totals[9], totals[10], totals[11], totals[12], totals[13], totals[14])
```

```python
import jax
import jax.numpy as jnp
from jax import lax
from jax.sharding import PartitionSpec as P

D = 768
HEADS = 12
HEAD = 64
CLUSTERS = 100
SEQ = 1024


def matmul(left, right):
    return jnp.dot(left, right, preferred_element_type=jnp.float32)


def matmul_nt(left, right):
    return lax.dot_general(left, right, (((1,), (1,)), ((), ())), preferred_element_type=jnp.float32)


def matmul_tn(left, right):
    return lax.dot_general(left, right, (((0,), (0,)), ((), ())), preferred_element_type=jnp.float32)


def swapped(array, axis, bit):
    count = lax.axis_size(axis)
    return lax.ppermute(array, axis, [(i, i ^ (1 << bit)) for i in range(count)])


def own_bit(axis, bit):
    return (lax.axis_index(axis) >> bit) & 1


def joined(own, other, mine, place):
    own, other = (jnp.expand_dims(own, place), jnp.expand_dims(other, place))
    shape = own.shape[:place] + (2,) + own.shape[place + 1 :]
    return jnp.where(lax.broadcasted_iota(jnp.int32, shape, place) == mine, own, other)


class Gather:
    def __init__(self, piece):
        self.piece, self.held = piece, []

    def step(self, axis, bit, rank):
        other = swapped(self.piece, axis, bit)
        place = 1 + sum(1 for h in self.held if h > rank)
        self.held.append(rank)
        self.piece = joined(self.piece, other, own_bit(axis, bit), place)
        return self


class Scatter:
    def __init__(self, total, held):
        self.total, self.held = total, sorted(held, reverse=True)

    def step(self, axis, bit, rank):
        place = 1 + self.held.index(rank)
        mine = own_bit(axis, bit)
        sent = lax.dynamic_index_in_dim(self.total, 1 - mine, place, keepdims=False)
        kept = lax.dynamic_index_in_dim(self.total, mine, place, keepdims=False)
        got = swapped(sent, axis, bit)
        self.held.remove(rank)
        self.total = (kept.astype(jnp.float32) + got.astype(jnp.float32)).astype(jnp.bfloat16)
        return self


def summed_everywhere(array, dp_bits):
    for axis, bit in [("mp", 0), ("hid", 0)] + [("dp", b) for b in range(dp_bits)]:
        array = array + swapped(array, axis, bit)
    return array


def moments(values):
    middle = jnp.mean(values, axis=-1, keepdims=True)
    centered = values - middle
    spread = jnp.mean(centered * centered, axis=-1, keepdims=True)
    return (centered * lax.rsqrt(spread + 1e-05), lax.rsqrt(spread + 1e-05))


def norm_pull(grad, gain, unit, scale):
    scaled = grad * gain
    first = jnp.mean(scaled, axis=-1, keepdims=True)
    second = jnp.mean(scaled * unit, axis=-1, keepdims=True)
    return scale * (scaled - first - unit * second)


def gate_and_slope(v):
    phi = 0.5 * (1.0 + lax.erf(v * 0.7071067811865476))
    density = 0.3989422804014327 * jnp.exp(-0.5 * v * v)
    return (v * phi, phi + v * density)


def attend(query, key_rows, value_rows, segments, clusters):
    members = clusters[:, None, :] == jnp.arange(CLUSTERS, dtype=jnp.int32)[None, :, None]
    one_hot = members.astype(jnp.bfloat16)
    counts = jnp.sum(members.astype(jnp.float32), axis=2)
    owners = jnp.max(jnp.where(members, segments[None, None, :], -1), axis=2)
    allowed = owners[:, :, None] == segments[None, None, :]
    heads = lambda rows: rows.reshape(SEQ, HEADS, HEAD)
    summed = jnp.einsum("hcl,lhd->hcd", one_hot, heads(query), preferred_element_type=jnp.float32)
    centroid = (summed / counts[:, :, None]).astype(jnp.bfloat16)
    scores = 0.125 * jnp.einsum("hcd,lhd->hcl", centroid, heads(key_rows), preferred_element_type=jnp.float32)
    masked = jnp.where(allowed, scores, -1e30)
    highest = jnp.max(masked, axis=2, keepdims=True)
    exponent = jnp.where(allowed, jnp.exp(masked - highest), 0.0)
    probability = exponent / jnp.sum(exponent, axis=2, keepdims=True)
    context = jnp.einsum(
        "hcl,lhd->hcd", probability.astype(jnp.bfloat16), heads(value_rows), preferred_element_type=jnp.float32
    ).astype(jnp.bfloat16)
    mixed = jnp.einsum("hcl,hcd->lhd", one_hot, context, preferred_element_type=jnp.float32)
    return (mixed.reshape(SEQ, D).astype(jnp.bfloat16), (members, one_hot, counts, centroid, probability))


def attend_back(kept, key_rows, value_rows, grad_mixed):
    members, one_hot, counts, centroid, probability = kept
    heads = lambda rows: rows.reshape(SEQ, HEADS, HEAD)
    prob_low = probability.astype(jnp.bfloat16)
    grad_context = jnp.einsum(
        "hcl,lhd->hcd", one_hot, heads(grad_mixed), preferred_element_type=jnp.float32
    ).astype(jnp.bfloat16)
    grad_value = jnp.einsum("hcl,hcd->lhd", prob_low, grad_context, preferred_element_type=jnp.float32)
    grad_prob = jnp.einsum("hcd,lhd->hcl", grad_context, heads(value_rows), preferred_element_type=jnp.float32)
    grad_scores = probability * (grad_prob - jnp.sum(probability * grad_prob, axis=2, keepdims=True))
    grad_scores = grad_scores.astype(jnp.bfloat16)
    grad_centroid = 0.125 * jnp.einsum(
        "hcl,lhd->hcd", grad_scores, heads(key_rows), preferred_element_type=jnp.float32
    )
    grad_key = 0.125 * jnp.einsum("hcl,hcd->lhd", grad_scores, centroid, preferred_element_type=jnp.float32)
    shared = (grad_centroid / counts[:, :, None]).astype(jnp.bfloat16)
    grad_query = jnp.einsum("hcl,hcd->lhd", one_hot, shared, preferred_element_type=jnp.float32)
    return tuple(g.reshape(SEQ, D).astype(jnp.bfloat16) for g in (grad_query, grad_key, grad_value))


def shards(
    tokens,
    segment_ids,
    cluster_ids,
    cotangent,
    first_gain,
    first_shift,
    w_query,
    b_query,
    w_key,
    w_value,
    b_value,
    w_out,
    b_out,
    second_gain,
    second_shift,
    w_up,
    b_up,
    w_down,
    b_down,
):
    dp_bits = lax.axis_size("dp").bit_length() - 1
    high = [("dp", b, b + 2) for b in range(1, dp_bits)]
    low, hid, mp = (("dp", 0, 2), ("hid", 0, 1), ("mp", 0, 0))
    bf = jnp.bfloat16
    part = D // (4 << dp_bits)
    wide = D // (1 << dp_bits)

    attn = Gather(jnp.stack([w.astype(bf) for w in (w_query, w_key, w_value, w_out)]))
    ff = Gather(jnp.stack([w_up.astype(bf), w_down.T.astype(bf)]))
    for at in high:
        attn.step(*at)
    for at in high:
        ff.step(*at)
    first, second = (Gather(attn.piece[:2]), Gather(attn.piece[2:]))
    first.held, second.held = (list(attn.held), list(attn.held))
    first.step(*low)
    second.step(*hid)
    first.step(*hid)
    second.step(*low)
    first.step(*mp)
    second.step(*mp)
    query_full, key_full = first.piece.reshape(2, D, D)
    value_full, out_full = second.piece.reshape(2, D, D)
    up, down = (Gather(ff.piece[:1]), Gather(ff.piece[1:]))
    up.held, down.held = (list(ff.held), list(ff.held))
    up.step(*low)
    down_mate = Gather(swapped(down.piece, "hid", 0))
    down_mate.held = list(down.held)
    up_own = up.piece.reshape(D, D)
    up_mate = swapped(up_own, "hid", 0)
    both = Gather(jnp.concatenate([down.piece, down_mate.piece]))
    both.held = list(down.held)
    both.step(*low)
    down_own, down_mate = both.piece.reshape(2, D, D)
    ups = [up_own, up_mate]
    ups += [swapped(u, "mp", 0) for u in ups]
    downs = [down_own, down_mate]
    downs += [swapped(d, "mp", 0) for d in downs]
    me = lax.axis_index(("hid", "mp"))
    blocks = [me, me ^ 2, me ^ 1, me ^ 3]

    inputs = tokens.astype(jnp.float32)
    unit_in, scale_in = moments(inputs)
    normed_in = (unit_in * first_gain + first_shift).astype(bf)
    query = (matmul(normed_in, query_full) + b_query).astype(bf)
    key_rows = matmul(normed_in, key_full).astype(bf)
    value_rows = (matmul(normed_in, value_full) + b_value).astype(bf)
    mixed, kept = attend(query, key_rows, value_rows, segment_ids, cluster_ids)
    residual = inputs + matmul(mixed, out_full) + b_out
    unit_mid, scale_mid = moments(residual)
    normed_mid = (unit_mid * second_gain + second_shift).astype(bf)
    grad_out = cotangent.astype(jnp.float32)

    branch, grad_mid = (0.0, 0.0)
    up_sends, down_sends, bias_up = ([], [], jnp.zeros((4, D), jnp.float32))
    for up_w, down_w, block in zip(ups, downs, blocks):
        up_bias = lax.dynamic_slice_in_dim(b_up, block * D, D)
        hidden, slope = gate_and_slope(matmul(normed_mid, up_w) + up_bias)
        hidden = hidden.astype(bf)
        branch = branch + matmul_nt(hidden, down_w)
        grad_pre = (matmul(cotangent, down_w) * slope).astype(bf)
        down_sends.append(matmul_tn(cotangent, hidden).astype(bf))
        up_sends.append(matmul_tn(normed_mid, grad_pre).astype(bf))
        bias_up = lax.dynamic_update_slice(bias_up, jnp.sum(grad_pre.astype(jnp.float32), axis=0)[None], (block, 0))
        grad_mid = grad_mid + matmul_nt(grad_pre, up_w)
    output = (residual + branch + b_down).astype(bf)

    def added(own, got):
        return (own.astype(jnp.float32) + got.astype(jnp.float32)).astype(bf)

    bits = [2] * dp_bits
    up_sum = [added(up_sends[k], swapped(up_sends[k + 2], "mp", 0)) for k in (0, 1)]
    up_sum = added(up_sum[0], swapped(up_sum[1], "hid", 0))
    up_sum = Scatter(up_sum.reshape(1, *bits, wide, D), [b + 2 for b in range(dp_bits)])
    up_sum.step(*low)
    down_sum = [added(down_sends[k], swapped(down_sends[k + 2], "mp", 0)) for k in (0, 1)]
    down_sum = Scatter(jnp.stack(down_sum).reshape(2, *bits, wide, D), [b + 2 for b in range(dp_bits)])
    down_sum.step(*low)
    down_sum.total = added(down_sum.total[:1], swapped(down_sum.total[1:], "hid", 0))
    for at in reversed(high):
        up_sum.step(*at)
        down_sum.step(*at)
    up_grad = up_sum.total[0].astype(jnp.float32)
    down_grad = down_sum.total[0].astype(jnp.float32).T

    second_shift_grad = jnp.sum(grad_mid, axis=0)
    second_gain_grad = jnp.sum(grad_mid * unit_mid, axis=0)
    grad_resid = grad_out + norm_pull(grad_mid, second_gain, unit_mid, scale_mid)
    grad_branch = grad_resid.astype(bf)
    out_grad = matmul_tn(mixed, grad_branch)
    grad_mixed = matmul_nt(grad_branch, out_full).astype(bf)
    grad_query, grad_key, grad_value = attend_back(kept, key_rows, value_rows, grad_mixed)
    query_grad = matmul_tn(normed_in, grad_query)
    key_grad = matmul_tn(normed_in, grad_key)
    value_grad = matmul_tn(normed_in, grad_value)
    grad_in = matmul_nt(grad_query, query_full) + matmul_nt(grad_key, key_full) + matmul_nt(grad_value, value_full)
    tokens_grad = (grad_resid + norm_pull(grad_in, first_gain, unit_in, scale_in)).astype(bf)

    every = [b + 2 for b in range(dp_bits)] + [1, 0]
    view = (2, *bits, 2, 2, part, D)
    one = Scatter(jnp.stack([query_grad.astype(bf), key_grad.astype(bf)]).reshape(view), every)
    two = Scatter(jnp.stack([value_grad.astype(bf), out_grad.astype(bf)]).reshape(view), every)
    one.step(*mp)
    two.step(*mp)
    one.step(*low)
    two.step(*hid)
    one.step(*hid)
    two.step(*low)
    for at in reversed(high):
        one.step(*at)
        two.step(*at)
    query_sum, key_sum = one.total.astype(jnp.float32)
    value_sum, out_sum = two.total.astype(jnp.float32)

    total = lambda rows: jnp.sum(rows.astype(jnp.float32), axis=0)
    small = jnp.concatenate(
        [
            jnp.stack(
                [
                    jnp.sum(grad_in * unit_in, axis=0),
                    jnp.sum(grad_in, axis=0),
                    total(grad_query),
                    total(grad_value),
                    total(grad_branch),
                    second_gain_grad,
                    second_shift_grad,
                    total(cotangent),
                ]
            ),
            bias_up,
        ]
    )
    small = summed_everywhere(small, dp_bits)
    return (
        output,
        tokens_grad,
        small[0],
        small[1],
        query_sum,
        small[2],
        key_sum,
        value_sum,
        small[3],
        out_sum,
        small[4],
        small[5],
        small[6],
        up_grad,
        small[8:].reshape(-1),
        down_grad,
        small[7],
    )


def solution(mesh):
    return jax.shard_map(
        shards,
        mesh=mesh,
        in_specs=(
            P(("dp", "hid", "mp"), None),
            P(("dp", "hid", "mp")),
            P(None, ("dp", "hid", "mp")),
            P(("dp", "hid", "mp"), None),
            P(),
            P(),
            P(("dp", "hid", "mp"), None),
            P(),
            P(("dp", "hid", "mp"), None),
            P(("dp", "hid", "mp"), None),
            P(),
            P(("dp", "hid", "mp"), None),
            P(),
            P(),
            P(),
            P("dp", ("hid", "mp")),
            P(),
            P(("hid", "mp"), "dp"),
            P(),
        ),
        out_specs=(
            P(("dp", "hid", "mp"), None),
            P(("dp", "hid", "mp"), None),
            P(),
            P(),
            P(("dp", "hid", "mp"), None),
            P(),
            P(("dp", "hid", "mp"), None),
            P(("dp", "hid", "mp"), None),
            P(),
            P(("dp", "hid", "mp"), None),
            P(),
            P(),
            P(),
            P("dp", ("hid", "mp")),
            P(),
            P(("hid", "mp"), "dp"),
            P(),
        ),
        check_vma=False,
    )
```

```python
import functools

import jax
import jax.numpy as jnp
from jax import lax
from jax.experimental import pallas as pl
from jax.experimental.pallas import tpu as pltpu
from jax.sharding import PartitionSpec as P

D = 768
HEADS = 12
HEAD = 64
CLUSTERS = 100
SEQ = 1024


def matmul(left, right):
    return jnp.dot(left, right, preferred_element_type=jnp.float32)


def matmul_nt(left, right):
    return lax.dot_general(left, right, (((1,), (1,)), ((), ())), preferred_element_type=jnp.float32)


def matmul_tn(left, right):
    return lax.dot_general(left, right, (((0,), (0,)), ((), ())), preferred_element_type=jnp.float32)


def swapped(array, axis, bit):
    count = lax.axis_size(axis)
    return lax.ppermute(array, axis, [(i, i ^ (1 << bit)) for i in range(count)])


def own_bit(axis, bit):
    return (lax.axis_index(axis) >> bit) & 1


def joined(own, other, mine, place):
    own, other = (jnp.expand_dims(own, place), jnp.expand_dims(other, place))
    shape = own.shape[:place] + (2,) + own.shape[place + 1 :]
    return jnp.where(lax.broadcasted_iota(jnp.int32, shape, place) == mine, own, other)


def halves(array, axis, bit, place):
    mine = own_bit(axis, bit)
    take = lambda k: lax.dynamic_index_in_dim(array, k, place, keepdims=False)
    return (take(mine), take(1 - mine))


def moments(values):
    middle = jnp.mean(values, axis=-1, keepdims=True)
    centered = values - middle
    spread = jnp.mean(centered * centered, axis=-1, keepdims=True)
    return (centered * lax.rsqrt(spread + 1e-05), lax.rsqrt(spread + 1e-05))


def norm_pull(grad, gain, unit, scale):
    scaled = grad * gain
    first = jnp.mean(scaled, axis=-1, keepdims=True)
    second = jnp.mean(scaled * unit, axis=-1, keepdims=True)
    return scale * (scaled - first - unit * second)


def gate_and_slope(v):
    size = jnp.abs(v)
    bell = jnp.exp(-0.5 * v * v)
    t = 1.0 / (1.0 + 0.23164189 * size)
    series = 0.7107068705 + t * (-0.7265760135 + t * 0.5307027145)
    tail = t * (0.127414796 + t * (-0.142248368 + t * series)) * bell
    phi = jnp.where(v < 0, tail, 1.0 - tail)
    return (v * phi, phi + v * (0.3989422804014327 * bell))


def ff_kernel(rows, x, cot, xt, cott, wu, wd, bu, branch_in, mid_in, branch, mid, dwu, dwd, dbu):
    nt = (((1,), (1,)), ((), ()))
    hs, gs = ([], [])
    total = jnp.zeros_like(dbu)
    for r in range(x.shape[0] // rows):
        at = pl.ds(r * rows, rows)
        pre = matmul(x[at, :], wu[...]) + bu[...]
        grad_hidden = matmul(cot[at, :], wd[...])
        h, slope = gate_and_slope(pre)
        h = h.astype(jnp.bfloat16)
        g = (grad_hidden * slope).astype(jnp.bfloat16)
        total += jnp.sum(g.astype(jnp.float32), axis=0, keepdims=True)
        branch[at, :] = branch_in[at, :] + lax.dot_general(h, wd[...], nt, preferred_element_type=jnp.float32)
        mid[at, :] = mid_in[at, :] + lax.dot_general(g, wu[...], nt, preferred_element_type=jnp.float32)
        hs.append(h)
        gs.append(g)
    dwd[...] = matmul(cott[...], jnp.concatenate(hs, axis=0)).astype(jnp.bfloat16)
    dwu[...] = matmul(xt[...], jnp.concatenate(gs, axis=0)).astype(jnp.bfloat16)
    dbu[...] = total


def near(array):
    return pltpu.with_memory_space_constraint(array, pltpu.VMEM)


def ff_block(x, cot, xt, cott, wu, wd, bu, branch, mid):
    f32, bf = (jnp.float32, jnp.bfloat16)
    count, wide = (x.shape[0], wu.shape[1])
    spec = pl.BlockSpec(memory_space=pltpu.VMEM)
    return pl.pallas_call(
        functools.partial(ff_kernel, 256),
        out_shape=(
            jax.ShapeDtypeStruct((count, D), f32),
            jax.ShapeDtypeStruct((count, D), f32),
            jax.ShapeDtypeStruct((D, wide), bf),
            jax.ShapeDtypeStruct((D, wide), bf),
            jax.ShapeDtypeStruct((1, wide), f32),
        ),
        in_specs=[spec] * 9,
        out_specs=(spec,) * 5,
        input_output_aliases={7: 0, 8: 1},
        compiler_params=pltpu.CompilerParams(vmem_limit_bytes=24 * 1024 * 1024),
        cost_estimate=pl.CostEstimate(
            flops=12 * count * D * wide, bytes_accessed=4 * D * wide, transcendentals=2 * count * wide
        ),
        name="ff_block",
    )(near(x), near(cot), near(xt), near(cott), near(wu), near(wd), bu, near(branch), near(mid))


def tied(*arrays):
    return lax.optimization_barrier(arrays)


def added(own, got):
    return (own.astype(jnp.float32) + got.astype(jnp.float32)).astype(jnp.bfloat16)


def memberships(segments, clusters):
    members = clusters[:, None, :] == jnp.arange(CLUSTERS, dtype=jnp.int32)[None, :, None]
    counts = jnp.sum(members.astype(jnp.float32), axis=2)
    owners = jnp.max(jnp.where(members, segments[None, None, :], -1), axis=2)
    return (members.astype(jnp.bfloat16), counts, owners)


def heads(rows):
    return rows.reshape(SEQ, HEADS, HEAD)


def probabilities(query, key_rows, segments, one_hot, counts, owners):
    allowed = owners[:, :, None] == segments[None, None, :]
    summed = jnp.einsum("hcl,lhd->hcd", one_hot, heads(query), preferred_element_type=jnp.float32)
    centroid = (summed / counts[:, :, None]).astype(jnp.bfloat16)
    scores = 0.125 * jnp.einsum("hcd,lhd->hcl", centroid, heads(key_rows), preferred_element_type=jnp.float32)
    masked = jnp.where(allowed, scores, -1e30)
    highest = jnp.max(masked, axis=2, keepdims=True)
    exponent = jnp.where(allowed, jnp.exp(masked - highest), 0.0)
    return (centroid, exponent / jnp.sum(exponent, axis=2, keepdims=True))


def mixture(probability, one_hot, value_rows):
    context = jnp.einsum(
        "hcl,lhd->hcd", probability.astype(jnp.bfloat16), heads(value_rows), preferred_element_type=jnp.float32
    ).astype(jnp.bfloat16)
    mixed = jnp.einsum("hcl,hcd->lhd", one_hot, context, preferred_element_type=jnp.float32)
    return mixed.reshape(SEQ, D).astype(jnp.bfloat16)


def attend_back(kept, key_rows, value_rows, grad_mixed):
    one_hot, counts, centroid, probability = kept
    prob_low = probability.astype(jnp.bfloat16)
    grad_context = jnp.einsum(
        "hcl,lhd->hcd", one_hot, heads(grad_mixed), preferred_element_type=jnp.float32
    ).astype(jnp.bfloat16)
    grad_value = jnp.einsum("hcl,hcd->lhd", prob_low, grad_context, preferred_element_type=jnp.float32)
    grad_prob = jnp.einsum("hcd,lhd->hcl", grad_context, heads(value_rows), preferred_element_type=jnp.float32)
    grad_scores = probability * (grad_prob - jnp.sum(probability * grad_prob, axis=2, keepdims=True))
    grad_scores = grad_scores.astype(jnp.bfloat16)
    grad_centroid = 0.125 * jnp.einsum(
        "hcl,lhd->hcd", grad_scores, heads(key_rows), preferred_element_type=jnp.float32
    )
    grad_key = 0.125 * jnp.einsum("hcl,hcd->lhd", grad_scores, centroid, preferred_element_type=jnp.float32)
    shared = (grad_centroid / counts[:, :, None]).astype(jnp.bfloat16)
    grad_query = jnp.einsum("hcl,hcd->lhd", one_hot, shared, preferred_element_type=jnp.float32)
    return tuple(g.reshape(SEQ, D).astype(jnp.bfloat16) for g in (grad_query, grad_key, grad_value))


def shards(
    tokens,
    segment_ids,
    cluster_ids,
    cotangent,
    first_gain,
    first_shift,
    w_query,
    b_query,
    w_key,
    w_value,
    b_value,
    w_out,
    b_out,
    second_gain,
    second_shift,
    w_up,
    b_up,
    w_down,
    b_down,
):
    dp_bits = lax.axis_size("dp").bit_length() - 1
    high = list(range(1, dp_bits))
    bf = jnp.bfloat16
    part = D // (4 << dp_bits)
    wide = D // (1 << dp_bits)
    up_high = [1 << len(high)]

    attn = jnp.stack([w.astype(bf) for w in (w_query, w_key, w_value, w_out)])
    ff = jnp.stack([w_up.astype(bf), w_down.T.astype(bf)])
    inputs = tokens.astype(jnp.float32)
    unit_in, scale_in = moments(inputs)
    normed_in = (unit_in * first_gain + first_shift).astype(bf)
    one_hot, counts, owners = memberships(segment_ids, cluster_ids)
    for bit in high:
        got = swapped(attn, "dp", bit)
        if bit == 1:
            got, normed_in = tied(got, normed_in)
        if bit == high[-1]:
            got, one_hot, counts, owners = tied(got, one_hot, counts, owners)
        attn = joined(attn, got, own_bit("dp", bit), 1)
    attn = attn.reshape(4, *up_high, part, D)
    first, second = (attn[:2], attn[2:])
    first_got, second_got = (swapped(first, "dp", 0), swapped(second, "hid", 0))
    for bit in high[:-1]:
        ff = joined(ff, swapped(ff, "dp", bit), own_bit("dp", bit), 1)
    ff_got = swapped(ff, "dp", high[-1])
    first = joined(first, first_got, own_bit("dp", 0), 2)
    first_got = swapped(first, "hid", 0)
    second = joined(second, second_got, own_bit("hid", 0), 2)
    second_got = swapped(second, "dp", 0)
    first = joined(first, first_got, own_bit("hid", 0), 3)
    second = joined(second, second_got, own_bit("dp", 0), 2)
    first_got, second_got = (swapped(first, "mp", 0), swapped(second, "mp", 0))
    first = joined(first, first_got, own_bit("mp", 0), 4)
    second = joined(second, second_got, own_bit("mp", 0), 4)
    query_full, key_full = first.reshape(2, D, D)
    value_full, out_full = second.reshape(2, D, D)

    query = (matmul(normed_in, query_full) + b_query).astype(bf)
    key_rows = matmul(normed_in, key_full).astype(bf)
    query, key_rows, ff_got = tied(query, key_rows, ff_got)
    ff = joined(ff, ff_got, own_bit("dp", high[-1]), 1)
    up, down = ff.reshape(2, *up_high, wide, D)
    up_got, down_got = (swapped(up, "dp", 0), swapped(down, "hid", 0))
    value_rows = (matmul(normed_in, value_full) + b_value).astype(bf)
    centroid, probability = probabilities(query, key_rows, segment_ids, one_hot, counts, owners)
    probability, value_rows, up_got, down_got = tied(probability, value_rows, up_got, down_got)
    up = joined(up, up_got, own_bit("dp", 0), 1).reshape(D, D)
    up_mate = swapped(up, "hid", 0)
    down = jnp.stack([down, down_got])
    down_got = swapped(down, "dp", 0)
    mixed = mixture(probability, one_hot, value_rows)
    residual = inputs + matmul(mixed, out_full) + b_out
    unit_mid, scale_mid = moments(residual)
    normed_mid = (unit_mid * second_gain + second_shift).astype(bf)
    normed_mid, up_mate, down_got = tied(normed_mid, up_mate, down_got)
    down, down_mate = joined(down, down_got, own_bit("dp", 0), 2).reshape(2, D, D)
    me = lax.axis_index(("hid", "mp"))
    blocks = [me ^ 2, me ^ 3, me, me ^ 1]
    ups = [up_mate, swapped(up_mate, "mp", 0), up, swapped(up, "mp", 0)]
    downs = [down_mate, swapped(down_mate, "mp", 0), down, swapped(down, "mp", 0)]

    cot_t, mid_t = (cotangent.T, normed_mid.T)
    branch, grad_mid = (residual + b_down, jnp.zeros((SEQ, D), jnp.float32))
    up_sends, down_sends, bias_up = ([], [], jnp.zeros((4, D), jnp.float32))
    up_tots, down_tots = ([], [])
    for k in range(4):
        up_bias = lax.dynamic_slice_in_dim(b_up, blocks[k] * D, D)[None]
        branch, grad_mid, up_send, down_send, bias = ff_block(
            normed_mid, cotangent, mid_t, cot_t, ups[k], downs[k], up_bias, branch, grad_mid
        )
        up_sends.append(up_send)
        down_sends.append(down_send)
        bias_up = lax.dynamic_update_slice(bias_up, bias, (blocks[k], 0))
        if k == 1:
            got = (swapped(up_send, "mp", 0), swapped(down_send, "mp", 0))
        if k == 2:
            branch, *got = tied(branch, *got)
            up_far, down_far = (added(up_sends[0], got[0]), added(down_sends[0], got[1]))
            up_far = swapped(up_far, "hid", 0)
            down_far, sent = halves(down_far.reshape(*up_high, 2, wide, D), "dp", 0, 1)
            down_far_got = swapped(sent, "dp", 0)
        if k == 3:
            got = (swapped(up_send, "mp", 0), swapped(down_send, "mp", 0))
    output = branch.astype(bf)

    grad_out = cotangent.astype(jnp.float32)
    second_shift_grad = jnp.sum(grad_mid, axis=0)
    second_gain_grad = jnp.sum(grad_mid * unit_mid, axis=0)
    grad_resid = grad_out + norm_pull(grad_mid, second_gain, unit_mid, scale_mid)
    grad_branch = grad_resid.astype(bf)
    grad_branch, *got = tied(grad_branch, *got)
    up_near, down_near = (added(up_sends[2], got[0]), added(down_sends[2], got[1]))
    down_near, sent = halves(down_near.reshape(*up_high, 2, wide, D), "dp", 0, 1)
    down_near_got = swapped(sent, "dp", 0)
    grad_mixed = matmul_nt(grad_branch, out_full).astype(bf)
    grad_mixed, up_far, down_far_got = tied(grad_mixed, up_far, down_far_got)
    up_near = added(up_near, up_far).reshape(*up_high, 2, wide, D)
    up_near, sent = halves(up_near, "dp", 0, 1)
    up_got = swapped(sent, "dp", 0)
    down_far = added(down_far, down_far_got)
    out_grad = matmul_tn(mixed, grad_branch).astype(bf)
    out_grad, down_near_got = tied(out_grad, down_near_got)
    down_got = swapped(down_far, "hid", 0)
    down_near = added(down_near, down_near_got)

    grad_query, grad_key, grad_value = attend_back(
        (one_hot, counts, centroid, probability), key_rows, value_rows, grad_mixed
    )
    grad_value, grad_key, up_got, down_got = tied(grad_value, grad_key, up_got, down_got)
    ff = jnp.stack([added(up_near, up_got), added(down_near, down_got)])
    bits = [2] * len(high)
    ff = ff.reshape(2, *bits, wide, D)
    ff, sent = halves(ff, "dp", high[-1], 1)
    ff_got = swapped(sent, "dp", high[-1])

    view = (*up_high, 2, 2, 2, part, D)

    def pair(left, right):
        both = jnp.stack([left, right]).reshape(2, *view)
        both, sent = halves(both, "mp", 0, 4)
        both = added(both, swapped(sent, "mp", 0))
        one, one_sent = halves(both[0], "dp", 0, 1)
        two, two_sent = halves(both[1], "hid", 0, 2)
        one_got, two_got = (swapped(one_sent, "dp", 0), swapped(two_sent, "hid", 0))
        return (one, two, one_got, two_got)

    def pair_on(one, two, one_got, two_got):
        one, one_sent = halves(added(one, one_got), "hid", 0, 1)
        two, two_sent = halves(added(two, two_got), "dp", 0, 1)
        return (one, two, swapped(one_sent, "hid", 0), swapped(two_sent, "dp", 0))

    def pair_up(one, two, one_got, two_got):
        return jnp.stack([added(one, one_got), added(two, two_got)]).reshape(2, *bits, part, D)

    value_grad = matmul_tn(normed_in, grad_value).astype(bf)
    vo = pair(value_grad, out_grad)
    key_grad = matmul_tn(normed_in, grad_key).astype(bf)
    query_grad = matmul_tn(normed_in, grad_query).astype(bf)
    key_grad, query_grad, *vo = tied(key_grad, query_grad, *vo)
    vo = pair_on(*vo)
    qk = pair(query_grad, key_grad)
    grad_in = matmul_nt(grad_query, query_full) + matmul_nt(grad_key, key_full) + matmul_nt(grad_value, value_full)
    grad_in, *vo = tied(grad_in, *vo)
    vo = pair_up(*vo)
    tokens_grad = (grad_resid + norm_pull(grad_in, first_gain, unit_in, scale_in)).astype(bf)
    tokens_grad, *qk = tied(tokens_grad, *qk)
    qk = pair_on(*qk)
    ff = added(ff, ff_got)

    total = lambda rows: jnp.sum(rows.astype(jnp.float32), axis=0)
    small = jnp.concatenate(
        [
            jnp.stack(
                [
                    jnp.sum(grad_in * unit_in, axis=0),
                    jnp.sum(grad_in, axis=0),
                    total(grad_query),
                    total(grad_value),
                    total(grad_branch),
                    second_gain_grad,
                    second_shift_grad,
                    total(cotangent),
                ]
            ),
            bias_up,
        ]
    )
    small = small + swapped(small, "mp", 0)
    small = small + swapped(small, "hid", 0)
    small = small + swapped(small, "dp", 0)
    qk = pair_up(*qk)
    attn = jnp.concatenate([qk, vo])
    for bit in reversed(high):
        attn, attn_sent = halves(attn, "dp", bit, 1)
        attn = added(attn, swapped(attn_sent, "dp", bit))
        if bit != high[-1]:
            ff, ff_sent = halves(ff, "dp", bit, 1)
            ff = added(ff, swapped(ff_sent, "dp", bit))
        small = small + swapped(small, "dp", bit)
    query_sum, key_sum, value_sum, out_sum = attn.astype(jnp.float32)
    up_grad = ff[0].astype(jnp.float32)
    down_grad = ff[1].astype(jnp.float32).T
    return (
        output,
        tokens_grad,
        small[0],
        small[1],
        query_sum,
        small[2],
        key_sum,
        value_sum,
        small[3],
        out_sum,
        small[4],
        small[5],
        small[6],
        up_grad,
        small[8:].reshape(-1),
        down_grad,
        small[7],
    )


def solution(mesh):
    return jax.shard_map(
        shards,
        mesh=mesh,
        in_specs=(
            P(("dp", "hid", "mp"), None),
            P(("dp", "hid", "mp")),
            P(None, ("dp", "hid", "mp")),
            P(("dp", "hid", "mp"), None),
            P(),
            P(),
            P(("dp", "hid", "mp"), None),
            P(),
            P(("dp", "hid", "mp"), None),
            P(("dp", "hid", "mp"), None),
            P(),
            P(("dp", "hid", "mp"), None),
            P(),
            P(),
            P(),
            P("dp", ("hid", "mp")),
            P(),
            P(("hid", "mp"), "dp"),
            P(),
        ),
        out_specs=(
            P(("dp", "hid", "mp"), None),
            P(("dp", "hid", "mp"), None),
            P(),
            P(),
            P(("dp", "hid", "mp"), None),
            P(),
            P(("dp", "hid", "mp"), None),
            P(("dp", "hid", "mp"), None),
            P(),
            P(("dp", "hid", "mp"), None),
            P(),
            P(),
            P(),
            P("dp", ("hid", "mp")),
            P(),
            P(("hid", "mp"), "dp"),
            P(),
        ),
        check_vma=False,
    )
```

```python
import functools

import jax
import jax.numpy as jnp
from jax import lax
from jax.experimental import pallas as pl
from jax.experimental.pallas import tpu as pltpu
from jax.sharding import PartitionSpec as P

D = 768
HEADS = 12
HEAD = 64
CLUSTERS = 100
SEQ = 1024
PAD = 128


def matmul(left, right):
    return jnp.dot(left, right, preferred_element_type=jnp.float32)


def matmul_nt(left, right):
    return lax.dot_general(left, right, (((1,), (1,)), ((), ())), preferred_element_type=jnp.float32)


def matmul_tn(left, right):
    return lax.dot_general(left, right, (((0,), (0,)), ((), ())), preferred_element_type=jnp.float32)


def swapped(array, axis, mask):
    count = lax.axis_size(axis)
    return lax.ppermute(array, axis, [(i, i ^ mask) for i in range(count)])


def own_bit(axis, bit):
    return (lax.axis_index(axis) >> bit) & 1


def joined(own, other, mine, place):
    own, other = (jnp.expand_dims(own, place), jnp.expand_dims(other, place))
    shape = own.shape[:place] + (2,) + own.shape[place + 1 :]
    return jnp.where(lax.broadcasted_iota(jnp.int32, shape, place) == mine, own, other)


def halves(array, axis, bit, place):
    mine = own_bit(axis, bit)
    take = lambda k: lax.dynamic_index_in_dim(array, k, place, keepdims=False)
    return (take(mine), take(1 - mine))


def high_groups():
    count = lax.axis_size("dp").bit_length() - 1
    return [(b, min(2, count - b)) for b in range(1, count, 2)]


def exchanged(piece, group):
    shift, bits = group
    return [swapped(piece, "dp", d << shift) for d in range(1, 1 << bits)]


def lined_up(own, others, group, place):
    shift, bits = group
    mine = (lax.axis_index("dp") >> shift) & ((1 << bits) - 1)
    pieces = [jnp.expand_dims(p, place) for p in [own, *others]]
    shape = pieces[0].shape[:place] + (1 << bits,) + pieces[0].shape[place + 1 :]
    apart = lax.broadcasted_iota(jnp.int32, shape, place) ^ mine
    out = jnp.broadcast_to(pieces[-1], shape)
    for d in reversed(range(len(pieces) - 1)):
        out = jnp.where(apart == d, pieces[d], out)
    return out


def dealt(array, group, place):
    shift, bits = group
    mine = (lax.axis_index("dp") >> shift) & ((1 << bits) - 1)
    take = lambda k: lax.dynamic_index_in_dim(array, k, place, keepdims=False)
    return [take(mine)] + [swapped(take(mine ^ d), "dp", d << shift) for d in range(1, 1 << bits)]


def summed(pieces):
    return sum(p.astype(jnp.float32) for p in pieces)


def moments(values):
    middle = jnp.mean(values, axis=-1, keepdims=True)
    centered = values - middle
    spread = jnp.mean(centered * centered, axis=-1, keepdims=True)
    return (centered * lax.rsqrt(spread + 1e-05), lax.rsqrt(spread + 1e-05))


def norm_pull(grad, gain, unit, scale):
    scaled = grad * gain
    first = jnp.mean(scaled, axis=-1, keepdims=True)
    second = jnp.mean(scaled * unit, axis=-1, keepdims=True)
    return scale * (scaled - first - unit * second)


def gate_and_slope(v):
    size = jnp.abs(v)
    bell = jnp.exp(-0.5 * v * v)
    t = 1.0 / (1.0 + 0.23164189 * size)
    series = 0.7107068705 + t * (-0.7265760135 + t * 0.5307027145)
    tail = t * (0.127414796 + t * (-0.142248368 + t * series)) * bell
    phi = jnp.where(v < 0, tail, 1.0 - tail)
    return (v * phi, phi + v * (0.3989422804014327 * bell))


def ff_kernel(rows, x, cot, xt, cott, wu, wd, bu, branch_in, mid_in, branch, mid, dwu, dwd, dbu):
    nt = (((1,), (1,)), ((), ()))
    hs, gs = ([], [])
    total = jnp.zeros_like(dbu)
    for r in range(x.shape[0] // rows):
        at = pl.ds(r * rows, rows)
        pre = matmul(x[at, :], wu[...]) + bu[...]
        grad_hidden = matmul(cot[at, :], wd[...])
        h, slope = gate_and_slope(pre)
        h = h.astype(jnp.bfloat16)
        g = (grad_hidden * slope).astype(jnp.bfloat16)
        total += jnp.sum(g.astype(jnp.float32), axis=0, keepdims=True)
        branch[at, :] = branch_in[at, :] + lax.dot_general(h, wd[...], nt, preferred_element_type=jnp.float32)
        mid[at, :] = mid_in[at, :] + lax.dot_general(g, wu[...], nt, preferred_element_type=jnp.float32)
        hs.append(h)
        gs.append(g)
    dwd[...] = matmul(cott[...], jnp.concatenate(hs, axis=0)).astype(jnp.bfloat16)
    dwu[...] = matmul(xt[...], jnp.concatenate(gs, axis=0)).astype(jnp.bfloat16)
    dbu[...] = total


def near(array):
    return pltpu.with_memory_space_constraint(array, pltpu.VMEM)


def ff_block(x, cot, xt, cott, wu, wd, bu, branch, mid):
    f32, bf = (jnp.float32, jnp.bfloat16)
    count, wide = (x.shape[0], wu.shape[1])
    spec = pl.BlockSpec(memory_space=pltpu.VMEM)
    return pl.pallas_call(
        functools.partial(ff_kernel, 256),
        out_shape=(
            jax.ShapeDtypeStruct((count, D), f32),
            jax.ShapeDtypeStruct((count, D), f32),
            jax.ShapeDtypeStruct((D, wide), bf),
            jax.ShapeDtypeStruct((D, wide), bf),
            jax.ShapeDtypeStruct((1, wide), f32),
        ),
        in_specs=[spec] * 9,
        out_specs=(spec,) * 5,
        input_output_aliases={7: 0, 8: 1},
        compiler_params=pltpu.CompilerParams(vmem_limit_bytes=24 * 1024 * 1024),
        cost_estimate=pl.CostEstimate(
            flops=12 * count * D * wide, bytes_accessed=4 * D * wide, transcendentals=2 * count * wide
        ),
        name="ff_block",
    )(x, cot, xt, cott, near(wu), near(wd), bu, branch, mid)


def tied(*arrays):
    return lax.optimization_barrier(arrays)


def added(own, got):
    return (own.astype(jnp.float32) + got.astype(jnp.float32)).astype(jnp.bfloat16)


def dot(a, b, ca=1, cb=0):
    return lax.dot_general(a, b, (((ca,), (cb,)), ((), ())), preferred_element_type=jnp.float32)


def own_half(wide):
    rows = lax.broadcasted_iota(jnp.int32, wide.shape, 0) // PAD
    columns = lax.broadcasted_iota(jnp.int32, wide.shape, 1) // HEAD
    return jnp.where(rows == columns, wide, 0.0)


def pair_rows(ids):
    at = lax.broadcasted_iota(jnp.int32, (PAD, SEQ), 0)
    return jnp.concatenate([jnp.where(ids[k : k + 1, :] == at, 1.0, 0.0) for k in (0, 1)], axis=0).astype(jnp.bfloat16)


def pair_columns(ids):
    at = lax.broadcasted_iota(jnp.int32, (SEQ, PAD), 1)
    return jnp.concatenate([jnp.where(ids[:, k : k + 1] == at, 1.0, 0.0) for k in (0, 1)], axis=1).astype(jnp.bfloat16)


def attend_kernel(q, k, v, rows, columns, seg_row, seg_col, mixed, prob, centroid, count):
    bf = jnp.bfloat16
    hot = pair_rows(rows[0])
    lanes = lax.broadcasted_iota(jnp.int32, (SEQ, PAD), 1)
    marks = jnp.where(lanes == 0, seg_col[...], jnp.where(lanes == 1, 1.0, 0.0)).astype(bf)
    sums = dot(hot, jnp.concatenate([q[...], marks], axis=1))
    owner, counts = (sums[:, 128:129], sums[:, 129:130])
    counts = jnp.maximum(counts, 1.0)
    middle = own_half(sums[:, :128] / counts).astype(bf)
    scores = 0.125 * dot(middle, k[...], 1, 1)
    allowed = jnp.abs(owner - counts * seg_row[...]) < 0.5
    masked = jnp.where(allowed, scores, -1e30)
    highest = jnp.max(masked, axis=1, keepdims=True)
    exponent = jnp.where(allowed, jnp.exp(masked - highest), 0.0)
    total = jnp.sum(exponent, axis=1, keepdims=True)
    p = exponent * (1.0 / jnp.maximum(total, 1e-30))
    context = own_half(dot(p.astype(bf), v[...])).astype(bf)
    mixed[...] = dot(pair_columns(columns[0]), context).astype(bf)
    prob[0] = p
    centroid[0] = middle
    count[0] = jnp.broadcast_to(counts, (2 * PAD, 128))


def attend(q, k, v, rows, columns, seg_row, seg_col):
    bf = jnp.bfloat16
    pair = pl.BlockSpec((SEQ, 128), lambda i: (0, i))
    return pl.pallas_call(
        attend_kernel,
        grid=(HEADS // 2,),
        in_specs=[pair, pair, pair,
            pl.BlockSpec((1, 2, SEQ), lambda i: (i, 0, 0)),
            pl.BlockSpec((1, SEQ, 2), lambda i: (i, 0, 0)),
            pl.BlockSpec((1, SEQ), lambda i: (0, 0)),
            pl.BlockSpec((SEQ, 1), lambda i: (0, 0))],
        out_specs=(pair, pl.BlockSpec((1, 2 * PAD, SEQ), lambda i: (i, 0, 0)), pl.BlockSpec((1, 2 * PAD, 128), lambda i: (i, 0, 0)), pl.BlockSpec((1, 2 * PAD, 128), lambda i: (i, 0, 0))),
        out_shape=(jax.ShapeDtypeStruct((SEQ, D), bf), jax.ShapeDtypeStruct((HEADS // 2, 2 * PAD, SEQ), jnp.float32), jax.ShapeDtypeStruct((HEADS // 2, 2 * PAD, 128), bf), jax.ShapeDtypeStruct((HEADS // 2, 2 * PAD, 128), jnp.float32)),
        cost_estimate=pl.CostEstimate(flops=12 * 5 * 2 * PAD * SEQ * HEAD, bytes_accessed=14 << 20, transcendentals=HEADS * PAD * SEQ),
        name="attend",
    )(q, k, v, rows, columns, seg_row, seg_col)


def attend_back_kernel(k, v, gm, rows, columns, prob, centroid, count, gq, gk, gv):
    bf = jnp.bfloat16
    hot = pair_rows(rows[0])
    p = prob[0]
    grad_context = own_half(dot(hot, gm[...])).astype(bf)
    gv[...] = dot(p.astype(bf), grad_context, 0, 0).astype(bf)
    grad_prob = dot(grad_context, v[...], 1, 1)
    grad_scores = (p * (grad_prob - jnp.sum(p * grad_prob, axis=1, keepdims=True))).astype(bf)
    grad_centroid = own_half(0.125 * dot(grad_scores, k[...]) / count[0]).astype(bf)
    gk[...] = (0.125 * dot(grad_scores, centroid[0], 0, 0)).astype(bf)
    gq[...] = dot(pair_columns(columns[0]), grad_centroid).astype(bf)


def attend_back(k, v, gm, rows, columns, prob, centroid, count):
    bf = jnp.bfloat16
    pair = pl.BlockSpec((SEQ, 128), lambda i: (0, i))
    wide = pl.BlockSpec((1, 2 * PAD, 128), lambda i: (i, 0, 0))
    out = jax.ShapeDtypeStruct((SEQ, D), bf)
    return pl.pallas_call(
        attend_back_kernel,
        grid=(HEADS // 2,),
        in_specs=[pair, pair, pair,
            pl.BlockSpec((1, 2, SEQ), lambda i: (i, 0, 0)),
            pl.BlockSpec((1, SEQ, 2), lambda i: (i, 0, 0)),
            pl.BlockSpec((1, 2 * PAD, SEQ), lambda i: (i, 0, 0)), wide, wide],
        out_specs=(pair, pair, pair),
        out_shape=(out, out, out),
        cost_estimate=pl.CostEstimate(flops=12 * 7 * 2 * PAD * SEQ * HEAD, bytes_accessed=16 << 20, transcendentals=0),
        name="attend_back",
    )(k, v, gm, rows, columns, prob, centroid, count)


def shards(
    tokens,
    segment_ids,
    cluster_ids,
    cotangent,
    first_gain,
    first_shift,
    w_query,
    b_query,
    w_key,
    w_value,
    b_value,
    w_out,
    b_out,
    second_gain,
    second_shift,
    w_up,
    b_up,
    w_down,
    b_down,
):
    groups = high_groups()
    tops = 1 << sum(bits for _, bits in groups)
    bf = jnp.bfloat16
    part = D // (8 * tops)
    wide = D // (2 * tops)
    whole = [1 << bits for _, bits in reversed(groups)]

    attn = jnp.stack([w.astype(bf) for w in (w_query, w_key, w_value, w_out)])
    ff = jnp.stack([w_up.astype(bf), w_down.T.astype(bf)])
    inputs = tokens.astype(jnp.float32)
    unit_in, scale_in = moments(inputs)
    normed_in = (unit_in * first_gain + first_shift).astype(bf)
    id_rows = cluster_ids.reshape(HEADS // 2, 2, SEQ)
    id_columns = id_rows.transpose(0, 2, 1)
    seg = segment_ids.astype(jnp.float32)
    seg_row, seg_col = (seg[None, :], seg[:, None])
    for group in groups:
        got = exchanged(attn, group)
        normed_in, id_columns, seg_col, *got = tied(normed_in, id_columns, seg_col, *got)
        attn = lined_up(attn, got, group, 1)
    attn = attn.reshape(4, tops, part, D)
    first, second = (attn[:2], attn[2:])
    first_got, second_got = (swapped(first, "dp", 1), swapped(second, "hid", 1))
    for group in groups[:-1]:
        ff = lined_up(ff, exchanged(ff, group), group, 1)
    ff_got = exchanged(ff, groups[-1])
    first = joined(first, first_got, own_bit("dp", 0), 2)
    second = joined(second, second_got, own_bit("hid", 0), 2)
    first_got, second_got = (swapped(first, "hid", 1), swapped(second, "dp", 1))
    first_got, second_got, *ff_got = tied(first_got, second_got, *ff_got)
    ff = lined_up(ff, ff_got, groups[-1], 1)
    up, down = ff.reshape(2, tops, wide, D)
    up_got, down_got = (swapped(up, "dp", 1), swapped(down, "hid", 1))
    first = joined(first, first_got, own_bit("hid", 0), 3)
    second = joined(second, second_got, own_bit("dp", 0), 2)
    first_got, second_got = (swapped(first, "mp", 1), swapped(second, "mp", 1))
    first = joined(first, first_got, own_bit("mp", 0), 4)
    second = joined(second, second_got, own_bit("mp", 0), 4)
    query_full, key_full = first.reshape(2, D, D)
    value_full, out_full = second.reshape(2, D, D)

    query = (matmul(normed_in, query_full) + b_query).astype(bf)
    key_rows = matmul(normed_in, key_full).astype(bf)
    value_rows = (matmul(normed_in, value_full) + b_value).astype(bf)
    query, key_rows, value_rows, up_got, down_got = tied(query, key_rows, value_rows, up_got, down_got)
    up = joined(up, up_got, own_bit("dp", 0), 1).reshape(D, D)
    up_mate = swapped(up, "hid", 1)
    down = jnp.stack([down, down_got])
    down_got = swapped(down, "dp", 1)
    mixed, probability, centroid, counts = attend(
        query, key_rows, value_rows, id_rows, id_columns, seg_row, seg_col
    )
    residual = inputs + matmul(mixed, out_full) + b_out
    unit_mid, scale_mid = moments(residual)
    normed_mid = (unit_mid * second_gain + second_shift).astype(bf)
    normed_mid, up_mate, down_got = tied(normed_mid, up_mate, down_got)
    down, down_mate = joined(down, down_got, own_bit("dp", 0), 2).reshape(2, D, D)
    me = lax.axis_index(("hid", "mp"))
    blocks = [me ^ 2, me ^ 3, me, me ^ 1]
    ups = [up_mate, swapped(up_mate, "mp", 1), up, swapped(up, "mp", 1)]
    downs = [down_mate, swapped(down_mate, "mp", 1), down, swapped(down, "mp", 1)]

    x, x_t, cot, cot_t = (near(normed_mid), near(normed_mid.T), near(cotangent), near(cotangent.T))
    branch, grad_mid = (near(residual + b_down), near(jnp.zeros((SEQ, D), jnp.float32)))
    up_sends, down_sends, bias_up = ([], [], jnp.zeros((4, D), jnp.float32))
    for k in range(4):
        up_bias = lax.dynamic_slice_in_dim(b_up, blocks[k] * D, D)[None]
        branch, grad_mid, up_send, down_send, bias = ff_block(
            x, cot, x_t, cot_t, ups[k], downs[k], up_bias, branch, grad_mid
        )
        up_sends.append(up_send)
        down_sends.append(down_send)
        bias_up = lax.dynamic_update_slice(bias_up, bias, (blocks[k], 0))
        if k == 1:
            got = (swapped(up_send, "mp", 1), swapped(down_send, "mp", 1))
        if k == 2:
            up_send, *got = tied(up_send, *got)
            up_far, down_far = (added(up_sends[0], got[0]), added(down_sends[0], got[1]))
            up_sends[2] = up_send
            up_far = swapped(up_far, "hid", 1)
            down_far, sent = halves(down_far.reshape(tops, 2, wide, D), "dp", 0, 1)
            down_far_got = swapped(sent, "dp", 1)
        if k == 3:
            got = (swapped(up_send, "mp", 1), swapped(down_send, "mp", 1))
    output = branch.astype(bf)

    grad_out = cotangent.astype(jnp.float32)
    second_shift_grad = jnp.sum(grad_mid, axis=0)
    second_gain_grad = jnp.sum(grad_mid * unit_mid, axis=0)
    grad_resid = grad_out + norm_pull(grad_mid, second_gain, unit_mid, scale_mid)
    grad_branch = grad_resid.astype(bf)
    grad_branch, down_far_got, *got = tied(grad_branch, down_far_got, *got)
    up_near, down_near = (added(up_sends[2], got[0]), added(down_sends[2], got[1]))
    down_near, sent = halves(down_near.reshape(tops, 2, wide, D), "dp", 0, 1)
    down_near_got = swapped(sent, "dp", 1)
    down_far = added(down_far, down_far_got)
    down_got = swapped(down_far, "hid", 1)
    grad_mixed = matmul_nt(grad_branch, out_full).astype(bf)
    grad_mixed, up_far = tied(grad_mixed, up_far)
    up_near = added(up_near, up_far).reshape(tops, 2, wide, D)
    up_near, sent = halves(up_near, "dp", 0, 1)
    up_got = swapped(sent, "dp", 1)
    out_grad = matmul_tn(mixed, grad_branch).astype(bf)

    grad_query, grad_key, grad_value = attend_back(
        key_rows, value_rows, grad_mixed, id_rows, id_columns, probability, centroid, counts
    )
    grad_value, up_got, down_got, down_near_got = tied(grad_value, up_got, down_got, down_near_got)
    ff = jnp.stack([added(up_near, up_got), summed([down_near, down_near_got, down_got]).astype(bf)])
    ff = ff.reshape(2, *whole, wide, D)
    ff_parts = dealt(ff, groups[-1], 1)

    def pair(left, right):
        both = jnp.stack([left, right]).reshape(2, tops, 2, 2, 2, part, D)
        both, sent = halves(both, "mp", 0, 4)
        both = added(both, swapped(sent, "mp", 1))
        one, one_sent = halves(both[0], "dp", 0, 1)
        two, two_sent = halves(both[1], "hid", 0, 2)
        one_got, two_got = (swapped(one_sent, "dp", 1), swapped(two_sent, "hid", 1))
        return (one, two, one_got, two_got)

    def pair_on(one, two, one_got, two_got):
        one, one_sent = halves(added(one, one_got), "hid", 0, 1)
        two, two_sent = halves(added(two, two_got), "dp", 0, 1)
        return (one, two, swapped(one_sent, "hid", 1), swapped(two_sent, "dp", 1))

    def pair_up(one, two, one_got, two_got):
        both = jnp.stack([added(one, one_got), added(two, two_got)]).reshape(2, *whole, part, D)
        for group in reversed(groups[1:]):
            both = summed(dealt(both, group, 1)).astype(bf)
        return dealt(both, groups[0], 1)

    value_grad = matmul_tn(normed_in, grad_value).astype(bf)
    vo = pair(value_grad, out_grad)
    key_grad = matmul_tn(normed_in, grad_key).astype(bf)
    query_grad = matmul_tn(normed_in, grad_query).astype(bf)
    key_grad, query_grad, *vo = tied(key_grad, query_grad, *vo)
    vo = pair_on(*vo)
    qk = pair(query_grad, key_grad)
    grad_in = matmul_nt(grad_query, query_full) + matmul_nt(grad_key, key_full) + matmul_nt(grad_value, value_full)
    grad_in, *qk = tied(grad_in, *qk)
    qk = pair_on(*qk)
    tokens_grad = (grad_resid + norm_pull(grad_in, first_gain, unit_in, scale_in)).astype(bf)
    total = lambda rows: jnp.sum(rows.astype(jnp.float32), axis=0)
    small = jnp.concatenate(
        [
            jnp.stack(
                [
                    jnp.sum(grad_in * unit_in, axis=0),
                    jnp.sum(grad_in, axis=0),
                    total(grad_query),
                    total(grad_value),
                    total(grad_branch),
                    second_gain_grad,
                    second_shift_grad,
                    total(cotangent),
                ]
            ),
            bias_up,
        ]
    )
    small, *vo = tied(small, *vo)
    vo_parts = pair_up(*vo)
    small = small + swapped(small, "mp", 1)
    small_got = swapped(small, "hid", 1)
    small_got, *qk = tied(small_got, *qk)
    qk_parts = pair_up(*qk)
    small = small + small_got
    small = small + swapped(small, "dp", 1)
    for group in groups:
        small = summed([small, *exchanged(small, group)])
    for group in reversed(groups[:-1]):
        ff_parts = dealt(summed(ff_parts).astype(bf), group, 1)
    up_grad, down_grad = summed(ff_parts)
    down_grad = down_grad.T
    value_sum, out_sum = summed(vo_parts)
    query_sum, key_sum = summed(qk_parts)
    return (
        output,
        tokens_grad,
        small[0],
        small[1],
        query_sum,
        small[2],
        key_sum,
        value_sum,
        small[3],
        out_sum,
        small[4],
        small[5],
        small[6],
        up_grad,
        small[8:].reshape(-1),
        down_grad,
        small[7],
    )


def solution(mesh):
    return jax.shard_map(
        shards,
        mesh=mesh,
        in_specs=(
            P(("dp", "hid", "mp"), None),
            P(("dp", "hid", "mp")),
            P(None, ("dp", "hid", "mp")),
            P(("dp", "hid", "mp"), None),
            P(),
            P(),
            P(("dp", "hid", "mp"), None),
            P(),
            P(("dp", "hid", "mp"), None),
            P(("dp", "hid", "mp"), None),
            P(),
            P(("dp", "hid", "mp"), None),
            P(),
            P(),
            P(),
            P("dp", ("hid", "mp")),
            P(),
            P(("hid", "mp"), "dp"),
            P(),
        ),
        out_specs=(
            P(("dp", "hid", "mp"), None),
            P(("dp", "hid", "mp"), None),
            P(),
            P(),
            P(("dp", "hid", "mp"), None),
            P(),
            P(("dp", "hid", "mp"), None),
            P(("dp", "hid", "mp"), None),
            P(),
            P(("dp", "hid", "mp"), None),
            P(),
            P(),
            P(),
            P("dp", ("hid", "mp")),
            P(),
            P(("hid", "mp"), "dp"),
            P(),
        ),
        check_vma=False,
    )
```

```python
import functools

import jax
import jax.numpy as jnp
from jax import lax
from jax.experimental import pallas as pl
from jax.experimental.pallas import tpu as pltpu
from jax.sharding import PartitionSpec as P

D = 768
HEADS = 12
HEAD = 64
CLUSTERS = 100
SEQ = 1024
PAD = 128


def matmul(left, right):
    return jnp.dot(left, right, preferred_element_type=jnp.float32)


def matmul_nt(left, right):
    return lax.dot_general(left, right, (((1,), (1,)), ((), ())), preferred_element_type=jnp.float32)


def matmul_tn(left, right):
    return lax.dot_general(left, right, (((0,), (0,)), ((), ())), preferred_element_type=jnp.float32)


def swapped(array, axis, mask):
    count = lax.axis_size(axis)
    return lax.ppermute(array, axis, [(i, i ^ mask) for i in range(count)])


def own_bit(axis, bit):
    return (lax.axis_index(axis) >> bit) & 1


def joined(own, other, mine, place):
    own, other = (jnp.expand_dims(own, place), jnp.expand_dims(other, place))
    shape = own.shape[:place] + (2,) + own.shape[place + 1 :]
    return jnp.where(lax.broadcasted_iota(jnp.int32, shape, place) == mine, own, other)


def halves(array, axis, bit, place):
    mine = own_bit(axis, bit)
    take = lambda k: lax.dynamic_index_in_dim(array, k, place, keepdims=False)
    return (take(mine), take(1 - mine))


def high_groups():
    count = lax.axis_size("dp").bit_length() - 1
    return [(b, min(2, count - b)) for b in range(1, count, 2)]


def exchanged(piece, group):
    shift, bits = group
    return [swapped(piece, "dp", d << shift) for d in range(1, 1 << bits)]


def lined_up(own, others, group, place):
    shift, bits = group
    mine = (lax.axis_index("dp") >> shift) & ((1 << bits) - 1)
    pieces = [jnp.expand_dims(p, place) for p in [own, *others]]
    shape = pieces[0].shape[:place] + (1 << bits,) + pieces[0].shape[place + 1 :]
    apart = lax.broadcasted_iota(jnp.int32, shape, place) ^ mine
    out = jnp.broadcast_to(pieces[-1], shape)
    for d in reversed(range(len(pieces) - 1)):
        out = jnp.where(apart == d, pieces[d], out)
    return out


def dealt(array, group, place):
    shift, bits = group
    mine = (lax.axis_index("dp") >> shift) & ((1 << bits) - 1)
    take = lambda k: lax.dynamic_index_in_dim(array, k, place, keepdims=False)
    return [take(mine)] + [swapped(take(mine ^ d), "dp", d << shift) for d in range(1, 1 << bits)]


def summed(pieces):
    return sum(p.astype(jnp.float32) for p in pieces)


def moments(values):
    middle = jnp.mean(values, axis=-1, keepdims=True)
    centered = values - middle
    spread = jnp.mean(centered * centered, axis=-1, keepdims=True)
    return (centered * lax.rsqrt(spread + 1e-05), lax.rsqrt(spread + 1e-05))


def norm_pull(grad, gain, unit, scale):
    scaled = grad * gain
    first = jnp.mean(scaled, axis=-1, keepdims=True)
    second = jnp.mean(scaled * unit, axis=-1, keepdims=True)
    return scale * (scaled - first - unit * second)


def gate_and_slope(v):
    size = jnp.abs(v)
    bell = jnp.exp(-0.5 * v * v)
    t = 1.0 / (1.0 + 0.23164189 * size)
    series = 0.7107068705 + t * (-0.7265760135 + t * 0.5307027145)
    tail = t * (0.127414796 + t * (-0.142248368 + t * series)) * bell
    phi = jnp.where(v < 0, tail, 1.0 - tail)
    return (v * phi, phi + v * (0.3989422804014327 * bell))


def ff_kernel(rows, up_at, down_at, x, cot, xt, cott, up_in, down_in, bu, branch_in, mid_in, branch, mid, grads, dbu, wu, wd, dw, sems):
    nt = (((1,), (1,)), ((), ()))
    up_copy = pltpu.make_async_copy(up_in.at[up_at], wu, sems.at[0])
    down_copy = pltpu.make_async_copy(down_in.at[down_at], wd, sems.at[1])
    up_copy.start()
    down_copy.start()
    up_copy.wait()
    hs, gs = ([], [])
    total = jnp.zeros_like(dbu)
    for r in range(x.shape[0] // rows):
        at = pl.ds(r * rows, rows)
        pre = matmul(x[at, :], wu[...]) + bu[...]
        if r == 0:
            down_copy.wait()
        grad_hidden = matmul(cot[at, :], wd[...])
        h, slope = gate_and_slope(pre)
        h = h.astype(jnp.bfloat16)
        g = (grad_hidden * slope).astype(jnp.bfloat16)
        total += jnp.sum(g.astype(jnp.float32), axis=0, keepdims=True)
        branch[at, :] = branch_in[at, :] + lax.dot_general(h, wd[...], nt, preferred_element_type=jnp.float32)
        mid[at, :] = mid_in[at, :] + lax.dot_general(g, wu[...], nt, preferred_element_type=jnp.float32)
        hs.append(h)
        gs.append(g)
    dbu[...] = total
    dw[1] = matmul(cott[...], jnp.concatenate(hs, axis=0)).astype(jnp.bfloat16)
    down_out = pltpu.make_async_copy(dw.at[1], grads.at[1], sems.at[1])
    down_out.start()
    dw[0] = matmul(xt[...], jnp.concatenate(gs, axis=0)).astype(jnp.bfloat16)
    up_out = pltpu.make_async_copy(dw.at[0], grads.at[0], sems.at[0])
    up_out.start()
    down_out.wait()
    up_out.wait()


def near(array):
    return pltpu.with_memory_space_constraint(array, pltpu.VMEM)


def ff_block(x, cot, xt, cott, up, up_at, down, down_at, bu, branch, mid):
    f32, bf = (jnp.float32, jnp.bfloat16)
    count, wide = (x.shape[0], up.shape[2])
    spec = pl.BlockSpec(memory_space=pltpu.VMEM)
    far = pl.BlockSpec(memory_space=pl.ANY)
    return pl.pallas_call(
        functools.partial(ff_kernel, 256, up_at, down_at),
        out_shape=(
            jax.ShapeDtypeStruct((count, D), f32),
            jax.ShapeDtypeStruct((count, D), f32),
            jax.ShapeDtypeStruct((2, D, wide), bf),
            jax.ShapeDtypeStruct((1, wide), f32),
        ),
        in_specs=[spec, spec, spec, spec, far, far, spec, spec, spec],
        out_specs=(spec, spec, far, spec),
        scratch_shapes=[
            pltpu.VMEM((D, wide), bf),
            pltpu.VMEM((D, wide), bf),
            pltpu.VMEM((2, D, wide), bf),
            pltpu.SemaphoreType.DMA((2,)),
        ],
        input_output_aliases={7: 0, 8: 1},
        compiler_params=pltpu.CompilerParams(vmem_limit_bytes=24 * 1024 * 1024),
        cost_estimate=pl.CostEstimate(
            flops=12 * count * D * wide, bytes_accessed=4 * D * wide, transcendentals=2 * count * wide
        ),
        name="ff_block",
    )(x, cot, xt, cott, up, down, bu, branch, mid)


def tied(*arrays):
    return lax.optimization_barrier(arrays)


def packed(sent, small):
    high = small.astype(jnp.bfloat16)
    low = (small - high.astype(jnp.float32)).astype(jnp.bfloat16)
    return jnp.concatenate([sent.reshape(-1, D), high, low])


def unpacked(got, like):
    rows = like.size // D
    high, low = jnp.split(got[rows:].astype(jnp.float32), 2)
    return (got[:rows].reshape(like.shape), high + low)


def added(own, got):
    return (own.astype(jnp.float32) + got.astype(jnp.float32)).astype(jnp.bfloat16)


def dot(a, b, ca=1, cb=0):
    return lax.dot_general(a, b, (((ca,), (cb,)), ((), ())), preferred_element_type=jnp.float32)


def own_half(wide):
    rows = lax.broadcasted_iota(jnp.int32, wide.shape, 0) // PAD
    columns = lax.broadcasted_iota(jnp.int32, wide.shape, 1) // HEAD
    return jnp.where(rows == columns, wide, 0.0)


def pair_rows(ids):
    at = lax.broadcasted_iota(jnp.int32, (PAD, SEQ), 0)
    return jnp.concatenate([jnp.where(ids[k : k + 1, :] == at, 1.0, 0.0) for k in (0, 1)], axis=0).astype(jnp.bfloat16)


def pair_columns(ids):
    at = lax.broadcasted_iota(jnp.int32, (SEQ, PAD), 1)
    return jnp.concatenate([jnp.where(ids[:, k : k + 1] == at, 1.0, 0.0) for k in (0, 1)], axis=1).astype(jnp.bfloat16)


def attend_kernel(q, k, v, rows, columns, seg_row, seg_col, mixed, prob, centroid, count):
    bf = jnp.bfloat16
    hot = pair_rows(rows[0])
    lanes = lax.broadcasted_iota(jnp.int32, (SEQ, PAD), 1)
    marks = jnp.where(lanes == 0, seg_col[...], jnp.where(lanes == 1, 1.0, 0.0)).astype(bf)
    sums = dot(hot, jnp.concatenate([q[...], marks], axis=1))
    owner, counts = (sums[:, 128:129], sums[:, 129:130])
    counts = jnp.maximum(counts, 1.0)
    middle = own_half(sums[:, :128] / counts).astype(bf)
    scores = 0.125 * dot(middle, k[...], 1, 1)
    allowed = jnp.abs(owner - counts * seg_row[...]) < 0.5
    masked = jnp.where(allowed, scores, -1e30)
    highest = jnp.max(masked, axis=1, keepdims=True)
    exponent = jnp.where(allowed, jnp.exp(masked - highest), 0.0)
    total = jnp.sum(exponent, axis=1, keepdims=True)
    p = exponent * (1.0 / jnp.maximum(total, 1e-30))
    context = own_half(dot(p.astype(bf), v[...])).astype(bf)
    mixed[...] = dot(pair_columns(columns[0]), context).astype(bf)
    prob[0] = p
    centroid[0] = middle
    count[0] = jnp.broadcast_to(counts, (2 * PAD, 128))


def attend(q, k, v, rows, columns, seg_row, seg_col):
    bf = jnp.bfloat16
    pair = pl.BlockSpec((SEQ, 128), lambda i: (0, i))
    return pl.pallas_call(
        attend_kernel,
        grid=(HEADS // 2,),
        in_specs=[pair, pair, pair,
            pl.BlockSpec((1, 2, SEQ), lambda i: (i, 0, 0)),
            pl.BlockSpec((1, SEQ, 2), lambda i: (i, 0, 0)),
            pl.BlockSpec((1, SEQ), lambda i: (0, 0)),
            pl.BlockSpec((SEQ, 1), lambda i: (0, 0))],
        out_specs=(pair, pl.BlockSpec((1, 2 * PAD, SEQ), lambda i: (i, 0, 0)), pl.BlockSpec((1, 2 * PAD, 128), lambda i: (i, 0, 0)), pl.BlockSpec((1, 2 * PAD, 128), lambda i: (i, 0, 0))),
        out_shape=(jax.ShapeDtypeStruct((SEQ, D), bf), jax.ShapeDtypeStruct((HEADS // 2, 2 * PAD, SEQ), jnp.float32), jax.ShapeDtypeStruct((HEADS // 2, 2 * PAD, 128), bf), jax.ShapeDtypeStruct((HEADS // 2, 2 * PAD, 128), jnp.float32)),
        cost_estimate=pl.CostEstimate(flops=12 * 5 * 2 * PAD * SEQ * HEAD, bytes_accessed=14 << 20, transcendentals=HEADS * PAD * SEQ),
        compiler_params=pltpu.CompilerParams(vmem_limit_bytes=24 * 1024 * 1024),
        name="attend",
    )(q, k, v, rows, columns, seg_row, seg_col)


def attend_back_kernel(k, v, gm, rows, columns, prob, centroid, count, gq, gk, gv):
    bf = jnp.bfloat16
    hot = pair_rows(rows[0])
    p = prob[0]
    grad_context = own_half(dot(hot, gm[...])).astype(bf)
    gv[...] = dot(p.astype(bf), grad_context, 0, 0).astype(bf)
    grad_prob = dot(grad_context, v[...], 1, 1)
    grad_scores = (p * (grad_prob - jnp.sum(p * grad_prob, axis=1, keepdims=True))).astype(bf)
    grad_centroid = own_half(0.125 * dot(grad_scores, k[...]) / count[0]).astype(bf)
    gk[...] = (0.125 * dot(grad_scores, centroid[0], 0, 0)).astype(bf)
    gq[...] = dot(pair_columns(columns[0]), grad_centroid).astype(bf)


def attend_back(k, v, gm, rows, columns, prob, centroid, count):
    bf = jnp.bfloat16
    pair = pl.BlockSpec((SEQ, 128), lambda i: (0, i))
    wide = pl.BlockSpec((1, 2 * PAD, 128), lambda i: (i, 0, 0))
    out = jax.ShapeDtypeStruct((SEQ, D), bf)
    return pl.pallas_call(
        attend_back_kernel,
        grid=(HEADS // 2,),
        in_specs=[pair, pair, pair,
            pl.BlockSpec((1, 2, SEQ), lambda i: (i, 0, 0)),
            pl.BlockSpec((1, SEQ, 2), lambda i: (i, 0, 0)),
            pl.BlockSpec((1, 2 * PAD, SEQ), lambda i: (i, 0, 0)), wide, wide],
        out_specs=(pair, pair, pair),
        out_shape=(out, out, out),
        cost_estimate=pl.CostEstimate(flops=12 * 7 * 2 * PAD * SEQ * HEAD, bytes_accessed=16 << 20, transcendentals=0),
        compiler_params=pltpu.CompilerParams(vmem_limit_bytes=24 * 1024 * 1024),
        name="attend_back",
    )(k, v, gm, rows, columns, prob, centroid, count)


def shards(
    tokens,
    segment_ids,
    cluster_ids,
    cotangent,
    first_gain,
    first_shift,
    w_query,
    b_query,
    w_key,
    w_value,
    b_value,
    w_out,
    b_out,
    second_gain,
    second_shift,
    w_up,
    b_up,
    w_down,
    b_down,
):
    groups = high_groups()
    tops = 1 << sum(bits for _, bits in groups)
    bf = jnp.bfloat16
    part = D // (8 * tops)
    wide = D // (2 * tops)
    whole = [1 << bits for _, bits in reversed(groups)]

    attn = jnp.stack([w.astype(bf) for w in (w_query, w_key, w_value, w_out)])
    ff = jnp.stack([w_up.astype(bf), w_down.T.astype(bf)])
    inputs = tokens.astype(jnp.float32)
    unit_in, scale_in = moments(inputs)
    normed_in = (unit_in * first_gain + first_shift).astype(bf)
    id_rows = cluster_ids.reshape(HEADS // 2, 2, SEQ)
    id_columns = id_rows.transpose(0, 2, 1)
    seg = segment_ids.astype(jnp.float32)
    seg_row, seg_col = (seg[None, :], seg[:, None])
    cot_t = cotangent.T
    for group in groups:
        got = exchanged(attn, group)
        normed_in, id_columns, seg_col, *got = tied(normed_in, id_columns, seg_col, *got)
        attn = lined_up(attn, got, group, 1)
    attn = attn.reshape(4, tops, part, D)
    first, second = (attn[:2], attn[2:])
    first_got, second_got = (swapped(first, "dp", 1), swapped(second, "hid", 1))
    for group in groups[:-1]:
        ff = lined_up(ff, exchanged(ff, group), group, 1)
    ff_got = exchanged(ff, groups[-1])
    cot_t, first_got, second_got = tied(cot_t, first_got, second_got)
    first = joined(first, first_got, own_bit("dp", 0), 2)
    second = joined(second, second_got, own_bit("hid", 0), 2)
    first_got, second_got = (swapped(first, "hid", 1), swapped(second, "dp", 1))
    first = joined(first, first_got, own_bit("hid", 0), 3)
    second = joined(second, second_got, own_bit("dp", 0), 2)
    first_got, second_got = (swapped(first, "mp", 1), swapped(second, "mp", 1))
    first = joined(first, first_got, own_bit("mp", 0), 4)
    second = joined(second, second_got, own_bit("mp", 0), 4)
    query_full, key_full = first.reshape(2, D, D)
    value_full, out_full = second.reshape(2, D, D)

    query = (matmul(normed_in, query_full) + b_query).astype(bf)
    query, *ff_got = tied(query, *ff_got)
    ff = lined_up(ff, ff_got, groups[-1], 1)
    up, down = ff.reshape(2, tops, wide, D)
    up_got, down_got = (swapped(up, "dp", 1), swapped(down, "hid", 1))
    key_rows = matmul(normed_in, key_full).astype(bf)
    value_rows = (matmul(normed_in, value_full) + b_value).astype(bf)
    mixed, probability, centroid, counts = attend(
        query, key_rows, value_rows, id_rows, id_columns, seg_row, seg_col
    )
    mixed, up_got, down_got = tied(mixed, up_got, down_got)
    up = joined(up, up_got, own_bit("dp", 0), 1).reshape(1, D, D)
    up_mate = swapped(up, "hid", 1)
    up_next = swapped(up, "mp", 1)
    down = jnp.stack([down, down_got])
    down_got = swapped(down, "dp", 1)
    residual = inputs + matmul(mixed, out_full) + b_out
    unit_mid, scale_mid = moments(residual)
    normed_mid = (unit_mid * second_gain + second_shift).astype(bf)
    x, x_t, cot, cot_t = (near(normed_mid), near(normed_mid.T), near(cotangent), near(cot_t))
    branch, grad_mid = (near(residual + b_down), near(jnp.zeros((SEQ, D), jnp.float32)))
    x, x_t, branch, up_mate, down_got = tied(x, x_t, branch, up_mate, down_got)
    down = joined(down, down_got, own_bit("dp", 0), 2).reshape(2, D, D)
    down_next = swapped(down, "mp", 1)
    up_across = swapped(up_mate, "mp", 1)
    me = lax.axis_index(("hid", "mp"))
    blocks = [(me ^ 2, up_mate, down, 1), (me ^ 3, up_across, down_next, 1), (me ^ 1, up_next, down_next, 0), (me, up, down, 0)]
    bias_up = jnp.zeros((4, D), jnp.float32)
    sends = []
    for k, (block, up_rows, down_rows, down_at) in enumerate(blocks):
        up_bias = lax.dynamic_slice_in_dim(b_up, block * D, D)[None]
        branch, grad_mid, send, bias = ff_block(
            x, cot, x_t, cot_t, up_rows, 0, down_rows, down_at, up_bias, branch, grad_mid
        )
        bias_up = lax.dynamic_update_slice(bias_up, bias, (block, 0))
        sends.append(send)
        if k == 1:
            far_got = swapped(send, "mp", 1)
        if k == 2:
            near_got = swapped(send, "mp", 1)
            far = added(sends[0], far_got)
            up_far = far[0]
            down_far, down_sent = halves(far[1].reshape(tops, 2, wide, D), "dp", 0, 1)
            branch, up_far, down_sent = tied(branch, up_far, down_sent)
            up_far_got = swapped(up_far, "hid", 1)
            down_far_got = swapped(down_sent, "dp", 1)
    output = branch.astype(bf)

    near_sum = added(sends[3], near_got)
    up_near, down_near = (near_sum[0], near_sum[1])
    down_near, down_sent = halves(down_near.reshape(tops, 2, wide, D), "dp", 0, 1)
    down_far = added(down_far, down_far_got)
    grad_mid, down_sent, down_far, up_near = tied(grad_mid, down_sent, down_far, up_near)
    down_near_got = swapped(down_sent, "dp", 1)
    down_got = swapped(down_far, "hid", 1)

    grad_out = cotangent.astype(jnp.float32)
    second_shift_grad = jnp.sum(grad_mid, axis=0)
    second_gain_grad = jnp.sum(grad_mid * unit_mid, axis=0)
    grad_resid = grad_out + norm_pull(grad_mid, second_gain, unit_mid, scale_mid)
    grad_branch = grad_resid.astype(bf)
    grad_branch, up_far_got = tied(grad_branch, up_far_got)
    up_near, up_sent = halves(added(up_near, up_far_got).reshape(tops, 2, wide, D), "dp", 0, 1)
    up_got = swapped(up_sent, "dp", 1)
    grad_mixed = matmul_nt(grad_branch, out_full).astype(bf)
    out_grad = matmul_tn(mixed, grad_branch).astype(bf)

    grad_query, grad_key, grad_value = attend_back(
        key_rows, value_rows, grad_mixed, id_rows, id_columns, probability, centroid, counts
    )
    grad_value, up_got, down_got, down_near_got = tied(grad_value, up_got, down_got, down_near_got)
    ff = jnp.stack([added(up_near, up_got), summed([down_near, down_near_got, down_got]).astype(bf)])
    ff = ff.reshape(2, *whole, wide, D)
    ff_parts = dealt(ff, groups[-1], 1)

    query_grad = matmul_tn(normed_in, grad_query).astype(bf)
    key_grad = matmul_tn(normed_in, grad_key).astype(bf)
    value_grad = matmul_tn(normed_in, grad_value).astype(bf)
    both = jnp.stack([query_grad, key_grad, value_grad, out_grad]).reshape(4, tops, 2, 2, 2, part, D)
    both, sent = halves(both, "mp", 0, 4)
    got = swapped(sent, "mp", 1)
    grad_in = matmul_nt(grad_query, query_full) + matmul_nt(grad_key, key_full) + matmul_nt(grad_value, value_full)
    tokens_grad = (grad_resid + norm_pull(grad_in, first_gain, unit_in, scale_in)).astype(bf)
    total = lambda rows: jnp.sum(rows.astype(jnp.float32), axis=0)
    small = jnp.concatenate(
        [
            jnp.stack(
                [
                    jnp.sum(grad_in * unit_in, axis=0),
                    jnp.sum(grad_in, axis=0),
                    total(grad_query),
                    total(grad_value),
                    total(grad_branch),
                    second_gain_grad,
                    second_shift_grad,
                    total(cotangent),
                ]
            ),
            bias_up,
        ]
    )
    small = small + swapped(small, "mp", 1)
    both = added(both, got)
    one, one_sent = halves(both[:2], "dp", 0, 2)
    two, two_sent = halves(both[2:], "hid", 0, 3)
    got, two_got = (swapped(packed(one_sent, small), "dp", 1), swapped(two_sent, "hid", 1))
    one_got, small_got = unpacked(got, one_sent)
    small = small + small_got
    one, one_sent = halves(added(one, one_got), "hid", 0, 2)
    two, two_sent = halves(added(two, two_got), "dp", 0, 2)
    got, two_got = (swapped(packed(one_sent, small), "hid", 1), swapped(two_sent, "dp", 1))
    one_got, small_got = unpacked(got, one_sent)
    small = small + small_got
    both = jnp.stack([added(one, one_got), added(two, two_got)]).reshape(4, *whole, part, D)
    for group in reversed(groups):
        shift, bits = group
        mine = (lax.axis_index("dp") >> shift) & ((1 << bits) - 1)
        take = lambda k: lax.dynamic_index_in_dim(both, k, 1, keepdims=False)
        got = [swapped(packed(take(mine ^ d), small), "dp", d << shift) for d in range(1, 1 << bits)]
        pieces = [unpacked(g, take(mine)) for g in got]
        sums = summed([take(mine)] + [piece for piece, _ in pieces])
        small = summed([small] + [piece for _, piece in pieces])
        both = sums.astype(bf)
    for group in reversed(groups[:-1]):
        ff_parts = dealt(summed(ff_parts).astype(bf), group, 1)
    up_grad, down_grad = summed(ff_parts)
    down_grad = down_grad.T
    query_sum, key_sum, value_sum, out_sum = sums
    return (
        output,
        tokens_grad,
        small[0],
        small[1],
        query_sum,
        small[2],
        key_sum,
        value_sum,
        small[3],
        out_sum,
        small[4],
        small[5],
        small[6],
        up_grad,
        small[8:].reshape(-1),
        down_grad,
        small[7],
    )


def solution(mesh):
    return jax.shard_map(
        shards,
        mesh=mesh,
        in_specs=(
            P(("dp", "hid", "mp"), None),
            P(("dp", "hid", "mp")),
            P(None, ("dp", "hid", "mp")),
            P(("dp", "hid", "mp"), None),
            P(),
            P(),
            P(("dp", "hid", "mp"), None),
            P(),
            P(("dp", "hid", "mp"), None),
            P(("dp", "hid", "mp"), None),
            P(),
            P(("dp", "hid", "mp"), None),
            P(),
            P(),
            P(),
            P("dp", ("hid", "mp")),
            P(),
            P(("hid", "mp"), "dp"),
            P(),
        ),
        out_specs=(
            P(("dp", "hid", "mp"), None),
            P(("dp", "hid", "mp"), None),
            P(),
            P(),
            P(("dp", "hid", "mp"), None),
            P(),
            P(("dp", "hid", "mp"), None),
            P(("dp", "hid", "mp"), None),
            P(),
            P(("dp", "hid", "mp"), None),
            P(),
            P(),
            P(),
            P("dp", ("hid", "mp")),
            P(),
            P(("hid", "mp"), "dp"),
            P(),
        ),
        check_vma=False,
    )
```

```python
import functools

import jax
import jax.numpy as jnp
from jax import lax
from jax.experimental import pallas as pl
from jax.experimental.pallas import tpu as pltpu
from jax.sharding import PartitionSpec as P

D = 768
HEADS = 12
HEAD = 64
CLUSTERS = 100
SEQ = 1024
PAD = 128


def matmul(left, right):
    return jnp.dot(left, right, preferred_element_type=jnp.float32)


def matmul_nt(left, right):
    return lax.dot_general(left, right, (((1,), (1,)), ((), ())), preferred_element_type=jnp.float32)


def matmul_tn(left, right):
    return lax.dot_general(left, right, (((0,), (0,)), ((), ())), preferred_element_type=jnp.float32)


def swapped(array, axis, mask):
    count = lax.axis_size(axis)
    return lax.ppermute(array, axis, [(i, i ^ mask) for i in range(count)])


def own_bit(axis, bit):
    return (lax.axis_index(axis) >> bit) & 1


def joined(own, other, mine, place):
    own, other = (jnp.expand_dims(own, place), jnp.expand_dims(other, place))
    shape = own.shape[:place] + (2,) + own.shape[place + 1 :]
    return jnp.where(lax.broadcasted_iota(jnp.int32, shape, place) == mine, own, other)


def halves(array, axis, bit, place):
    mine = own_bit(axis, bit)
    take = lambda k: lax.dynamic_index_in_dim(array, k, place, keepdims=False)
    return (take(mine), take(1 - mine))


def high_groups():
    count = lax.axis_size("dp").bit_length() - 1
    return [(b, min(2, count - b)) for b in range(1, count, 2)]


def exchanged(piece, group):
    shift, bits = group
    return [swapped(piece, "dp", d << shift) for d in range(1, 1 << bits)]


def lined_up(own, others, group, place):
    shift, bits = group
    mine = (lax.axis_index("dp") >> shift) & ((1 << bits) - 1)
    pieces = [jnp.expand_dims(p, place) for p in [own, *others]]
    shape = pieces[0].shape[:place] + (1 << bits,) + pieces[0].shape[place + 1 :]
    apart = lax.broadcasted_iota(jnp.int32, shape, place) ^ mine
    out = jnp.broadcast_to(pieces[-1], shape)
    for d in reversed(range(len(pieces) - 1)):
        out = jnp.where(apart == d, pieces[d], out)
    return out


def dealt(array, group, place):
    shift, bits = group
    mine = (lax.axis_index("dp") >> shift) & ((1 << bits) - 1)
    take = lambda k: lax.dynamic_index_in_dim(array, k, place, keepdims=False)
    return [take(mine)] + [swapped(take(mine ^ d), "dp", d << shift) for d in range(1, 1 << bits)]


def summed(pieces):
    return sum(p.astype(jnp.float32) for p in pieces)


def moments(values):
    middle = jnp.mean(values, axis=-1, keepdims=True)
    centered = values - middle
    spread = jnp.mean(centered * centered, axis=-1, keepdims=True)
    return (centered * lax.rsqrt(spread + 1e-05), lax.rsqrt(spread + 1e-05))


def norm_pull(grad, gain, unit, scale):
    scaled = grad * gain
    first = jnp.mean(scaled, axis=-1, keepdims=True)
    second = jnp.mean(scaled * unit, axis=-1, keepdims=True)
    return scale * (scaled - first - unit * second)


def gate_and_slope(v):
    size = jnp.abs(v)
    bell = jnp.exp(-0.5 * v * v)
    t = 1.0 / (1.0 + 0.23164189 * size)
    series = 0.7107068705 + t * (-0.7265760135 + t * 0.5307027145)
    tail = t * (0.127414796 + t * (-0.142248368 + t * series)) * bell
    phi = jnp.where(v < 0, tail, 1.0 - tail)
    return (v * phi, phi + v * (0.3989422804014327 * bell))


def ff_kernel(first, rows, up_at, down_at, *refs):
    x_in, cot_in, xt_in, cott_in, up_in, down_in, bu = refs[:7]
    refs = refs[7:]
    if not first:
        branch_in, mid_in = refs[:2]
        refs = refs[2:]
    branch_out, mid_out, grads, dbu, x, cot, xt, cott, wu, wd, branch, mid, dw, sems = refs
    nt = (((1,), (1,)), ((), ()))
    count = x.shape[0] // rows
    parts = [pl.ds(r * rows, rows) for r in range(count)]
    used = [0]

    def copy(source, target):
        used[0] += 1
        return pltpu.make_async_copy(source, target, sems.at[used[0] - 1])

    def started(source, target):
        made = copy(source, target)
        made.start()
        return made

    up_copy = started(up_in.at[up_at], wu)
    x_copies = [started(x_in.at[parts[0]], x.at[parts[0]])]
    down_copy = started(down_in.at[down_at], wd)
    cot_copies = [started(cot_in.at[parts[0]], cot.at[parts[0]])]
    sum_copies = []
    for r in range(count):
        if r:
            x_copies.append(started(x_in.at[parts[r]], x.at[parts[r]]))
            cot_copies.append(started(cot_in.at[parts[r]], cot.at[parts[r]]))
        if not first:
            sum_copies.append([started(branch_in.at[parts[r]], branch.at[parts[r]]), started(mid_in.at[parts[r]], mid.at[parts[r]])])
    cott_copy, xt_copy = (started(cott_in, cott), started(xt_in, xt))
    outs = []
    hs, gs = ([], [])
    total = jnp.zeros_like(dbu)
    for r in range(count):
        at = parts[r]
        if r == 0:
            up_copy.wait()
        x_copies[r].wait()
        pre = matmul(x[at, :], wu[...]) + bu[...]
        if r == 0:
            down_copy.wait()
        cot_copies[r].wait()
        grad_hidden = matmul(cot[at, :], wd[...])
        h, slope = gate_and_slope(pre)
        h = h.astype(jnp.bfloat16)
        g = (grad_hidden * slope).astype(jnp.bfloat16)
        total += jnp.sum(g.astype(jnp.float32), axis=0, keepdims=True)
        forth = lax.dot_general(h, wd[...], nt, preferred_element_type=jnp.float32)
        back = lax.dot_general(g, wu[...], nt, preferred_element_type=jnp.float32)
        if not first:
            for made in sum_copies[r]:
                made.wait()
            forth += branch[at, :]
            back += mid[at, :]
        branch[at, :] = forth
        mid[at, :] = back
        outs += [started(branch.at[at], branch_out.at[at]), started(mid.at[at], mid_out.at[at])]
        hs.append(h)
        gs.append(g)
    dbu[...] = total
    cott_copy.wait()
    dw[1] = matmul(cott[...], jnp.concatenate(hs, axis=0)).astype(jnp.bfloat16)
    outs.append(started(dw.at[1], grads.at[1]))
    xt_copy.wait()
    dw[0] = matmul(xt[...], jnp.concatenate(gs, axis=0)).astype(jnp.bfloat16)
    outs.append(started(dw.at[0], grads.at[0]))
    for made in outs:
        made.wait()


def ff_block(x, cot, xt, cott, up, up_at, down, down_at, bu, *sums):
    f32, bf = (jnp.float32, jnp.bfloat16)
    count, wide = (x.shape[0], up.shape[2])
    spec = pl.BlockSpec(memory_space=pltpu.VMEM)
    far = pl.BlockSpec(memory_space=pl.ANY)
    rows = jax.ShapeDtypeStruct((count, D), f32)
    return pl.pallas_call(
        functools.partial(ff_kernel, not sums, 256, up_at, down_at),
        out_shape=(rows, rows, jax.ShapeDtypeStruct((2, D, wide), bf), jax.ShapeDtypeStruct((1, wide), f32)),
        in_specs=[far] * 6 + [spec] + [far] * len(sums),
        out_specs=(far, far, far, spec),
        scratch_shapes=[
            pltpu.VMEM((count, D), bf),
            pltpu.VMEM((count, D), bf),
            pltpu.VMEM((D, count), bf),
            pltpu.VMEM((D, count), bf),
            pltpu.VMEM((D, wide), bf),
            pltpu.VMEM((D, wide), bf),
            pltpu.VMEM((count, D), f32),
            pltpu.VMEM((count, D), f32),
            pltpu.VMEM((2, D, wide), bf),
            pltpu.SemaphoreType.DMA((40,)),
        ],
        compiler_params=pltpu.CompilerParams(vmem_limit_bytes=40 * 1024 * 1024),
        cost_estimate=pl.CostEstimate(
            flops=12 * count * D * wide, bytes_accessed=4 * D * wide, transcendentals=2 * count * wide
        ),
        name="ff_block",
    )(x, cot, xt, cott, up, down, bu, *sums)


STEP = 256
ROWS = pl.BlockSpec((STEP, D), lambda i: (i, 0))
WHOLE = pl.BlockSpec((D, D), lambda i: (0, 0))
LINE = pl.BlockSpec((1, D), lambda i: (0, 0))
LINES = pl.BlockSpec((8, D), lambda i: (0, 0))


def by_rows(kernel, name, in_specs, out_specs, out_shape, scratch, flops, moved):
    return pl.pallas_call(
        kernel,
        grid=(SEQ // STEP,),
        in_specs=in_specs,
        out_specs=out_specs,
        out_shape=out_shape,
        scratch_shapes=scratch,
        compiler_params=pltpu.CompilerParams(vmem_limit_bytes=32 * 1024 * 1024),
        cost_estimate=pl.CostEstimate(flops=flops, bytes_accessed=moved, transcendentals=SEQ),
        name=name,
    )


def middle_kernel(mixed, tokens, out_full, b_out, gain, shift, residual, x, x_t):
    value = tokens[...].astype(jnp.float32) + (matmul(mixed[...], out_full[...]) + b_out[...])
    residual[...] = value
    unit, _ = moments(value)
    normed = (unit * gain[...] + shift[...]).astype(jnp.bfloat16)
    x[...] = normed
    x_t[...] = normed.T


def middle(mixed, tokens, out_full, b_out, gain, shift):
    f32, bf = (jnp.float32, jnp.bfloat16)
    return by_rows(
        middle_kernel,
        "middle",
        [ROWS, ROWS, WHOLE, LINE, LINE, LINE],
        (ROWS, ROWS, pl.BlockSpec((D, STEP), lambda i: (0, i))),
        (jax.ShapeDtypeStruct((SEQ, D), f32), jax.ShapeDtypeStruct((SEQ, D), bf), jax.ShapeDtypeStruct((D, SEQ), bf)),
        [],
        2 * SEQ * D * D,
        12 * SEQ * D,
    )(mixed, tokens, out_full, b_out[None], gain[None], shift[None])


def add_lines(ref, lines):
    @pl.when(pl.program_id(0) == 0)
    def _():
        ref[...] = jnp.zeros_like(ref)

    sums = [jnp.sum(line.astype(jnp.float32), axis=0, keepdims=True) for line in lines]
    ref[: len(lines), :] += jnp.concatenate(sums, axis=0)


def turn_kernel(branch, grad_mid, residual, cot, mixed, out_full, b_down, gain, output, grad_resid, grad_mixed, out_grad, lines, held):
    value = residual[...]
    output[...] = (value + branch[...] + b_down[...]).astype(jnp.bfloat16)
    grad = grad_mid[...]
    unit, scale = moments(value)
    pulled = cot[...].astype(jnp.float32) + norm_pull(grad, gain[...], unit, scale)
    grad_resid[...] = pulled
    low = pulled.astype(jnp.bfloat16)
    grad_mixed[...] = matmul_nt(low, out_full[...]).astype(jnp.bfloat16)
    add_lines(lines, [low, grad * unit, grad, cot[...]])

    @pl.when(pl.program_id(0) == 0)
    def _():
        held[...] = jnp.zeros_like(held)

    held[...] += matmul_tn(mixed[...], low)

    @pl.when(pl.program_id(0) == pl.num_programs(0) - 1)
    def _():
        out_grad[...] = held[...].astype(jnp.bfloat16)


def turn(branch, grad_mid, residual, cot, mixed, out_full, b_down, gain):
    f32, bf = (jnp.float32, jnp.bfloat16)
    low = jax.ShapeDtypeStruct((SEQ, D), bf)
    return by_rows(
        turn_kernel,
        "turn",
        [ROWS, ROWS, ROWS, ROWS, ROWS, WHOLE, LINE, LINE],
        (ROWS, ROWS, ROWS, WHOLE, LINES),
        (low, jax.ShapeDtypeStruct((SEQ, D), f32), low, jax.ShapeDtypeStruct((D, D), bf), jax.ShapeDtypeStruct((8, D), f32)),
        [pltpu.VMEM((D, D), f32)],
        4 * SEQ * D * D,
        24 * SEQ * D,
    )(branch, grad_mid, residual, cot, mixed, out_full, b_down[None], gain[None])


def last_kernel(gq, gk, gv, wq, wk, wv, tokens, grad_resid, gain, tokens_grad, lines):
    grad = matmul_nt(gq[...], wq[...]) + matmul_nt(gk[...], wk[...]) + matmul_nt(gv[...], wv[...])
    unit, scale = moments(tokens[...].astype(jnp.float32))
    tokens_grad[...] = (grad_resid[...] + norm_pull(grad, gain[...], unit, scale)).astype(jnp.bfloat16)
    add_lines(lines, [grad * unit, grad, gq[...], gv[...]])


def last(gq, gk, gv, wq, wk, wv, tokens, grad_resid, gain):
    return by_rows(
        last_kernel,
        "last",
        [ROWS, ROWS, ROWS, WHOLE, WHOLE, WHOLE, ROWS, ROWS, LINE],
        (ROWS, LINES),
        (jax.ShapeDtypeStruct((SEQ, D), jnp.bfloat16), jax.ShapeDtypeStruct((8, D), jnp.float32)),
        [],
        6 * SEQ * D * D,
        14 * SEQ * D,
    )(gq, gk, gv, wq, wk, wv, tokens, grad_resid, gain[None])


def tied(*arrays):
    return lax.optimization_barrier(arrays)


def packed(sent, small):
    high = small.astype(jnp.bfloat16)
    low = (small - high.astype(jnp.float32)).astype(jnp.bfloat16)
    return jnp.concatenate([sent.reshape(-1, D), high, low])


def unpacked(got, like):
    rows = like.size // D
    high, low = jnp.split(got[rows:].astype(jnp.float32), 2)
    return (got[:rows].reshape(like.shape), high + low)


def added(own, got):
    return (own.astype(jnp.float32) + got.astype(jnp.float32)).astype(jnp.bfloat16)


def dot(a, b, ca=1, cb=0):
    return lax.dot_general(a, b, (((ca,), (cb,)), ((), ())), preferred_element_type=jnp.float32)


def rounded_sum(pieces):
    return summed(pieces).astype(jnp.bfloat16)


def sum_halves(pieces, axis, bit, place):
    both = [halves(piece, axis, bit, place) for piece in pieces]
    return (rounded_sum([kept for kept, _ in both]), rounded_sum([sent for _, sent in both]))


def own_half(wide):
    rows = lax.broadcasted_iota(jnp.int32, wide.shape, 0) // PAD
    columns = lax.broadcasted_iota(jnp.int32, wide.shape, 1) // HEAD
    return jnp.where(rows == columns, wide, 0.0)


def pair_rows(ids):
    at = lax.broadcasted_iota(jnp.int32, (PAD, SEQ), 0)
    return jnp.concatenate([jnp.where(ids[k : k + 1, :] == at, 1.0, 0.0) for k in (0, 1)], axis=0).astype(jnp.bfloat16)


def pair_columns(ids):
    at = lax.broadcasted_iota(jnp.int32, (SEQ, PAD), 1)
    return jnp.concatenate([jnp.where(ids[:, k : k + 1] == at, 1.0, 0.0) for k in (0, 1)], axis=1).astype(jnp.bfloat16)


def attend_kernel(q, k, v, rows, columns, seg_row, seg_col, mixed, prob, centroid, count):
    bf = jnp.bfloat16
    hot = pair_rows(rows[0])
    lanes = lax.broadcasted_iota(jnp.int32, (SEQ, PAD), 1)
    marks = jnp.where(lanes == 0, seg_col[...], jnp.where(lanes == 1, 1.0, 0.0)).astype(bf)
    sums = dot(hot, jnp.concatenate([q[...], marks], axis=1))
    owner, counts = (sums[:, 128:129], sums[:, 129:130])
    counts = jnp.maximum(counts, 1.0)
    middle = own_half(sums[:, :128] / counts).astype(bf)
    scores = 0.125 * dot(middle, k[...], 1, 1)
    allowed = jnp.abs(owner - counts * seg_row[...]) < 0.5
    masked = jnp.where(allowed, scores, -1e30)
    highest = jnp.max(masked, axis=1, keepdims=True)
    exponent = jnp.where(allowed, jnp.exp(masked - highest), 0.0)
    total = jnp.sum(exponent, axis=1, keepdims=True)
    p = exponent * (1.0 / jnp.maximum(total, 1e-30))
    context = own_half(dot(p.astype(bf), v[...])).astype(bf)
    mixed[...] = dot(pair_columns(columns[0]), context).astype(bf)
    prob[0] = p
    centroid[0] = middle
    count[0] = jnp.broadcast_to(counts, (2 * PAD, 128))


def attend(q, k, v, rows, columns, seg_row, seg_col):
    bf = jnp.bfloat16
    pair = pl.BlockSpec((SEQ, 128), lambda i: (0, i))
    return pl.pallas_call(
        attend_kernel,
        grid=(HEADS // 2,),
        in_specs=[pair, pair, pair,
            pl.BlockSpec((1, 2, SEQ), lambda i: (i, 0, 0)),
            pl.BlockSpec((1, SEQ, 2), lambda i: (i, 0, 0)),
            pl.BlockSpec((1, SEQ), lambda i: (0, 0)),
            pl.BlockSpec((SEQ, 1), lambda i: (0, 0))],
        out_specs=(pair, pl.BlockSpec((1, 2 * PAD, SEQ), lambda i: (i, 0, 0)), pl.BlockSpec((1, 2 * PAD, 128), lambda i: (i, 0, 0)), pl.BlockSpec((1, 2 * PAD, 128), lambda i: (i, 0, 0))),
        out_shape=(jax.ShapeDtypeStruct((SEQ, D), bf), jax.ShapeDtypeStruct((HEADS // 2, 2 * PAD, SEQ), jnp.float32), jax.ShapeDtypeStruct((HEADS // 2, 2 * PAD, 128), bf), jax.ShapeDtypeStruct((HEADS // 2, 2 * PAD, 128), jnp.float32)),
        cost_estimate=pl.CostEstimate(flops=12 * 5 * 2 * PAD * SEQ * HEAD, bytes_accessed=14 << 20, transcendentals=HEADS * PAD * SEQ),
        compiler_params=pltpu.CompilerParams(vmem_limit_bytes=24 * 1024 * 1024),
        name="attend",
    )(q, k, v, rows, columns, seg_row, seg_col)


def attend_back_kernel(k, v, gm, rows, columns, prob, centroid, count, gq, gk, gv):
    bf = jnp.bfloat16
    hot = pair_rows(rows[0])
    p = prob[0]
    grad_context = own_half(dot(hot, gm[...])).astype(bf)
    gv[...] = dot(p.astype(bf), grad_context, 0, 0).astype(bf)
    grad_prob = dot(grad_context, v[...], 1, 1)
    grad_scores = (p * (grad_prob - jnp.sum(p * grad_prob, axis=1, keepdims=True))).astype(bf)
    grad_centroid = own_half(0.125 * dot(grad_scores, k[...]) / count[0]).astype(bf)
    gk[...] = (0.125 * dot(grad_scores, centroid[0], 0, 0)).astype(bf)
    gq[...] = dot(pair_columns(columns[0]), grad_centroid).astype(bf)


def attend_back(k, v, gm, rows, columns, prob, centroid, count):
    bf = jnp.bfloat16
    pair = pl.BlockSpec((SEQ, 128), lambda i: (0, i))
    wide = pl.BlockSpec((1, 2 * PAD, 128), lambda i: (i, 0, 0))
    out = jax.ShapeDtypeStruct((SEQ, D), bf)
    return pl.pallas_call(
        attend_back_kernel,
        grid=(HEADS // 2,),
        in_specs=[pair, pair, pair,
            pl.BlockSpec((1, 2, SEQ), lambda i: (i, 0, 0)),
            pl.BlockSpec((1, SEQ, 2), lambda i: (i, 0, 0)),
            pl.BlockSpec((1, 2 * PAD, SEQ), lambda i: (i, 0, 0)), wide, wide],
        out_specs=(pair, pair, pair),
        out_shape=(out, out, out),
        cost_estimate=pl.CostEstimate(flops=12 * 7 * 2 * PAD * SEQ * HEAD, bytes_accessed=16 << 20, transcendentals=0),
        compiler_params=pltpu.CompilerParams(vmem_limit_bytes=24 * 1024 * 1024),
        name="attend_back",
    )(k, v, gm, rows, columns, prob, centroid, count)


def shards(
    tokens,
    segment_ids,
    cluster_ids,
    cotangent,
    first_gain,
    first_shift,
    w_query,
    b_query,
    w_key,
    w_value,
    b_value,
    w_out,
    b_out,
    second_gain,
    second_shift,
    w_up,
    b_up,
    w_down,
    b_down,
):
    groups = high_groups()
    tops = 1 << sum(bits for _, bits in groups)
    bf = jnp.bfloat16
    part = D // (8 * tops)
    wide = D // (2 * tops)
    whole = [1 << bits for _, bits in reversed(groups)]

    attn = jnp.stack([w.astype(bf) for w in (w_query, w_key, w_value, w_out)])
    up, down = (w_up.astype(bf), w_down.T.astype(bf))
    unit_in, _ = moments(tokens.astype(jnp.float32))
    normed_in = (unit_in * first_gain + first_shift).astype(bf)
    id_rows = cluster_ids.reshape(HEADS // 2, 2, SEQ)
    id_columns = id_rows.transpose(0, 2, 1)
    seg = segment_ids.astype(jnp.float32)
    seg_row, seg_col = (seg[None, :], seg[:, None])
    cot_t = cotangent.T
    for group in groups:
        got = exchanged(attn, group)
        normed_in, id_columns, seg_col, *got = tied(normed_in, id_columns, seg_col, *got)
        attn = lined_up(attn, got, group, 1)
    attn = attn.reshape(4, tops, part, D)
    first, second = (attn[:2], attn[2:])
    first_got, second_got = (swapped(first, "dp", 1), swapped(second, "hid", 1))
    for group in groups[:-1]:
        up = lined_up(up, exchanged(up, group), group, 0)
        down = lined_up(down, exchanged(down, group), group, 0)
    up_got, down_got = (exchanged(up, groups[-1]), exchanged(down, groups[-1]))
    cot_t, first_got, second_got = tied(cot_t, first_got, second_got)
    first = joined(first, first_got, own_bit("dp", 0), 2)
    second = joined(second, second_got, own_bit("hid", 0), 2)
    first_got, second_got = (swapped(first, "hid", 1), swapped(second, "dp", 1))
    first_got, second_got, *up_got = tied(first_got, second_got, *up_got)
    up = lined_up(up, up_got, groups[-1], 0).reshape(tops, wide, D)
    up_got = swapped(up, "dp", 1)
    first = joined(first, first_got, own_bit("hid", 0), 3)
    second = joined(second, second_got, own_bit("dp", 0), 2)
    first_got, second_got = (swapped(first, "mp", 1), swapped(second, "mp", 1))
    first = joined(first, first_got, own_bit("mp", 0), 4)
    second = joined(second, second_got, own_bit("mp", 0), 4)
    query_full, key_full = first.reshape(2, D, D)
    value_full, out_full = second.reshape(2, D, D)

    query = (matmul(normed_in, query_full) + b_query).astype(bf)
    query, *down_got = tied(query, *down_got)
    down = lined_up(down, down_got, groups[-1], 0).reshape(tops, wide, D)
    down_got = swapped(down, "hid", 1)
    key_rows = matmul(normed_in, key_full).astype(bf)
    value_rows = (matmul(normed_in, value_full) + b_value).astype(bf)
    key_rows, up_got = tied(key_rows, up_got)
    up = joined(up, up_got, own_bit("dp", 0), 1).reshape(1, D, D)
    up_mate = swapped(up, "hid", 1)
    up_next = swapped(up, "mp", 1)
    mixed, probability, centroid, counts = attend(
        query, key_rows, value_rows, id_rows, id_columns, seg_row, seg_col
    )
    mixed, down_got = tied(mixed, down_got)
    down = jnp.stack([down, down_got])
    down_got = swapped(down, "dp", 1)
    residual, x, x_t = middle(mixed, tokens, out_full, b_out, second_gain, second_shift)
    x, up_mate, down_got = tied(x, up_mate, down_got)
    down = joined(down, down_got, own_bit("dp", 0), 2).reshape(2, D, D)
    down_next = swapped(down, "mp", 1)
    up_across = swapped(up_mate, "mp", 1)
    me = lax.axis_index(("hid", "mp"))
    blocks = [(me ^ 2, up_mate, down, 1), (me ^ 3, up_across, down_next, 1), (me ^ 1, up_next, down_next, 0), (me, up, down, 0)]
    bias_up = jnp.zeros((4, D), jnp.float32)
    sends, sums = ([], [])
    for k, (block, up_rows, down_rows, down_at) in enumerate(blocks):
        up_bias = lax.dynamic_slice_in_dim(b_up, block * D, D)[None]
        *sums, send, bias = ff_block(x, cotangent, x_t, cot_t, up_rows, 0, down_rows, down_at, up_bias, *sums)
        bias_up = lax.dynamic_update_slice(bias_up, bias, (block, 0))
        sends.append(send)
        if k == 1:
            far_got = swapped(send, "mp", 1)
        if k == 2:
            near_got = swapped(send, "mp", 1)
            up_far = added(sends[0][0], far_got[0])
            split = lambda piece: piece.reshape(tops, 2, wide, D)
            down_far, down_sent = sum_halves([split(sends[0][1]), split(far_got[1])], "dp", 0, 1)
            *sums, up_far, down_sent = tied(*sums, up_far, down_sent)
            up_far_got = swapped(up_far, "hid", 1)
            down_far_got = swapped(down_sent, "dp", 1)

    down_near, down_sent = sum_halves([split(sends[3][1]), split(near_got[1])], "dp", 0, 1)
    down_far = added(down_far, down_far_got)
    branch, grad_mid, down_sent, down_far = tied(*sums, down_sent, down_far)
    down_near_got = swapped(down_sent, "dp", 1)
    down_got = swapped(down_far, "hid", 1)

    output, grad_resid, grad_mixed, out_grad, turn_lines = turn(
        branch, grad_mid, residual, cotangent, mixed, out_full, b_down, second_gain
    )
    grad_mixed, up_far_got = tied(grad_mixed, up_far_got)
    up_near, up_sent = sum_halves([split(sends[3][0]), split(near_got[0]), split(up_far_got)], "dp", 0, 1)
    up_got = swapped(up_sent, "dp", 1)

    grad_query, grad_key, grad_value = attend_back(
        key_rows, value_rows, grad_mixed, id_rows, id_columns, probability, centroid, counts
    )
    grad_value, down_got, down_near_got = tied(grad_value, down_got, down_near_got)
    down_sum = rounded_sum([down_near, down_near_got, down_got]).reshape(*whole, wide, D)
    down_parts = dealt(down_sum, groups[-1], 0)

    query_grad = matmul_tn(normed_in, grad_query).astype(bf)
    key_grad = matmul_tn(normed_in, grad_key).astype(bf)
    value_grad = matmul_tn(normed_in, grad_value).astype(bf)
    value_grad, up_got = tied(value_grad, up_got)
    up_parts = dealt(added(up_near, up_got).reshape(*whole, wide, D), groups[-1], 0)
    both = jnp.stack([query_grad, key_grad, value_grad, out_grad]).reshape(4, tops, 2, 2, 2, part, D)
    both, sent = halves(both, "mp", 0, 4)
    got = swapped(sent, "mp", 1)
    tokens_grad, last_lines = last(
        grad_query, grad_key, grad_value, query_full, key_full, value_full, tokens, grad_resid, first_gain
    )
    small = jnp.concatenate([last_lines[:4], turn_lines[:4], bias_up])
    small, *down_parts = tied(small, *down_parts)
    small = small + swapped(small, "mp", 1)
    both = added(both, got)
    one, one_sent = halves(both[:2], "dp", 0, 2)
    two, two_sent = halves(both[2:], "hid", 0, 3)
    got, two_got = (swapped(packed(one_sent, small), "dp", 1), swapped(two_sent, "hid", 1))
    got, two_got, *up_parts = tied(got, two_got, *up_parts)
    one_got, small_got = unpacked(got, one_sent)
    small = small + small_got
    one, one_sent = halves(added(one, one_got), "hid", 0, 2)
    two, two_sent = halves(added(two, two_got), "dp", 0, 2)
    got, two_got = (swapped(packed(one_sent, small), "hid", 1), swapped(two_sent, "dp", 1))
    one_got, small_got = unpacked(got, one_sent)
    small = small + small_got
    both = jnp.stack([added(one, one_got), added(two, two_got)]).reshape(4, *whole, part, D)
    for group in reversed(groups):
        shift, bits = group
        mine = (lax.axis_index("dp") >> shift) & ((1 << bits) - 1)
        take = lambda k: lax.dynamic_index_in_dim(both, k, 1, keepdims=False)
        got = [swapped(packed(take(mine ^ d), small), "dp", d << shift) for d in range(1, 1 << bits)]
        pieces = [unpacked(g, take(mine)) for g in got]
        sums = summed([take(mine)] + [piece for piece, _ in pieces])
        small = summed([small] + [piece for _, piece in pieces])
        both = sums.astype(bf)
    for group in reversed(groups[:-1]):
        up_parts = dealt(rounded_sum(up_parts), group, 0)
        down_parts = dealt(rounded_sum(down_parts), group, 0)
    up_grad, down_grad = (summed(up_parts), summed(down_parts).T)
    query_sum, key_sum, value_sum, out_sum = sums
    return (
        output,
        tokens_grad,
        small[0],
        small[1],
        query_sum,
        small[2],
        key_sum,
        value_sum,
        small[3],
        out_sum,
        small[4],
        small[5],
        small[6],
        up_grad,
        small[8:].reshape(-1),
        down_grad,
        small[7],
    )


def solution(mesh):
    return jax.shard_map(
        shards,
        mesh=mesh,
        in_specs=(
            P(("dp", "hid", "mp"), None),
            P(("dp", "hid", "mp")),
            P(None, ("dp", "hid", "mp")),
            P(("dp", "hid", "mp"), None),
            P(),
            P(),
            P(("dp", "hid", "mp"), None),
            P(),
            P(("dp", "hid", "mp"), None),
            P(("dp", "hid", "mp"), None),
            P(),
            P(("dp", "hid", "mp"), None),
            P(),
            P(),
            P(),
            P("dp", ("hid", "mp")),
            P(),
            P(("hid", "mp"), "dp"),
            P(),
        ),
        out_specs=(
            P(("dp", "hid", "mp"), None),
            P(("dp", "hid", "mp"), None),
            P(),
            P(),
            P(("dp", "hid", "mp"), None),
            P(),
            P(("dp", "hid", "mp"), None),
            P(("dp", "hid", "mp"), None),
            P(),
            P(("dp", "hid", "mp"), None),
            P(),
            P(),
            P(),
            P("dp", ("hid", "mp")),
            P(),
            P(("hid", "mp"), "dp"),
            P(),
        ),
        check_vma=False,
    )
```

```python
import functools

import jax
import jax.numpy as jnp
from jax import lax
from jax.experimental import pallas as pl
from jax.experimental.pallas import tpu as pltpu
from jax.sharding import PartitionSpec as P

D = 768
HEADS = 12
HEAD = 64
CLUSTERS = 100
SEQ = 1024
PAD = 128


def matmul(left, right):
    return jnp.dot(left, right, preferred_element_type=jnp.float32)


def matmul_nt(left, right):
    return lax.dot_general(left, right, (((1,), (1,)), ((), ())), preferred_element_type=jnp.float32)


def matmul_tn(left, right):
    return lax.dot_general(left, right, (((0,), (0,)), ((), ())), preferred_element_type=jnp.float32)


def swapped(array, axis, mask):
    count = lax.axis_size(axis)
    return lax.ppermute(array, axis, [(i, i ^ mask) for i in range(count)])


def own_bit(axis, bit):
    return (lax.axis_index(axis) >> bit) & 1


def joined(own, other, mine, place):
    own, other = (jnp.expand_dims(own, place), jnp.expand_dims(other, place))
    shape = own.shape[:place] + (2,) + own.shape[place + 1 :]
    return jnp.where(lax.broadcasted_iota(jnp.int32, shape, place) == mine, own, other)


def halves(array, axis, bit, place):
    mine = own_bit(axis, bit)
    take = lambda k: lax.dynamic_index_in_dim(array, k, place, keepdims=False)
    return (take(mine), take(1 - mine))


def high_groups():
    count = lax.axis_size("dp").bit_length() - 1
    return [(b, min(2, count - b)) for b in range(1, count, 2)]


def exchanged(piece, group):
    shift, bits = group
    return [swapped(piece, "dp", d << shift) for d in range(1, 1 << bits)]


def lined_up(own, others, group, place):
    shift, bits = group
    mine = (lax.axis_index("dp") >> shift) & ((1 << bits) - 1)
    pieces = [jnp.expand_dims(p, place) for p in [own, *others]]
    shape = pieces[0].shape[:place] + (1 << bits,) + pieces[0].shape[place + 1 :]
    apart = lax.broadcasted_iota(jnp.int32, shape, place) ^ mine
    out = jnp.broadcast_to(pieces[-1], shape)
    for d in reversed(range(len(pieces) - 1)):
        out = jnp.where(apart == d, pieces[d], out)
    return out


def dealt(array, group, place):
    shift, bits = group
    mine = (lax.axis_index("dp") >> shift) & ((1 << bits) - 1)
    take = lambda k: lax.dynamic_index_in_dim(array, k, place, keepdims=False)
    return [take(mine)] + [swapped(take(mine ^ d), "dp", d << shift) for d in range(1, 1 << bits)]


def summed(pieces):
    return sum(p.astype(jnp.float32) for p in pieces)


def moments(values):
    middle = jnp.mean(values, axis=-1, keepdims=True)
    centered = values - middle
    spread = jnp.mean(centered * centered, axis=-1, keepdims=True)
    return (centered * lax.rsqrt(spread + 1e-05), lax.rsqrt(spread + 1e-05))


def norm_pull(grad, gain, unit, scale):
    scaled = grad * gain
    first = jnp.mean(scaled, axis=-1, keepdims=True)
    second = jnp.mean(scaled * unit, axis=-1, keepdims=True)
    return scale * (scaled - first - unit * second)


def gate_and_slope(v):
    size = jnp.abs(v)
    bell = jnp.exp(-0.5 * v * v)
    t = 1.0 / (1.0 + 0.23164189 * size)
    series = 0.7107068705 + t * (-0.7265760135 + t * 0.5307027145)
    tail = t * (0.127414796 + t * (-0.142248368 + t * series)) * bell
    phi = jnp.where(v < 0, tail, 1.0 - tail)
    return (v * phi, phi + v * (0.3989422804014327 * bell))


def ff_kernel(first, rows, places, *refs):
    x_in, cot_in, xt_in, cott_in, *weights, bu = refs[:9]
    refs = refs[9:]
    if not first:
        branch_in, mid_in = refs[:2]
        refs = refs[2:]
    branch_out, mid_out, *grads = refs[:4]
    dbu, x, cot, xt, cott, wu, wd, branch, mid, dw, sems = refs[4:]
    nt = (((1,), (1,)), ((), ()))
    count = x.shape[0] // rows
    parts = [pl.ds(r * rows, rows) for r in range(count)]
    used = [0]

    def started(source, target):
        used[0] += 1
        made = pltpu.make_async_copy(source, target, sems.at[used[0] - 1])
        made.start()
        return made

    def fetch_weight(k, target):
        ref, place = (weights[k], places[k])
        return started(ref.at[place], target.at[k // 2])

    def fetch_rows(r):
        return [started(x_in.at[parts[r]], x.at[parts[r]]), started(cot_in.at[parts[r]], cot.at[parts[r]])]

    weight_copies = [fetch_weight(0, wu)]
    row_copies = [fetch_rows(0)]
    weight_copies.append(fetch_weight(1, wd))
    outs = []
    for block in (0, 1):
        hs, gs = ([], [])
        total = jnp.zeros((1, dbu.shape[1]), jnp.float32)
        for r in range(count):
            at = parts[r]
            if r == 0:
                weight_copies[2 * block].wait()
            if block == 0:
                row_copies[r][0].wait()
            pre = matmul(x[at, :], wu[block]) + bu[block : block + 1, :]
            if r == 0:
                weight_copies[2 * block + 1].wait()
            if block == 0:
                row_copies[r][1].wait()
                if not first:
                    sum_copies = [started(branch_in.at[at], branch.at[at]), started(mid_in.at[at], mid.at[at])]
                if r + 1 < count:
                    row_copies.append(fetch_rows(r + 1))
                if r == 1:
                    cott_copy = started(cott_in, cott)
                if r == 2:
                    xt_copy = started(xt_in, xt)
                if r == 3:
                    weight_copies += [fetch_weight(2, wu), fetch_weight(3, wd)]
            grad_hidden = matmul(cot[at, :], wd[block])
            h, slope = gate_and_slope(pre)
            h = h.astype(jnp.bfloat16)
            g = (grad_hidden * slope).astype(jnp.bfloat16)
            total += jnp.sum(g.astype(jnp.float32), axis=0, keepdims=True)
            forth = lax.dot_general(h, wd[block], nt, preferred_element_type=jnp.float32)
            back = lax.dot_general(g, wu[block], nt, preferred_element_type=jnp.float32)
            if block or not first:
                if not block:
                    for made in sum_copies:
                        made.wait()
                forth += branch[at, :]
                back += mid[at, :]
            branch[at, :] = forth
            mid[at, :] = back
            if block:
                outs += [started(branch.at[at], branch_out.at[at]), started(mid.at[at], mid_out.at[at])]
            hs.append(h)
            gs.append(g)
        dbu[block : block + 1, :] = total
        if block == 0:
            cott_copy.wait()
        dw[block, 1] = matmul(cott[...], jnp.concatenate(hs, axis=0)).astype(jnp.bfloat16)
        outs.append(started(dw.at[block, 1], grads[block].at[1]))
        if block == 0:
            xt_copy.wait()
        dw[block, 0] = matmul(xt[...], jnp.concatenate(gs, axis=0)).astype(jnp.bfloat16)
        outs.append(started(dw.at[block, 0], grads[block].at[0]))
    for made in outs:
        made.wait()


def ff_blocks(x, cot, xt, cott, weights, places, bu, *sums):
    f32, bf = (jnp.float32, jnp.bfloat16)
    count, wide = (x.shape[0], bu.shape[1])
    spec = pl.BlockSpec(memory_space=pltpu.VMEM)
    far = pl.BlockSpec(memory_space=pl.ANY)
    return pl.pallas_call(
        functools.partial(ff_kernel, not sums, 256, places),
        out_shape=(
            pltpu.HBM((count, D), f32),
            pltpu.HBM((count, D), f32),
            pltpu.HBM((2, D, wide), bf),
            pltpu.HBM((2, D, wide), bf),
            jax.ShapeDtypeStruct((2, wide), f32),
        ),
        in_specs=[far] * 8 + [spec] + [far] * len(sums),
        out_specs=(far, far, far, far, spec),
        scratch_shapes=[
            pltpu.VMEM((count, D), bf),
            pltpu.VMEM((count, D), bf),
            pltpu.VMEM((D, count), bf),
            pltpu.VMEM((D, count), bf),
            pltpu.VMEM((2, D, wide), bf),
            pltpu.VMEM((2, D, wide), bf),
            pltpu.VMEM((count, D), f32),
            pltpu.VMEM((count, D), f32),
            pltpu.VMEM((2, 2, D, wide), bf),
            pltpu.SemaphoreType.DMA((40,)),
        ],
        compiler_params=pltpu.CompilerParams(vmem_limit_bytes=48 * 1024 * 1024),
        cost_estimate=pl.CostEstimate(
            flops=24 * count * D * wide, bytes_accessed=8 * D * wide, transcendentals=4 * count * wide
        ),
        name="ff_blocks",
    )(x, cot, xt, cott, *weights, bu, *sums)


STEP = 256
ROWS = pl.BlockSpec((STEP, D), lambda i: (i, 0))
WHOLE = pl.BlockSpec((D, D), lambda i: (0, 0))
LINE = pl.BlockSpec((1, D), lambda i: (0, 0))
LINES = pl.BlockSpec((8, D), lambda i: (0, 0))


def by_rows(kernel, name, in_specs, out_specs, out_shape, scratch, flops, moved):
    return pl.pallas_call(
        kernel,
        grid=(SEQ // STEP,),
        in_specs=in_specs,
        out_specs=out_specs,
        out_shape=out_shape,
        scratch_shapes=scratch,
        compiler_params=pltpu.CompilerParams(vmem_limit_bytes=32 * 1024 * 1024),
        cost_estimate=pl.CostEstimate(flops=flops, bytes_accessed=moved, transcendentals=SEQ),
        name=name,
    )


def middle_kernel(mixed, tokens, out_full, b_out, gain, shift, residual, x, x_t):
    value = tokens[...].astype(jnp.float32) + (matmul(mixed[...], out_full[...]) + b_out[...])
    residual[...] = value
    unit, _ = moments(value)
    normed = (unit * gain[...] + shift[...]).astype(jnp.bfloat16)
    x[...] = normed
    x_t[...] = normed.T


def middle(mixed, tokens, out_full, b_out, gain, shift):
    f32, bf = (jnp.float32, jnp.bfloat16)
    return by_rows(
        middle_kernel,
        "middle",
        [ROWS, ROWS, WHOLE, LINE, LINE, LINE],
        (ROWS, ROWS, pl.BlockSpec((D, STEP), lambda i: (0, i))),
        (pltpu.HBM((SEQ, D), f32), pltpu.HBM((SEQ, D), bf), pltpu.HBM((D, SEQ), bf)),
        [],
        2 * SEQ * D * D,
        12 * SEQ * D,
    )(mixed, tokens, out_full, b_out[None], gain[None], shift[None])


def add_lines(ref, lines):
    @pl.when(pl.program_id(0) == 0)
    def _():
        ref[...] = jnp.zeros_like(ref)

    sums = [jnp.sum(line.astype(jnp.float32), axis=0, keepdims=True) for line in lines]
    ref[: len(lines), :] += jnp.concatenate(sums, axis=0)


def turn_kernel(branch, grad_mid, residual, cot, mixed, out_full, b_down, gain, output, grad_resid, grad_mixed, out_grad, lines, held):
    value = residual[...]
    output[...] = (value + branch[...] + b_down[...]).astype(jnp.bfloat16)
    grad = grad_mid[...]
    unit, scale = moments(value)
    pulled = cot[...].astype(jnp.float32) + norm_pull(grad, gain[...], unit, scale)
    grad_resid[...] = pulled
    low = pulled.astype(jnp.bfloat16)
    grad_mixed[...] = matmul_nt(low, out_full[...]).astype(jnp.bfloat16)
    add_lines(lines, [low, grad * unit, grad, cot[...]])

    @pl.when(pl.program_id(0) == 0)
    def _():
        held[...] = jnp.zeros_like(held)

    held[...] += matmul_tn(mixed[...], low)

    @pl.when(pl.program_id(0) == pl.num_programs(0) - 1)
    def _():
        out_grad[...] = held[...].astype(jnp.bfloat16)


def turn(branch, grad_mid, residual, cot, mixed, out_full, b_down, gain):
    f32, bf = (jnp.float32, jnp.bfloat16)
    low = jax.ShapeDtypeStruct((SEQ, D), bf)
    return by_rows(
        turn_kernel,
        "turn",
        [ROWS, ROWS, ROWS, ROWS, ROWS, WHOLE, LINE, LINE],
        (ROWS, ROWS, ROWS, WHOLE, LINES),
        (pltpu.HBM((SEQ, D), bf), pltpu.HBM((SEQ, D), f32), low, pltpu.HBM((D, D), bf), jax.ShapeDtypeStruct((8, D), f32)),
        [pltpu.VMEM((D, D), f32)],
        4 * SEQ * D * D,
        24 * SEQ * D,
    )(branch, grad_mid, residual, cot, mixed, out_full, b_down[None], gain[None])


def last_kernel(gq, gk, gv, wq, wk, wv, tokens, grad_resid, gain, tokens_grad, lines):
    grad = matmul_nt(gq[...], wq[...]) + matmul_nt(gk[...], wk[...]) + matmul_nt(gv[...], wv[...])
    unit, scale = moments(tokens[...].astype(jnp.float32))
    tokens_grad[...] = (grad_resid[...] + norm_pull(grad, gain[...], unit, scale)).astype(jnp.bfloat16)
    add_lines(lines, [grad * unit, grad, gq[...], gv[...]])


def last(gq, gk, gv, wq, wk, wv, tokens, grad_resid, gain):
    return by_rows(
        last_kernel,
        "last",
        [ROWS, ROWS, ROWS, WHOLE, WHOLE, WHOLE, ROWS, ROWS, LINE],
        (ROWS, LINES),
        (jax.ShapeDtypeStruct((SEQ, D), jnp.bfloat16), jax.ShapeDtypeStruct((8, D), jnp.float32)),
        [],
        6 * SEQ * D * D,
        14 * SEQ * D,
    )(gq, gk, gv, wq, wk, wv, tokens, grad_resid, gain[None])


def tied(*arrays):
    return lax.optimization_barrier(arrays)


def packed(sent, small):
    high = small.astype(jnp.bfloat16)
    low = (small - high.astype(jnp.float32)).astype(jnp.bfloat16)
    return jnp.concatenate([sent.reshape(-1, D), high, low])


def unpacked(got, like):
    rows = like.size // D
    high, low = jnp.split(got[rows:].astype(jnp.float32), 2)
    return (got[:rows].reshape(like.shape), high + low)


def added(own, got):
    return (own.astype(jnp.float32) + got.astype(jnp.float32)).astype(jnp.bfloat16)


def dot(a, b, ca=1, cb=0):
    return lax.dot_general(a, b, (((ca,), (cb,)), ((), ())), preferred_element_type=jnp.float32)


def rounded_sum(pieces):
    return summed(pieces).astype(jnp.bfloat16)


def sum_halves(pieces, axis, bit, place):
    both = [halves(piece, axis, bit, place) for piece in pieces]
    return (rounded_sum([kept for kept, _ in both]), rounded_sum([sent for _, sent in both]))


def own_half(wide):
    rows = lax.broadcasted_iota(jnp.int32, wide.shape, 0) // PAD
    columns = lax.broadcasted_iota(jnp.int32, wide.shape, 1) // HEAD
    return jnp.where(rows == columns, wide, 0.0)


def pair_rows(ids):
    at = lax.broadcasted_iota(jnp.int32, (PAD, SEQ), 0)
    return jnp.concatenate([jnp.where(ids[k : k + 1, :] == at, 1.0, 0.0) for k in (0, 1)], axis=0).astype(jnp.bfloat16)


def pair_columns(ids):
    at = lax.broadcasted_iota(jnp.int32, (SEQ, PAD), 1)
    return jnp.concatenate([jnp.where(ids[:, k : k + 1] == at, 1.0, 0.0) for k in (0, 1)], axis=1).astype(jnp.bfloat16)


def attend_kernel(q, k, v, rows, columns, seg_row, seg_col, mixed, prob, centroid, count):
    bf = jnp.bfloat16
    hot = pair_rows(rows[0])
    lanes = lax.broadcasted_iota(jnp.int32, (SEQ, PAD), 1)
    marks = jnp.where(lanes == 0, seg_col[...], jnp.where(lanes == 1, 1.0, 0.0)).astype(bf)
    sums = dot(hot, jnp.concatenate([q[...], marks], axis=1))
    owner, counts = (sums[:, 128:129], sums[:, 129:130])
    counts = jnp.maximum(counts, 1.0)
    middle = own_half(sums[:, :128] / counts).astype(bf)
    scores = 0.125 * dot(middle, k[...], 1, 1)
    allowed = jnp.abs(owner - counts * seg_row[...]) < 0.5
    masked = jnp.where(allowed, scores, -1e30)
    highest = jnp.max(masked, axis=1, keepdims=True)
    exponent = jnp.where(allowed, jnp.exp(masked - highest), 0.0)
    total = jnp.sum(exponent, axis=1, keepdims=True)
    p = exponent * (1.0 / jnp.maximum(total, 1e-30))
    context = own_half(dot(p.astype(bf), v[...])).astype(bf)
    mixed[...] = dot(pair_columns(columns[0]), context).astype(bf)
    prob[0] = p
    centroid[0] = middle
    count[0] = jnp.broadcast_to(counts, (2 * PAD, 128))


def attend(q, k, v, rows, columns, seg_row, seg_col):
    bf = jnp.bfloat16
    pair = pl.BlockSpec((SEQ, 128), lambda i: (0, i))
    return pl.pallas_call(
        attend_kernel,
        grid=(HEADS // 2,),
        in_specs=[pair, pair, pair,
            pl.BlockSpec((1, 2, SEQ), lambda i: (i, 0, 0)),
            pl.BlockSpec((1, SEQ, 2), lambda i: (i, 0, 0)),
            pl.BlockSpec((1, SEQ), lambda i: (0, 0)),
            pl.BlockSpec((SEQ, 1), lambda i: (0, 0))],
        out_specs=(pair, pl.BlockSpec((1, 2 * PAD, SEQ), lambda i: (i, 0, 0)), pl.BlockSpec((1, 2 * PAD, 128), lambda i: (i, 0, 0)), pl.BlockSpec((1, 2 * PAD, 128), lambda i: (i, 0, 0))),
        out_shape=(pltpu.HBM((SEQ, D), bf), pltpu.HBM((HEADS // 2, 2 * PAD, SEQ), jnp.float32), pltpu.HBM((HEADS // 2, 2 * PAD, 128), bf), pltpu.HBM((HEADS // 2, 2 * PAD, 128), jnp.float32)),
        cost_estimate=pl.CostEstimate(flops=12 * 5 * 2 * PAD * SEQ * HEAD, bytes_accessed=14 << 20, transcendentals=HEADS * PAD * SEQ),
        compiler_params=pltpu.CompilerParams(vmem_limit_bytes=24 * 1024 * 1024),
        name="attend",
    )(q, k, v, rows, columns, seg_row, seg_col)


def attend_back_kernel(k, v, gm, rows, columns, prob, centroid, count, gq, gk, gv):
    bf = jnp.bfloat16
    hot = pair_rows(rows[0])
    p = prob[0]
    grad_context = own_half(dot(hot, gm[...])).astype(bf)
    gv[...] = dot(p.astype(bf), grad_context, 0, 0).astype(bf)
    grad_prob = dot(grad_context, v[...], 1, 1)
    grad_scores = (p * (grad_prob - jnp.sum(p * grad_prob, axis=1, keepdims=True))).astype(bf)
    grad_centroid = own_half(0.125 * dot(grad_scores, k[...]) / count[0]).astype(bf)
    gk[...] = (0.125 * dot(grad_scores, centroid[0], 0, 0)).astype(bf)
    gq[...] = dot(pair_columns(columns[0]), grad_centroid).astype(bf)


def attend_back(k, v, gm, rows, columns, prob, centroid, count):
    bf = jnp.bfloat16
    pair = pl.BlockSpec((SEQ, 128), lambda i: (0, i))
    wide = pl.BlockSpec((1, 2 * PAD, 128), lambda i: (i, 0, 0))
    out = pltpu.HBM((SEQ, D), bf)
    return pl.pallas_call(
        attend_back_kernel,
        grid=(HEADS // 2,),
        in_specs=[pair, pair, pair,
            pl.BlockSpec((1, 2, SEQ), lambda i: (i, 0, 0)),
            pl.BlockSpec((1, SEQ, 2), lambda i: (i, 0, 0)),
            pl.BlockSpec((1, 2 * PAD, SEQ), lambda i: (i, 0, 0)), wide, wide],
        out_specs=(pair, pair, pair),
        out_shape=(out, out, out),
        cost_estimate=pl.CostEstimate(flops=12 * 7 * 2 * PAD * SEQ * HEAD, bytes_accessed=16 << 20, transcendentals=0),
        compiler_params=pltpu.CompilerParams(vmem_limit_bytes=24 * 1024 * 1024),
        name="attend_back",
    )(k, v, gm, rows, columns, prob, centroid, count)


def shards(
    tokens,
    segment_ids,
    cluster_ids,
    cotangent,
    first_gain,
    first_shift,
    w_query,
    b_query,
    w_key,
    w_value,
    b_value,
    w_out,
    b_out,
    second_gain,
    second_shift,
    w_up,
    b_up,
    w_down,
    b_down,
):
    groups = high_groups()
    tops = 1 << sum(bits for _, bits in groups)
    bf = jnp.bfloat16
    part = D // (8 * tops)
    wide = D // (2 * tops)
    whole = [1 << bits for _, bits in reversed(groups)]

    attn = jnp.stack([w.astype(bf) for w in (w_query, w_key, w_value, w_out)])
    up, down = (w_up.astype(bf), w_down.T.astype(bf))
    unit_in, _ = moments(tokens.astype(jnp.float32))
    normed_in = (unit_in * first_gain + first_shift).astype(bf)
    id_rows = cluster_ids.reshape(HEADS // 2, 2, SEQ)
    id_columns = id_rows.transpose(0, 2, 1)
    seg = segment_ids.astype(jnp.float32)
    seg_row, seg_col = (seg[None, :], seg[:, None])
    cot_t = cotangent.T
    for group in groups:
        got = exchanged(attn, group)
        normed_in, id_columns, seg_col, *got = tied(normed_in, id_columns, seg_col, *got)
        attn = lined_up(attn, got, group, 1)
    attn = attn.reshape(4, tops, part, D)
    first, second = (attn[:2], attn[2:])
    first_got, second_got = (swapped(first, "dp", 1), swapped(second, "hid", 1))
    for group in groups[:-1]:
        up = lined_up(up, exchanged(up, group), group, 0)
        down = lined_up(down, exchanged(down, group), group, 0)
    up_got, down_got = (exchanged(up, groups[-1]), exchanged(down, groups[-1]))
    cot_t, first_got, second_got = tied(cot_t, first_got, second_got)
    first = joined(first, first_got, own_bit("dp", 0), 2)
    second = joined(second, second_got, own_bit("hid", 0), 2)
    first_got, second_got = (swapped(first, "hid", 1), swapped(second, "dp", 1))
    first_got, second_got, *up_got = tied(first_got, second_got, *up_got)
    half = tops // 2
    up = lined_up(up, up_got, groups[-1], 0).reshape(tops, wide, D)
    up_one, up_two = (up[:half], up[half:])
    up_one_got, up_two_got = (swapped(up_one, "dp", 1), swapped(up_two, "hid", 1))
    first = joined(first, first_got, own_bit("hid", 0), 3)
    second = joined(second, second_got, own_bit("dp", 0), 2)
    first_got, second_got = (swapped(first, "mp", 1), swapped(second, "mp", 1))
    first = joined(first, first_got, own_bit("mp", 0), 4)
    second = joined(second, second_got, own_bit("mp", 0), 4)
    query_full, key_full = first.reshape(2, D, D)
    value_full, out_full = second.reshape(2, D, D)

    query = (matmul(normed_in, query_full) + b_query).astype(bf)
    query, up_one_got, up_two_got = tied(query, up_one_got, up_two_got)
    up_one, up_two = (joined(up_one, up_one_got, own_bit("dp", 0), 1), jnp.stack([up_two, up_two_got]))
    up_one_got, up_two_got = (swapped(up_one, "hid", 1), swapped(up_two, "dp", 1))
    key_rows = matmul(normed_in, key_full).astype(bf)
    key_rows, *down_got = tied(key_rows, *down_got)
    down = lined_up(down, down_got, groups[-1], 0).reshape(tops, wide, D)
    down_one, down_two = (down[:half], down[half:])
    down_one_got, down_two_got = (swapped(down_one, "dp", 1), swapped(down_two, "hid", 1))
    value_rows = (matmul(normed_in, value_full) + b_value).astype(bf)
    mixed, probability, centroid, counts = attend(
        query, key_rows, value_rows, id_rows, id_columns, seg_row, seg_col
    )
    mixed, down_one_got, down_two_got, up_one_got, up_two_got = tied(
        mixed, down_one_got, down_two_got, up_one_got, up_two_got
    )
    down_one, down_two = (joined(down_one, down_one_got, own_bit("dp", 0), 1), jnp.stack([down_two, down_two_got]))
    down_one_got, down_two_got = (swapped(down_one, "hid", 1), swapped(down_two, "dp", 1))
    up_two = joined(up_two, up_two_got, own_bit("dp", 0), 2)
    ups = jnp.stack([jnp.concatenate([up_one, up_two[0]]), jnp.concatenate([up_one_got, up_two[1]])])
    ups = ups.reshape(2, D, D)
    ups_next = swapped(ups, "mp", 1)
    residual, x, x_t = middle(mixed, tokens, out_full, b_out, second_gain, second_shift)
    x, down_one_got, down_two_got, ups_next = tied(x, down_one_got, down_two_got, ups_next)
    down_two = joined(down_two, down_two_got, own_bit("dp", 0), 2)
    down_mate = jnp.concatenate([down_one_got, down_two[1]]).reshape(1, D, D)
    down_across = swapped(down_mate, "mp", 1)
    down = jnp.concatenate([down_one, down_two[0]]).reshape(1, D, D)
    down_next = swapped(down, "mp", 1)
    me = lax.axis_index(("hid", "mp"))
    biases = lambda blocks: jnp.stack([lax.dynamic_slice_in_dim(b_up, block * D, D) for block in blocks])
    split = lambda piece: piece.reshape(tops, 2, wide, D)
    *sums, sent, own, far_bias = ff_blocks(
        x, cotangent, x_t, cot_t, (ups_next, down_across, ups, down_mate), (1, 0, 1, 0), biases((me ^ 3, me ^ 2))
    )
    got = swapped(sent, "mp", 1)
    up_far = added(own[0], got[0])
    down_far, down_sent = sum_halves([split(own[1]), split(got[1])], "dp", 0, 1)
    *sums, up_far, down_sent = tied(*sums, up_far, down_sent)
    up_far_got = swapped(up_far, "hid", 1)
    down_far_got = swapped(down_sent, "dp", 1)
    branch, grad_mid, sent, own, near_bias = ff_blocks(
        x, cotangent, x_t, cot_t, (ups_next, down_next, ups, down), (0, 0, 0, 0), biases((me ^ 1, me)), *sums
    )
    near_got = swapped(sent, "mp", 1)
    bias_up = jnp.zeros((4, D), jnp.float32)
    for block, bias in ((me ^ 3, far_bias[:1]), (me ^ 2, far_bias[1:]), (me ^ 1, near_bias[:1]), (me, near_bias[1:])):
        bias_up = lax.dynamic_update_slice(bias_up, bias, (block, 0))
    down_far = added(down_far, down_far_got)
    branch, grad_mid, down_far = tied(branch, grad_mid, down_far)
    down_got = swapped(down_far, "hid", 1)

    output, grad_resid, grad_mixed, out_grad, turn_lines = turn(
        branch, grad_mid, residual, cotangent, mixed, out_full, b_down, second_gain
    )
    grad_mixed, near_got, up_far_got = tied(grad_mixed, near_got, up_far_got)
    down_near, down_sent = sum_halves([split(own[1]), split(near_got[1])], "dp", 0, 1)
    up_near, up_sent = sum_halves([split(own[0]), split(near_got[0]), split(up_far_got)], "dp", 0, 1)
    grad_mixed, down_sent, up_sent = tied(grad_mixed, down_sent, up_sent)
    down_near_got = swapped(down_sent, "dp", 1)
    up_got = swapped(up_sent, "dp", 1)

    grad_query, grad_key, grad_value = attend_back(
        key_rows, value_rows, grad_mixed, id_rows, id_columns, probability, centroid, counts
    )
    grad_value, down_got, down_near_got = tied(grad_value, down_got, down_near_got)
    down_sum = rounded_sum([down_near, down_near_got, down_got]).reshape(*whole, wide, D)
    down_parts = dealt(down_sum, groups[-1], 0)

    query_grad = matmul_tn(normed_in, grad_query).astype(bf)
    key_grad = matmul_tn(normed_in, grad_key).astype(bf)
    value_grad = matmul_tn(normed_in, grad_value).astype(bf)
    value_grad, up_got = tied(value_grad, up_got)
    up_parts = dealt(added(up_near, up_got).reshape(*whole, wide, D), groups[-1], 0)
    both = jnp.stack([query_grad, key_grad, value_grad, out_grad]).reshape(4, tops, 2, 2, 2, part, D)
    both, sent = halves(both, "mp", 0, 4)
    got = swapped(sent, "mp", 1)
    tokens_grad, last_lines = last(
        grad_query, grad_key, grad_value, query_full, key_full, value_full, tokens, grad_resid, first_gain
    )
    small = jnp.concatenate([last_lines[:4], turn_lines[:4], bias_up])
    small, *down_parts = tied(small, *down_parts)
    small = small + swapped(small, "mp", 1)
    both = added(both, got)
    one, one_sent = halves(both[:2], "dp", 0, 2)
    two, two_sent = halves(both[2:], "hid", 0, 3)
    got, two_got = (swapped(packed(one_sent, small), "dp", 1), swapped(two_sent, "hid", 1))
    got, two_got, *up_parts = tied(got, two_got, *up_parts)
    one_got, small_got = unpacked(got, one_sent)
    small = small + small_got
    one, one_sent = halves(added(one, one_got), "hid", 0, 2)
    two, two_sent = halves(added(two, two_got), "dp", 0, 2)
    got, two_got = (swapped(packed(one_sent, small), "hid", 1), swapped(two_sent, "dp", 1))
    one_got, small_got = unpacked(got, one_sent)
    small = small + small_got
    both = jnp.stack([added(one, one_got), added(two, two_got)]).reshape(4, *whole, part, D)
    for group in reversed(groups):
        shift, bits = group
        mine = (lax.axis_index("dp") >> shift) & ((1 << bits) - 1)
        take = lambda k: lax.dynamic_index_in_dim(both, k, 1, keepdims=False)
        got = [swapped(packed(take(mine ^ d), small), "dp", d << shift) for d in range(1, 1 << bits)]
        pieces = [unpacked(g, take(mine)) for g in got]
        sums = summed([take(mine)] + [piece for piece, _ in pieces])
        small = summed([small] + [piece for _, piece in pieces])
        both = sums.astype(bf)
    for group in reversed(groups[:-1]):
        up_parts = dealt(rounded_sum(up_parts), group, 0)
        down_parts = dealt(rounded_sum(down_parts), group, 0)
    up_grad, down_grad = (summed(up_parts), summed(down_parts).T)
    query_sum, key_sum, value_sum, out_sum = sums
    return (
        output,
        tokens_grad,
        small[0],
        small[1],
        query_sum,
        small[2],
        key_sum,
        value_sum,
        small[3],
        out_sum,
        small[4],
        small[5],
        small[6],
        up_grad,
        small[8:].reshape(-1),
        down_grad,
        small[7],
    )


def solution(mesh):
    return jax.shard_map(
        shards,
        mesh=mesh,
        in_specs=(
            P(("dp", "hid", "mp"), None),
            P(("dp", "hid", "mp")),
            P(None, ("dp", "hid", "mp")),
            P(("dp", "hid", "mp"), None),
            P(),
            P(),
            P(("dp", "hid", "mp"), None),
            P(),
            P(("dp", "hid", "mp"), None),
            P(("dp", "hid", "mp"), None),
            P(),
            P(("dp", "hid", "mp"), None),
            P(),
            P(),
            P(),
            P("dp", ("hid", "mp")),
            P(),
            P(("hid", "mp"), "dp"),
            P(),
        ),
        out_specs=(
            P(("dp", "hid", "mp"), None),
            P(("dp", "hid", "mp"), None),
            P(),
            P(),
            P(("dp", "hid", "mp"), None),
            P(),
            P(("dp", "hid", "mp"), None),
            P(("dp", "hid", "mp"), None),
            P(),
            P(("dp", "hid", "mp"), None),
            P(),
            P(),
            P(),
            P("dp", ("hid", "mp")),
            P(),
            P(("hid", "mp"), "dp"),
            P(),
        ),
        check_vma=False,
    )
```

```python
import functools

import jax
import jax.numpy as jnp
from jax import lax
from jax.experimental import pallas as pl
from jax.experimental.pallas import tpu as pltpu
from jax.sharding import PartitionSpec as P

D = 768
HEADS = 12
HEAD = 64
CLUSTERS = 100
SEQ = 1024
PAD = 128


def matmul(left, right):
    return jnp.dot(left, right, preferred_element_type=jnp.float32)


def matmul_nt(left, right):
    return lax.dot_general(left, right, (((1,), (1,)), ((), ())), preferred_element_type=jnp.float32)


def matmul_tn(left, right):
    return lax.dot_general(left, right, (((0,), (0,)), ((), ())), preferred_element_type=jnp.float32)


def swapped(array, axis, mask):
    count = lax.axis_size(axis)
    return lax.ppermute(array, axis, [(i, i ^ mask) for i in range(count)])


def own_bit(axis, bit):
    return (lax.axis_index(axis) >> bit) & 1


def joined(own, other, mine, place):
    own, other = (jnp.expand_dims(own, place), jnp.expand_dims(other, place))
    shape = own.shape[:place] + (2,) + own.shape[place + 1 :]
    return jnp.where(lax.broadcasted_iota(jnp.int32, shape, place) == mine, own, other)


def halves(array, axis, bit, place):
    mine = own_bit(axis, bit)
    take = lambda k: lax.dynamic_index_in_dim(array, k, place, keepdims=False)
    return (take(mine), take(1 - mine))


def high_groups():
    count = lax.axis_size("dp").bit_length() - 1
    return [(b, min(2, count - b)) for b in range(1, count, 2)]


def exchanged(piece, group):
    shift, bits = group
    return [swapped(piece, "dp", d << shift) for d in range(1, 1 << bits)]


def lined_up(own, others, group, place):
    shift, bits = group
    mine = (lax.axis_index("dp") >> shift) & ((1 << bits) - 1)
    pieces = [jnp.expand_dims(p, place) for p in [own, *others]]
    shape = pieces[0].shape[:place] + (1 << bits,) + pieces[0].shape[place + 1 :]
    apart = lax.broadcasted_iota(jnp.int32, shape, place) ^ mine
    out = jnp.broadcast_to(pieces[-1], shape)
    for d in reversed(range(len(pieces) - 1)):
        out = jnp.where(apart == d, pieces[d], out)
    return out


def dealt(array, group, place):
    shift, bits = group
    mine = (lax.axis_index("dp") >> shift) & ((1 << bits) - 1)
    take = lambda k: lax.dynamic_index_in_dim(array, k, place, keepdims=False)
    return [take(mine)] + [swapped(take(mine ^ d), "dp", d << shift) for d in range(1, 1 << bits)]


def summed(pieces):
    return sum(p.astype(jnp.float32) for p in pieces)


def moments(values):
    middle = jnp.mean(values, axis=-1, keepdims=True)
    centered = values - middle
    spread = jnp.mean(centered * centered, axis=-1, keepdims=True)
    return (centered * lax.rsqrt(spread + 1e-05), lax.rsqrt(spread + 1e-05))


def norm_pull(grad, gain, unit, scale):
    scaled = grad * gain
    first = jnp.mean(scaled, axis=-1, keepdims=True)
    second = jnp.mean(scaled * unit, axis=-1, keepdims=True)
    return scale * (scaled - first - unit * second)


def gate_and_slope(v):
    size = jnp.abs(v)
    bell = jnp.exp(-0.5 * v * v)
    t = 1.0 / (1.0 + 0.23164189 * size)
    series = 0.7107068705 + t * (-0.7265760135 + t * 0.5307027145)
    tail = t * (0.127414796 + t * (-0.142248368 + t * series)) * bell
    phi = jnp.where(v < 0, tail, 1.0 - tail)
    return (v * phi, phi + v * (0.3989422804014327 * bell))


def ff_kernel(first, rows, places, *refs):
    x_in, cot_in, xt_in, cott_in, *weights, bu = refs[:9]
    refs = refs[9:]
    if not first:
        branch_in, mid_in = refs[:2]
        refs = refs[2:]
    branch_out, mid_out, *grads = refs[:4]
    dbu, x, cot, xt, cott, wu, wd, branch, mid, branch_old, mid_old, dw, sems = refs[4:]
    nt = (((1,), (1,)), ((), ()))
    parts = [pl.ds(r * rows, rows) for r in range(x.shape[0] // rows)]
    used = [0]

    def started(source, target):
        used[0] += 1
        made = pltpu.make_async_copy(source, target, sems.at[used[0] - 1])
        made.start()
        return made

    def finish(made):
        for one in made:
            one.wait()

    def fetch_weight(k, target):
        ref, place = (weights[k], places[k])
        return started(ref.at[place], target.at[k // 2])

    early = [fetch_weight(0, wu), started(x_in, x), fetch_weight(1, wd), started(cot_in, cot)]
    finish(early)
    late = [started(cott_in, cott), started(xt_in, xt), fetch_weight(2, wu), fetch_weight(3, wd)]
    if not first:
        late += [started(branch_in, branch_old), started(mid_in, mid_old)]
    outs = []
    for block in (0, 1):
        hs, gs = ([], [])
        total = jnp.zeros((1, dbu.shape[1]), jnp.float32)
        for at in parts:
            pre = matmul(x[at, :], wu[block]) + bu[block : block + 1, :]
            grad_hidden = matmul(cot[at, :], wd[block])
            h, slope = gate_and_slope(pre)
            h = h.astype(jnp.bfloat16)
            g = (grad_hidden * slope).astype(jnp.bfloat16)
            total += jnp.sum(g.astype(jnp.float32), axis=0, keepdims=True)
            forth = lax.dot_general(h, wd[block], nt, preferred_element_type=jnp.float32)
            back = lax.dot_general(g, wu[block], nt, preferred_element_type=jnp.float32)
            if block:
                forth += branch[at, :]
                back += mid[at, :]
                if not first:
                    forth += branch_old[at, :]
                    back += mid_old[at, :]
            branch[at, :] = forth
            mid[at, :] = back
            hs.append(h)
            gs.append(g)
        dbu[block : block + 1, :] = total
        if block == 0:
            finish(late)
        else:
            outs += [started(branch, branch_out), started(mid, mid_out)]
        dw[block, 1] = matmul(cott[...], jnp.concatenate(hs, axis=0)).astype(jnp.bfloat16)
        outs.append(started(dw.at[block, 1], grads[block].at[1]))
        dw[block, 0] = matmul(xt[...], jnp.concatenate(gs, axis=0)).astype(jnp.bfloat16)
        outs.append(started(dw.at[block, 0], grads[block].at[0]))
    finish(outs)


def ff_blocks(x, cot, xt, cott, weights, places, bu, *sums):
    f32, bf = (jnp.float32, jnp.bfloat16)
    count, wide = (x.shape[0], bu.shape[1])
    spec = pl.BlockSpec(memory_space=pltpu.VMEM)
    far = pl.BlockSpec(memory_space=pl.ANY)
    return pl.pallas_call(
        functools.partial(ff_kernel, not sums, 256, places),
        out_shape=(
            pltpu.HBM((count, D), f32),
            pltpu.HBM((count, D), f32),
            pltpu.HBM((2, D, wide), bf),
            pltpu.HBM((2, D, wide), bf),
            jax.ShapeDtypeStruct((2, wide), f32),
        ),
        in_specs=[far] * 8 + [spec] + [far] * len(sums),
        out_specs=(far, far, far, far, spec),
        scratch_shapes=[
            pltpu.VMEM((count, D), bf),
            pltpu.VMEM((count, D), bf),
            pltpu.VMEM((D, count), bf),
            pltpu.VMEM((D, count), bf),
            pltpu.VMEM((2, D, wide), bf),
            pltpu.VMEM((2, D, wide), bf),
            pltpu.VMEM((count, D), f32),
            pltpu.VMEM((count, D), f32),
            pltpu.VMEM((count, D), f32),
            pltpu.VMEM((count, D), f32),
            pltpu.VMEM((2, 2, D, wide), bf),
            pltpu.SemaphoreType.DMA((16,)),
        ],
        compiler_params=pltpu.CompilerParams(vmem_limit_bytes=60 * 1024 * 1024),
        cost_estimate=pl.CostEstimate(
            flops=24 * count * D * wide, bytes_accessed=8 * D * wide, transcendentals=4 * count * wide
        ),
        name="ff_blocks",
    )(x, cot, xt, cott, *weights, bu, *sums)


STEP = 256
ROWS = pl.BlockSpec((STEP, D), lambda i: (i, 0))
WHOLE = pl.BlockSpec((D, D), lambda i: (0, 0))
LINE = pl.BlockSpec((1, D), lambda i: (0, 0))
LINES = pl.BlockSpec((8, D), lambda i: (0, 0))


def by_rows(kernel, name, in_specs, out_specs, out_shape, scratch, flops, moved):
    return pl.pallas_call(
        kernel,
        grid=(SEQ // STEP,),
        in_specs=in_specs,
        out_specs=out_specs,
        out_shape=out_shape,
        scratch_shapes=scratch,
        compiler_params=pltpu.CompilerParams(vmem_limit_bytes=60 * 1024 * 1024),
        cost_estimate=pl.CostEstimate(flops=flops, bytes_accessed=moved, transcendentals=SEQ),
        name=name,
    )


def middle_kernel(mixed, tokens, out_full, b_out, gain, shift, residual, x, x_t):
    value = tokens[...].astype(jnp.float32) + (matmul(mixed[...], out_full[...]) + b_out[...])
    residual[...] = value
    unit, _ = moments(value)
    normed = (unit * gain[...] + shift[...]).astype(jnp.bfloat16)
    x[...] = normed
    x_t[...] = normed.T


def middle(mixed, tokens, out_full, b_out, gain, shift):
    f32, bf = (jnp.float32, jnp.bfloat16)
    return by_rows(
        middle_kernel,
        "middle",
        [ROWS, ROWS, WHOLE, LINE, LINE, LINE],
        (ROWS, ROWS, pl.BlockSpec((D, STEP), lambda i: (0, i))),
        (pltpu.HBM((SEQ, D), f32), pltpu.HBM((SEQ, D), bf), pltpu.HBM((D, SEQ), bf)),
        [],
        2 * SEQ * D * D,
        12 * SEQ * D,
    )(mixed, tokens, out_full, b_out[None], gain[None], shift[None])


def add_lines(ref, lines):
    @pl.when(pl.program_id(0) == 0)
    def _():
        ref[...] = jnp.zeros_like(ref)

    sums = [jnp.sum(line.astype(jnp.float32), axis=0, keepdims=True) for line in lines]
    ref[: len(lines), :] += jnp.concatenate(sums, axis=0)


def turn_kernel(branch, grad_mid, residual, cot, mixed, out_full, b_down, gain, output, grad_resid, grad_mixed, out_grad, lines, held):
    value = residual[...]
    output[...] = (value + branch[...] + b_down[...]).astype(jnp.bfloat16)
    grad = grad_mid[...]
    unit, scale = moments(value)
    pulled = cot[...].astype(jnp.float32) + norm_pull(grad, gain[...], unit, scale)
    grad_resid[...] = pulled
    low = pulled.astype(jnp.bfloat16)
    grad_mixed[...] = matmul_nt(low, out_full[...]).astype(jnp.bfloat16)
    add_lines(lines, [low, grad * unit, grad, cot[...]])

    @pl.when(pl.program_id(0) == 0)
    def _():
        held[...] = jnp.zeros_like(held)

    held[...] += matmul_tn(mixed[...], low)

    @pl.when(pl.program_id(0) == pl.num_programs(0) - 1)
    def _():
        out_grad[...] = held[...].astype(jnp.bfloat16)


def turn(branch, grad_mid, residual, cot, mixed, out_full, b_down, gain):
    f32, bf = (jnp.float32, jnp.bfloat16)
    low = jax.ShapeDtypeStruct((SEQ, D), bf)
    return by_rows(
        turn_kernel,
        "turn",
        [ROWS, ROWS, ROWS, ROWS, ROWS, WHOLE, LINE, LINE],
        (ROWS, ROWS, ROWS, WHOLE, LINES),
        (pltpu.HBM((SEQ, D), bf), pltpu.HBM((SEQ, D), f32), low, pltpu.HBM((D, D), bf), jax.ShapeDtypeStruct((8, D), f32)),
        [pltpu.VMEM((D, D), f32)],
        4 * SEQ * D * D,
        24 * SEQ * D,
    )(branch, grad_mid, residual, cot, mixed, out_full, b_down[None], gain[None])


def last_kernel(gq, gk, gv, wq, wk, wv, tokens, grad_resid, gain, tokens_grad, lines):
    grad = matmul_nt(gq[...], wq[...]) + matmul_nt(gk[...], wk[...]) + matmul_nt(gv[...], wv[...])
    unit, scale = moments(tokens[...].astype(jnp.float32))
    tokens_grad[...] = (grad_resid[...] + norm_pull(grad, gain[...], unit, scale)).astype(jnp.bfloat16)
    add_lines(lines, [grad * unit, grad, gq[...], gv[...]])


def last(gq, gk, gv, wq, wk, wv, tokens, grad_resid, gain):
    return by_rows(
        last_kernel,
        "last",
        [ROWS, ROWS, ROWS, WHOLE, WHOLE, WHOLE, ROWS, ROWS, LINE],
        (ROWS, LINES),
        (jax.ShapeDtypeStruct((SEQ, D), jnp.bfloat16), jax.ShapeDtypeStruct((8, D), jnp.float32)),
        [],
        6 * SEQ * D * D,
        14 * SEQ * D,
    )(gq, gk, gv, wq, wk, wv, tokens, grad_resid, gain[None])


def tied(*arrays):
    return lax.optimization_barrier(arrays)


def packed(sent, small):
    high = small.astype(jnp.bfloat16)
    low = (small - high.astype(jnp.float32)).astype(jnp.bfloat16)
    return jnp.concatenate([sent.reshape(-1, D), high, low])


def unpacked(got, like):
    rows = like.size // D
    high, low = jnp.split(got[rows:].astype(jnp.float32), 2)
    return (got[:rows].reshape(like.shape), high + low)


def added(own, got):
    return (own.astype(jnp.float32) + got.astype(jnp.float32)).astype(jnp.bfloat16)


def dot(a, b, ca=1, cb=0):
    return lax.dot_general(a, b, (((ca,), (cb,)), ((), ())), preferred_element_type=jnp.float32)


def rounded_sum(pieces):
    return summed(pieces).astype(jnp.bfloat16)


def sum_halves(pieces, axis, bit, place):
    both = [halves(piece, axis, bit, place) for piece in pieces]
    return (rounded_sum([kept for kept, _ in both]), rounded_sum([sent for _, sent in both]))


def own_half(wide):
    rows = lax.broadcasted_iota(jnp.int32, wide.shape, 0) // PAD
    columns = lax.broadcasted_iota(jnp.int32, wide.shape, 1) // HEAD
    return jnp.where(rows == columns, wide, 0.0)


def pair_rows(ids):
    at = lax.broadcasted_iota(jnp.int32, (PAD, SEQ), 0)
    return jnp.concatenate([jnp.where(ids[k : k + 1, :] == at, 1.0, 0.0) for k in (0, 1)], axis=0).astype(jnp.bfloat16)


def pair_columns(ids):
    at = lax.broadcasted_iota(jnp.int32, (SEQ, PAD), 1)
    return jnp.concatenate([jnp.where(ids[:, k : k + 1] == at, 1.0, 0.0) for k in (0, 1)], axis=1).astype(jnp.bfloat16)


def attend_kernel(q, k, v, rows, columns, seg_row, seg_col, mixed, prob, centroid, count):
    bf = jnp.bfloat16
    hot = pair_rows(rows[0])
    lanes = lax.broadcasted_iota(jnp.int32, (SEQ, PAD), 1)
    marks = jnp.where(lanes == 0, seg_col[...], jnp.where(lanes == 1, 1.0, 0.0)).astype(bf)
    sums = dot(hot, jnp.concatenate([q[...], marks], axis=1))
    owner, counts = (sums[:, 128:129], sums[:, 129:130])
    counts = jnp.maximum(counts, 1.0)
    middle = own_half(sums[:, :128] / counts).astype(bf)
    scores = 0.125 * dot(middle, k[...], 1, 1)
    allowed = jnp.abs(owner - counts * seg_row[...]) < 0.5
    masked = jnp.where(allowed, scores, -1e30)
    highest = jnp.max(masked, axis=1, keepdims=True)
    exponent = jnp.where(allowed, jnp.exp(masked - highest), 0.0)
    total = jnp.sum(exponent, axis=1, keepdims=True)
    p = exponent * (1.0 / jnp.maximum(total, 1e-30))
    context = own_half(dot(p.astype(bf), v[...])).astype(bf)
    mixed[...] = dot(pair_columns(columns[0]), context).astype(bf)
    prob[0] = p
    centroid[0] = middle
    count[0] = jnp.broadcast_to(counts, (2 * PAD, 128))


def attend(q, k, v, rows, columns, seg_row, seg_col):
    bf = jnp.bfloat16
    pair = pl.BlockSpec((SEQ, 128), lambda i: (0, i))
    return pl.pallas_call(
        attend_kernel,
        grid=(HEADS // 2,),
        in_specs=[pair, pair, pair,
            pl.BlockSpec((1, 2, SEQ), lambda i: (i, 0, 0)),
            pl.BlockSpec((1, SEQ, 2), lambda i: (i, 0, 0)),
            pl.BlockSpec((1, SEQ), lambda i: (0, 0)),
            pl.BlockSpec((SEQ, 1), lambda i: (0, 0))],
        out_specs=(pair, pl.BlockSpec((1, 2 * PAD, SEQ), lambda i: (i, 0, 0)), pl.BlockSpec((1, 2 * PAD, 128), lambda i: (i, 0, 0)), pl.BlockSpec((1, 2 * PAD, 128), lambda i: (i, 0, 0))),
        out_shape=(pltpu.HBM((SEQ, D), bf), pltpu.HBM((HEADS // 2, 2 * PAD, SEQ), jnp.float32), pltpu.HBM((HEADS // 2, 2 * PAD, 128), bf), pltpu.HBM((HEADS // 2, 2 * PAD, 128), jnp.float32)),
        cost_estimate=pl.CostEstimate(flops=12 * 5 * 2 * PAD * SEQ * HEAD, bytes_accessed=14 << 20, transcendentals=HEADS * PAD * SEQ),
        compiler_params=pltpu.CompilerParams(vmem_limit_bytes=24 * 1024 * 1024),
        name="attend",
    )(q, k, v, rows, columns, seg_row, seg_col)


def attend_back_kernel(k, v, gm, rows, columns, prob, centroid, count, gq, gk, gv):
    bf = jnp.bfloat16
    hot = pair_rows(rows[0])
    p = prob[0]
    grad_context = own_half(dot(hot, gm[...])).astype(bf)
    gv[...] = dot(p.astype(bf), grad_context, 0, 0).astype(bf)
    grad_prob = dot(grad_context, v[...], 1, 1)
    grad_scores = (p * (grad_prob - jnp.sum(p * grad_prob, axis=1, keepdims=True))).astype(bf)
    grad_centroid = own_half(0.125 * dot(grad_scores, k[...]) / count[0]).astype(bf)
    gk[...] = (0.125 * dot(grad_scores, centroid[0], 0, 0)).astype(bf)
    gq[...] = dot(pair_columns(columns[0]), grad_centroid).astype(bf)


def attend_back(k, v, gm, rows, columns, prob, centroid, count):
    bf = jnp.bfloat16
    pair = pl.BlockSpec((SEQ, 128), lambda i: (0, i))
    wide = pl.BlockSpec((1, 2 * PAD, 128), lambda i: (i, 0, 0))
    out = pltpu.HBM((SEQ, D), bf)
    return pl.pallas_call(
        attend_back_kernel,
        grid=(HEADS // 2,),
        in_specs=[pair, pair, pair,
            pl.BlockSpec((1, 2, SEQ), lambda i: (i, 0, 0)),
            pl.BlockSpec((1, SEQ, 2), lambda i: (i, 0, 0)),
            pl.BlockSpec((1, 2 * PAD, SEQ), lambda i: (i, 0, 0)), wide, wide],
        out_specs=(pair, pair, pair),
        out_shape=(out, out, out),
        cost_estimate=pl.CostEstimate(flops=12 * 7 * 2 * PAD * SEQ * HEAD, bytes_accessed=16 << 20, transcendentals=0),
        compiler_params=pltpu.CompilerParams(vmem_limit_bytes=24 * 1024 * 1024),
        name="attend_back",
    )(k, v, gm, rows, columns, prob, centroid, count)


def shards(
    tokens,
    segment_ids,
    cluster_ids,
    cotangent,
    first_gain,
    first_shift,
    w_query,
    b_query,
    w_key,
    w_value,
    b_value,
    w_out,
    b_out,
    second_gain,
    second_shift,
    w_up,
    b_up,
    w_down,
    b_down,
):
    groups = high_groups()
    tops = 1 << sum(bits for _, bits in groups)
    bf = jnp.bfloat16
    part = D // (8 * tops)
    wide = D // (2 * tops)
    whole = [1 << bits for _, bits in reversed(groups)]

    attn = jnp.stack([w.astype(bf) for w in (w_query, w_key, w_value, w_out)])
    up, down = (w_up.astype(bf), w_down.T.astype(bf))
    unit_in, _ = moments(tokens.astype(jnp.float32))
    normed_in = (unit_in * first_gain + first_shift).astype(bf)
    id_rows = cluster_ids.reshape(HEADS // 2, 2, SEQ)
    id_columns = id_rows.transpose(0, 2, 1)
    seg = segment_ids.astype(jnp.float32)
    seg_row, seg_col = (seg[None, :], seg[:, None])
    cot_t = cotangent.T
    for group in groups:
        got = exchanged(attn, group)
        normed_in, id_columns, seg_col, *got = tied(normed_in, id_columns, seg_col, *got)
        attn = lined_up(attn, got, group, 1)
    attn = attn.reshape(4, tops, part, D)
    first, second = (attn[:2], attn[2:])
    first_got, second_got = (swapped(first, "dp", 1), swapped(second, "hid", 1))
    for group in groups[:-1]:
        up = lined_up(up, exchanged(up, group), group, 0)
        down = lined_up(down, exchanged(down, group), group, 0)
    up_got, down_got = (exchanged(up, groups[-1]), exchanged(down, groups[-1]))
    cot_t, first_got, second_got, *up_got = tied(cot_t, first_got, second_got, *up_got)
    first = joined(first, first_got, own_bit("dp", 0), 2)
    second = joined(second, second_got, own_bit("hid", 0), 2)
    first_got, second_got = (swapped(first, "hid", 1), swapped(second, "dp", 1))
    first_got, second_got, *down_got = tied(first_got, second_got, *down_got)
    half = tops // 2
    up = lined_up(up, up_got, groups[-1], 0).reshape(tops, wide, D)
    up_one, up_two = (up[:half], up[half:])
    up_one_got, up_two_got = (swapped(up_one, "dp", 1), swapped(up_two, "hid", 1))
    down = lined_up(down, down_got, groups[-1], 0).reshape(tops, wide, D)
    down_one, down_two = (down[:half], down[half:])
    down_one_got, down_two_got = (swapped(down_one, "dp", 1), swapped(down_two, "hid", 1))
    first = joined(first, first_got, own_bit("hid", 0), 3)
    second = joined(second, second_got, own_bit("dp", 0), 2)
    first_got, second_got = (swapped(first, "mp", 1), swapped(second, "mp", 1))
    first_got, second_got, up_one_got, up_two_got = tied(first_got, second_got, up_one_got, up_two_got)
    first = joined(first, first_got, own_bit("mp", 0), 4)
    second = joined(second, second_got, own_bit("mp", 0), 4)
    query_full, key_full = first.reshape(2, D, D)
    value_full, out_full = second.reshape(2, D, D)

    query = (matmul(normed_in, query_full) + b_query).astype(bf)
    up_one, up_two = (joined(up_one, up_one_got, own_bit("dp", 0), 1), jnp.stack([up_two, up_two_got]))
    up_one_got, up_two_got = (swapped(up_one, "hid", 1), swapped(up_two, "dp", 1))
    key_rows = matmul(normed_in, key_full).astype(bf)
    value_rows = (matmul(normed_in, value_full) + b_value).astype(bf)
    value_rows, down_one_got, down_two_got = tied(value_rows, down_one_got, down_two_got)
    down_one, down_two = (joined(down_one, down_one_got, own_bit("dp", 0), 1), jnp.stack([down_two, down_two_got]))
    down_one_got, down_two_got = (swapped(down_one, "hid", 1), swapped(down_two, "dp", 1))
    mixed, probability, centroid, counts = attend(
        query, key_rows, value_rows, id_rows, id_columns, seg_row, seg_col
    )
    mixed, down_one_got, down_two_got, up_one_got, up_two_got = tied(
        mixed, down_one_got, down_two_got, up_one_got, up_two_got
    )
    up_two = joined(up_two, up_two_got, own_bit("dp", 0), 2)
    ups = jnp.stack([jnp.concatenate([up_one, up_two[0]]), jnp.concatenate([up_one_got, up_two[1]])])
    ups = ups.reshape(2, D, D)
    ups_next = swapped(ups, "mp", 1)
    residual, x, x_t = middle(mixed, tokens, out_full, b_out, second_gain, second_shift)
    down_two = joined(down_two, down_two_got, own_bit("dp", 0), 2)
    down_mate = jnp.concatenate([down_one_got, down_two[1]]).reshape(1, D, D)
    down_across = swapped(down_mate, "mp", 1)
    down = jnp.concatenate([down_one, down_two[0]]).reshape(1, D, D)
    down_next = swapped(down, "mp", 1)
    me = lax.axis_index(("hid", "mp"))
    biases = lambda blocks: jnp.stack([lax.dynamic_slice_in_dim(b_up, block * D, D) for block in blocks])
    split = lambda piece: piece.reshape(tops, 2, wide, D)
    *sums, sent, own, far_bias = ff_blocks(
        x, cotangent, x_t, cot_t, (ups_next, down_across, ups, down_mate), (1, 0, 1, 0), biases((me ^ 3, me ^ 2))
    )
    got = swapped(sent, "mp", 1)
    up_far = added(own[0], got[0])
    down_far, down_sent = sum_halves([split(own[1]), split(got[1])], "dp", 0, 1)
    *sums, up_far, down_sent = tied(*sums, up_far, down_sent)
    up_far_got = swapped(up_far, "hid", 1)
    down_far_got = swapped(down_sent, "dp", 1)
    branch, grad_mid, sent, own, near_bias = ff_blocks(
        x, cotangent, x_t, cot_t, (ups_next, down_next, ups, down), (0, 0, 0, 0), biases((me ^ 1, me)), *sums
    )
    branch, grad_mid, sent, up_far_got, down_far_got = tied(branch, grad_mid, sent, up_far_got, down_far_got)
    near_got = swapped(sent, "mp", 1)
    bias_up = jnp.zeros((4, D), jnp.float32)
    for block, bias in ((me ^ 3, far_bias[:1]), (me ^ 2, far_bias[1:]), (me ^ 1, near_bias[:1]), (me, near_bias[1:])):
        bias_up = lax.dynamic_update_slice(bias_up, bias, (block, 0))
    down_far = added(down_far, down_far_got)
    branch, grad_mid, down_far = tied(branch, grad_mid, down_far)
    down_got = swapped(down_far, "hid", 1)

    output, grad_resid, grad_mixed, out_grad, turn_lines = turn(
        branch, grad_mid, residual, cotangent, mixed, out_full, b_down, second_gain
    )
    grad_mixed, near_got = tied(grad_mixed, near_got)
    down_near, down_sent = sum_halves([split(own[1]), split(near_got[1])], "dp", 0, 1)
    up_near, up_sent = sum_halves([split(own[0]), split(near_got[0]), split(up_far_got)], "dp", 0, 1)
    grad_mixed, down_sent, up_sent = tied(grad_mixed, down_sent, up_sent)
    down_near_got = swapped(down_sent, "dp", 1)
    up_got = swapped(up_sent, "dp", 1)

    grad_query, grad_key, grad_value = attend_back(
        key_rows, value_rows, grad_mixed, id_rows, id_columns, probability, centroid, counts
    )
    grad_value, down_got, down_near_got = tied(grad_value, down_got, down_near_got)
    down_sum = rounded_sum([down_near, down_near_got, down_got]).reshape(*whole, wide, D)
    down_parts = dealt(down_sum, groups[-1], 0)

    query_grad = matmul_tn(normed_in, grad_query).astype(bf)
    key_grad = matmul_tn(normed_in, grad_key).astype(bf)
    value_grad = matmul_tn(normed_in, grad_value).astype(bf)
    both = jnp.stack([query_grad, key_grad, value_grad, out_grad]).reshape(4, tops, 2, 2, 2, part, D)
    both, sent = halves(both, "mp", 0, 4)
    got = swapped(sent, "mp", 1)
    tokens_grad, last_lines = last(
        grad_query, grad_key, grad_value, query_full, key_full, value_full, tokens, grad_resid, first_gain
    )
    small = jnp.concatenate([last_lines[:4], turn_lines[:4], bias_up])
    small, up_got, *down_parts = tied(small, up_got, *down_parts)
    up_parts = dealt(added(up_near, up_got).reshape(*whole, wide, D), groups[-1], 0)
    small = small + swapped(small, "mp", 1)
    both = added(both, got)
    one, one_sent = halves(both[:2], "dp", 0, 2)
    two, two_sent = halves(both[2:], "hid", 0, 3)
    got, two_got = (swapped(packed(one_sent, small), "dp", 1), swapped(two_sent, "hid", 1))
    got, two_got, *up_parts = tied(got, two_got, *up_parts)
    one_got, small_got = unpacked(got, one_sent)
    small = small + small_got
    one, one_sent = halves(added(one, one_got), "hid", 0, 2)
    two, two_sent = halves(added(two, two_got), "dp", 0, 2)
    got, two_got = (swapped(packed(one_sent, small), "hid", 1), swapped(two_sent, "dp", 1))
    one_got, small_got = unpacked(got, one_sent)
    small = small + small_got
    both = jnp.stack([added(one, one_got), added(two, two_got)]).reshape(4, *whole, part, D)
    for group in reversed(groups):
        shift, bits = group
        mine = (lax.axis_index("dp") >> shift) & ((1 << bits) - 1)
        take = lambda k: lax.dynamic_index_in_dim(both, k, 1, keepdims=False)
        got = [swapped(packed(take(mine ^ d), small), "dp", d << shift) for d in range(1, 1 << bits)]
        pieces = [unpacked(g, take(mine)) for g in got]
        sums = summed([take(mine)] + [piece for piece, _ in pieces])
        small = summed([small] + [piece for _, piece in pieces])
        both = sums.astype(bf)
    for group in reversed(groups[:-1]):
        up_parts = dealt(rounded_sum(up_parts), group, 0)
        down_parts = dealt(rounded_sum(down_parts), group, 0)
    up_grad, down_grad = (summed(up_parts), summed(down_parts).T)
    query_sum, key_sum, value_sum, out_sum = sums
    return (
        output,
        tokens_grad,
        small[0],
        small[1],
        query_sum,
        small[2],
        key_sum,
        value_sum,
        small[3],
        out_sum,
        small[4],
        small[5],
        small[6],
        up_grad,
        small[8:].reshape(-1),
        down_grad,
        small[7],
    )


def solution(mesh):
    return jax.shard_map(
        shards,
        mesh=mesh,
        in_specs=(
            P(("dp", "hid", "mp"), None),
            P(("dp", "hid", "mp")),
            P(None, ("dp", "hid", "mp")),
            P(("dp", "hid", "mp"), None),
            P(),
            P(),
            P(("dp", "hid", "mp"), None),
            P(),
            P(("dp", "hid", "mp"), None),
            P(("dp", "hid", "mp"), None),
            P(),
            P(("dp", "hid", "mp"), None),
            P(),
            P(),
            P(),
            P("dp", ("hid", "mp")),
            P(),
            P(("hid", "mp"), "dp"),
            P(),
        ),
        out_specs=(
            P(("dp", "hid", "mp"), None),
            P(("dp", "hid", "mp"), None),
            P(),
            P(),
            P(("dp", "hid", "mp"), None),
            P(),
            P(("dp", "hid", "mp"), None),
            P(("dp", "hid", "mp"), None),
            P(),
            P(("dp", "hid", "mp"), None),
            P(),
            P(),
            P(),
            P("dp", ("hid", "mp")),
            P(),
            P(("hid", "mp"), "dp"),
            P(),
        ),
        check_vma=False,
    )
```

```python
import functools

import jax
import jax.numpy as jnp
from jax import lax
from jax.experimental import pallas as pl
from jax.experimental.pallas import tpu as pltpu
from jax.sharding import PartitionSpec as P

D = 768
HEADS = 12
HEAD = 64
CLUSTERS = 100
SEQ = 1024
PAD = 128


def matmul(left, right):
    return jnp.dot(left, right, preferred_element_type=jnp.float32)


def matmul_nt(left, right):
    return lax.dot_general(left, right, (((1,), (1,)), ((), ())), preferred_element_type=jnp.float32)


def matmul_tn(left, right):
    return lax.dot_general(left, right, (((0,), (0,)), ((), ())), preferred_element_type=jnp.float32)


def swapped(array, axis, mask):
    count = lax.axis_size(axis)
    return lax.ppermute(array, axis, [(i, i ^ mask) for i in range(count)])


def own_bit(axis, bit):
    return (lax.axis_index(axis) >> bit) & 1


def joined(own, other, mine, place):
    own, other = (jnp.expand_dims(own, place), jnp.expand_dims(other, place))
    shape = own.shape[:place] + (2,) + own.shape[place + 1 :]
    return jnp.where(lax.broadcasted_iota(jnp.int32, shape, place) == mine, own, other)


def halves(array, axis, bit, place):
    mine = own_bit(axis, bit)
    take = lambda k: lax.dynamic_index_in_dim(array, k, place, keepdims=False)
    return (take(mine), take(1 - mine))


def high_groups():
    count = lax.axis_size("dp").bit_length() - 1
    return [(b, min(2, count - b)) for b in range(1, count, 2)]


def exchanged(piece, group):
    shift, bits = group
    return [swapped(piece, "dp", d << shift) for d in range(1, 1 << bits)]


def lined_up(own, others, group, place):
    shift, bits = group
    mine = (lax.axis_index("dp") >> shift) & ((1 << bits) - 1)
    pieces = [jnp.expand_dims(p, place) for p in [own, *others]]
    shape = pieces[0].shape[:place] + (1 << bits,) + pieces[0].shape[place + 1 :]
    apart = lax.broadcasted_iota(jnp.int32, shape, place) ^ mine
    out = jnp.broadcast_to(pieces[-1], shape)
    for d in reversed(range(len(pieces) - 1)):
        out = jnp.where(apart == d, pieces[d], out)
    return out


def dealt(array, group, place):
    shift, bits = group
    mine = (lax.axis_index("dp") >> shift) & ((1 << bits) - 1)
    take = lambda k: lax.dynamic_index_in_dim(array, k, place, keepdims=False)
    return [take(mine)] + [swapped(take(mine ^ d), "dp", d << shift) for d in range(1, 1 << bits)]


def summed(pieces):
    return sum(p.astype(jnp.float32) for p in pieces)


def moments(values):
    middle = jnp.mean(values, axis=-1, keepdims=True)
    centered = values - middle
    spread = jnp.mean(centered * centered, axis=-1, keepdims=True)
    return (centered * lax.rsqrt(spread + 1e-05), lax.rsqrt(spread + 1e-05))


def norm_pull(grad, gain, unit, scale):
    scaled = grad * gain
    first = jnp.mean(scaled, axis=-1, keepdims=True)
    second = jnp.mean(scaled * unit, axis=-1, keepdims=True)
    return scale * (scaled - first - unit * second)


def gate_and_slope(v):
    size = jnp.abs(v)
    bell = jnp.exp(-0.5 * v * v)
    t = 1.0 / (1.0 + 0.23164189 * size)
    series = 0.7107068705 + t * (-0.7265760135 + t * 0.5307027145)
    tail = t * (0.127414796 + t * (-0.142248368 + t * series)) * bell
    phi = jnp.where(v < 0, tail, 1.0 - tail)
    return (v * phi, phi + v * (0.3989422804014327 * bell))


def ff_kernel(first, rows, places, *refs):
    x_in, cot_in, xt_in, cott_in, *weights, bu, branch_in = refs[:10]
    refs = refs[10:]
    if not first:
        mid_in, b_down = refs[:2]
        refs = refs[2:]
    branch_out, mid_out, *grads = refs[:6]
    dbu, x, cot, xt, cott, wu, wd, branch, mid, branch_old, mid_old, dw, sems = refs[6:]
    nt = (((1,), (1,)), ((), ()))
    parts = [pl.ds(r * rows, rows) for r in range(x.shape[0] // rows)]
    used = [0]

    def started(source, target):
        used[0] += 1
        made = pltpu.make_async_copy(source, target, sems.at[used[0] - 1])
        made.start()
        return made

    def finish(made):
        for one in made:
            one.wait()

    def fetch_weight(k, target):
        ref, place = (weights[k], places[k])
        return started(ref.at[place], target.at[k // 2])

    early = [fetch_weight(0, wu), started(x_in, x), fetch_weight(1, wd), started(cot_in, cot)]
    finish(early)
    late = [started(cott_in, cott), started(xt_in, xt), fetch_weight(2, wu), fetch_weight(3, wd)]
    late.append(started(branch_in, branch_old))
    if not first:
        late.append(started(mid_in, mid_old))
    outs = []
    for block in (0, 1):
        hs, gs = ([], [])
        total = jnp.zeros((1, dbu.shape[1]), jnp.float32)
        for at in parts:
            pre = matmul(x[at, :], wu[block]) + bu[block : block + 1, :]
            grad_hidden = matmul(cot[at, :], wd[block])
            h, slope = gate_and_slope(pre)
            h = h.astype(jnp.bfloat16)
            g = (grad_hidden * slope).astype(jnp.bfloat16)
            total += jnp.sum(g.astype(jnp.float32), axis=0, keepdims=True)
            forth = lax.dot_general(h, wd[block], nt, preferred_element_type=jnp.float32)
            back = lax.dot_general(g, wu[block], nt, preferred_element_type=jnp.float32)
            if block:
                forth += branch[at, :] + branch_old[at, :]
                back += mid[at, :]
                if not first:
                    forth += b_down[...]
                    back += mid_old[at, :]
            if block and not first:
                x[at, :] = forth.astype(jnp.bfloat16)
            else:
                branch[at, :] = forth
            mid[at, :] = back
            hs.append(h)
            gs.append(g)
        dbu[block : block + 1, :] = total
        if block == 0:
            finish(late)
        else:
            outs += [started(branch if first else x, branch_out), started(mid, mid_out)]
        dw[block, 1] = matmul(cott[...], jnp.concatenate(hs, axis=0)).astype(jnp.bfloat16)
        outs.append(started(dw.at[block, 1], grads[2 * block + 1]))
        dw[block, 0] = matmul(xt[...], jnp.concatenate(gs, axis=0)).astype(jnp.bfloat16)
        outs.append(started(dw.at[block, 0], grads[2 * block]))
    finish(outs)


def ff_blocks(x, cot, xt, cott, weights, places, bu, residual, *sums):
    f32, bf = (jnp.float32, jnp.bfloat16)
    count, wide = (x.shape[0], bu.shape[1])
    spec = pl.BlockSpec(memory_space=pltpu.VMEM)
    far = pl.BlockSpec(memory_space=pl.ANY)
    return pl.pallas_call(
        functools.partial(ff_kernel, not sums, 256, places),
        out_shape=(
            pltpu.HBM((count, D), bf if sums else f32),
            pltpu.HBM((count, D), f32),
            pltpu.HBM((D, wide), bf),
            pltpu.HBM((D, wide), bf),
            pltpu.HBM((D, wide), bf),
            pltpu.HBM((D, wide), bf),
            jax.ShapeDtypeStruct((2, wide), f32),
        ),
        in_specs=[far] * 8 + [spec, far] + [far, spec][: len(sums)],
        out_specs=(far,) * 6 + (spec,),
        scratch_shapes=[
            pltpu.VMEM((count, D), bf),
            pltpu.VMEM((count, D), bf),
            pltpu.VMEM((D, count), bf),
            pltpu.VMEM((D, count), bf),
            pltpu.VMEM((2, D, wide), bf),
            pltpu.VMEM((2, D, wide), bf),
            pltpu.VMEM((count, D), f32),
            pltpu.VMEM((count, D), f32),
            pltpu.VMEM((count, D), f32),
            pltpu.VMEM((count, D), f32),
            pltpu.VMEM((2, 2, D, wide), bf),
            pltpu.SemaphoreType.DMA((16,)),
        ],
        compiler_params=pltpu.CompilerParams(vmem_limit_bytes=60 * 1024 * 1024),
        cost_estimate=pl.CostEstimate(
            flops=24 * count * D * wide, bytes_accessed=8 * D * wide, transcendentals=4 * count * wide
        ),
        name="ff_blocks",
    )(x, cot, xt, cott, *weights, bu, residual, *sums)


STEP = 256
ROWS = pl.BlockSpec((STEP, D), lambda i: (i, 0))
WHOLE = pl.BlockSpec((D, D), lambda i: (0, 0))
LINE = pl.BlockSpec((1, D), lambda i: (0, 0))
LINES = pl.BlockSpec((8, D), lambda i: (0, 0))


def by_rows(kernel, name, in_specs, out_specs, out_shape, scratch, flops, moved):
    return pl.pallas_call(
        kernel,
        grid=(SEQ // STEP,),
        in_specs=in_specs,
        out_specs=out_specs,
        out_shape=out_shape,
        scratch_shapes=scratch,
        compiler_params=pltpu.CompilerParams(vmem_limit_bytes=60 * 1024 * 1024),
        cost_estimate=pl.CostEstimate(flops=flops, bytes_accessed=moved, transcendentals=SEQ),
        name=name,
    )


def middle_kernel(mixed, tokens, out_full, b_out, gain, shift, residual, x, x_t):
    value = tokens[...].astype(jnp.float32) + (matmul(mixed[...], out_full[...]) + b_out[...])
    residual[...] = value
    unit, _ = moments(value)
    normed = (unit * gain[...] + shift[...]).astype(jnp.bfloat16)
    x[...] = normed
    x_t[...] = normed.T


def middle(mixed, tokens, out_full, b_out, gain, shift):
    f32, bf = (jnp.float32, jnp.bfloat16)
    return by_rows(
        middle_kernel,
        "middle",
        [ROWS, ROWS, WHOLE, LINE, LINE, LINE],
        (ROWS, ROWS, pl.BlockSpec((D, STEP), lambda i: (0, i))),
        (pltpu.HBM((SEQ, D), f32), pltpu.HBM((SEQ, D), bf), pltpu.HBM((D, SEQ), bf)),
        [],
        SEQ,
        SEQ,
    )(mixed, tokens, out_full, b_out[None], gain[None], shift[None])


def add_lines(ref, lines):
    @pl.when(pl.program_id(0) == 0)
    def _():
        ref[...] = jnp.zeros_like(ref)

    sums = [jnp.sum(line.astype(jnp.float32), axis=0, keepdims=True) for line in lines]
    ref[: len(lines), :] += jnp.concatenate(sums, axis=0)


def turn_kernel(grad_mid, residual, cot, mixed, out_full, gain, grad_resid, grad_mixed, out_grad, lines, held):
    value = residual[...]
    grad = grad_mid[...]
    unit, scale = moments(value)
    pulled = cot[...].astype(jnp.float32) + norm_pull(grad, gain[...], unit, scale)
    grad_resid[...] = pulled
    low = pulled.astype(jnp.bfloat16)
    grad_mixed[...] = matmul_nt(low, out_full[...]).astype(jnp.bfloat16)
    add_lines(lines, [low, grad * unit, grad, cot[...]])

    @pl.when(pl.program_id(0) == 0)
    def _():
        held[...] = jnp.zeros_like(held)

    held[...] += matmul_tn(mixed[...], low)

    @pl.when(pl.program_id(0) == pl.num_programs(0) - 1)
    def _():
        out_grad[...] = held[...].astype(jnp.bfloat16)


def turn(grad_mid, residual, cot, mixed, out_full, gain):
    f32, bf = (jnp.float32, jnp.bfloat16)
    low = jax.ShapeDtypeStruct((SEQ, D), bf)
    return by_rows(
        turn_kernel,
        "turn",
        [ROWS, ROWS, ROWS, ROWS, WHOLE, LINE],
        (ROWS, ROWS, WHOLE, LINES),
        (pltpu.HBM((SEQ, D), f32), low, pltpu.HBM((D, D), bf), jax.ShapeDtypeStruct((8, D), f32)),
        [pltpu.VMEM((D, D), f32)],
        SEQ,
        SEQ,
    )(grad_mid, residual, cot, mixed, out_full, gain[None])


def last_kernel(gq, gk, gv, wq, wk, wv, tokens, grad_resid, gain, tokens_grad, lines):
    grad = matmul_nt(gq[...], wq[...]) + matmul_nt(gk[...], wk[...]) + matmul_nt(gv[...], wv[...])
    unit, scale = moments(tokens[...].astype(jnp.float32))
    tokens_grad[...] = (grad_resid[...] + norm_pull(grad, gain[...], unit, scale)).astype(jnp.bfloat16)
    add_lines(lines, [grad * unit, grad, gq[...], gv[...]])


def last(gq, gk, gv, wq, wk, wv, tokens, grad_resid, gain):
    return by_rows(
        last_kernel,
        "last",
        [ROWS, ROWS, ROWS, WHOLE, WHOLE, WHOLE, ROWS, ROWS, LINE],
        (ROWS, LINES),
        (jax.ShapeDtypeStruct((SEQ, D), jnp.bfloat16), jax.ShapeDtypeStruct((8, D), jnp.float32)),
        [],
        SEQ,
        SEQ,
    )(gq, gk, gv, wq, wk, wv, tokens, grad_resid, gain[None])


def tied(*arrays):
    return lax.optimization_barrier(arrays)


def packed(sent, small):
    high = small.astype(jnp.bfloat16)
    low = (small - high.astype(jnp.float32)).astype(jnp.bfloat16)
    return jnp.concatenate([sent.reshape(-1, D), high, low])


def unpacked(got, like):
    rows = like.size // D
    high, low = jnp.split(got[rows:].astype(jnp.float32), 2)
    return (got[:rows].reshape(like.shape), high + low)


def added(own, got):
    return (own.astype(jnp.float32) + got.astype(jnp.float32)).astype(jnp.bfloat16)


def dot(a, b, ca=1, cb=0):
    return lax.dot_general(a, b, (((ca,), (cb,)), ((), ())), preferred_element_type=jnp.float32)


def rounded_sum(pieces):
    return summed(pieces).astype(jnp.bfloat16)


def sum_halves(pieces, axis, bit, place):
    both = [halves(piece, axis, bit, place) for piece in pieces]
    return (rounded_sum([kept for kept, _ in both]), rounded_sum([sent for _, sent in both]))


def own_half(wide):
    rows = lax.broadcasted_iota(jnp.int32, wide.shape, 0) // PAD
    columns = lax.broadcasted_iota(jnp.int32, wide.shape, 1) // HEAD
    return jnp.where(rows == columns, wide, 0.0)


def pair_rows(ids):
    at = lax.broadcasted_iota(jnp.int32, (PAD, SEQ), 0)
    return jnp.concatenate([jnp.where(ids[k : k + 1, :] == at, 1.0, 0.0) for k in (0, 1)], axis=0).astype(jnp.bfloat16)


def pair_columns(ids):
    at = lax.broadcasted_iota(jnp.int32, (SEQ, PAD), 1)
    return jnp.concatenate([jnp.where(ids[:, k : k + 1] == at, 1.0, 0.0) for k in (0, 1)], axis=1).astype(jnp.bfloat16)


def attend_kernel(q, k, v, rows, columns, seg_row, seg_col, mixed, prob, centroid, count):
    bf = jnp.bfloat16
    hot = pair_rows(rows[0])
    lanes = lax.broadcasted_iota(jnp.int32, (SEQ, PAD), 1)
    marks = jnp.where(lanes == 0, seg_col[...], jnp.where(lanes == 1, 1.0, 0.0)).astype(bf)
    sums = dot(hot, jnp.concatenate([q[...], marks], axis=1))
    owner, counts = (sums[:, 128:129], sums[:, 129:130])
    counts = jnp.maximum(counts, 1.0)
    middle = own_half(sums[:, :128] / counts).astype(bf)
    scores = 0.125 * dot(middle, k[...], 1, 1)
    allowed = jnp.abs(owner - counts * seg_row[...]) < 0.5
    masked = jnp.where(allowed, scores, -1e30)
    highest = jnp.max(masked, axis=1, keepdims=True)
    exponent = jnp.where(allowed, jnp.exp(masked - highest), 0.0)
    total = jnp.sum(exponent, axis=1, keepdims=True)
    p = exponent * (1.0 / jnp.maximum(total, 1e-30))
    context = own_half(dot(p.astype(bf), v[...])).astype(bf)
    mixed[...] = dot(pair_columns(columns[0]), context).astype(bf)
    prob[0] = p
    centroid[0] = middle
    count[0] = jnp.broadcast_to(counts, (2 * PAD, 128))


def attend(q, k, v, rows, columns, seg_row, seg_col):
    bf = jnp.bfloat16
    pair = pl.BlockSpec((SEQ, 128), lambda i: (0, i))
    return pl.pallas_call(
        attend_kernel,
        grid=(HEADS // 2,),
        in_specs=[pair, pair, pair,
            pl.BlockSpec((1, 2, SEQ), lambda i: (i, 0, 0)),
            pl.BlockSpec((1, SEQ, 2), lambda i: (i, 0, 0)),
            pl.BlockSpec((1, SEQ), lambda i: (0, 0)),
            pl.BlockSpec((SEQ, 1), lambda i: (0, 0))],
        out_specs=(pair, pl.BlockSpec((1, 2 * PAD, SEQ), lambda i: (i, 0, 0)), pl.BlockSpec((1, 2 * PAD, 128), lambda i: (i, 0, 0)), pl.BlockSpec((1, 2 * PAD, 128), lambda i: (i, 0, 0))),
        out_shape=(pltpu.HBM((SEQ, D), bf), pltpu.HBM((HEADS // 2, 2 * PAD, SEQ), jnp.float32), pltpu.HBM((HEADS // 2, 2 * PAD, 128), bf), pltpu.HBM((HEADS // 2, 2 * PAD, 128), jnp.float32)),
        cost_estimate=pl.CostEstimate(flops=12 * 5 * 2 * PAD * SEQ * HEAD, bytes_accessed=14 << 20, transcendentals=HEADS * PAD * SEQ),
        compiler_params=pltpu.CompilerParams(vmem_limit_bytes=24 * 1024 * 1024),
        name="attend",
    )(q, k, v, rows, columns, seg_row, seg_col)


def attend_back_kernel(k, v, gm, rows, columns, prob, centroid, count, gq, gk, gv):
    bf = jnp.bfloat16
    hot = pair_rows(rows[0])
    p = prob[0]
    grad_context = own_half(dot(hot, gm[...])).astype(bf)
    gv[...] = dot(p.astype(bf), grad_context, 0, 0).astype(bf)
    grad_prob = dot(grad_context, v[...], 1, 1)
    grad_scores = (p * (grad_prob - jnp.sum(p * grad_prob, axis=1, keepdims=True))).astype(bf)
    grad_centroid = own_half(0.125 * dot(grad_scores, k[...]) / count[0]).astype(bf)
    gk[...] = (0.125 * dot(grad_scores, centroid[0], 0, 0)).astype(bf)
    gq[...] = dot(pair_columns(columns[0]), grad_centroid).astype(bf)


def attend_back(k, v, gm, rows, columns, prob, centroid, count):
    bf = jnp.bfloat16
    pair = pl.BlockSpec((SEQ, 128), lambda i: (0, i))
    wide = pl.BlockSpec((1, 2 * PAD, 128), lambda i: (i, 0, 0))
    out = pltpu.HBM((SEQ, D), bf)
    return pl.pallas_call(
        attend_back_kernel,
        grid=(HEADS // 2,),
        in_specs=[pair, pair, pair,
            pl.BlockSpec((1, 2, SEQ), lambda i: (i, 0, 0)),
            pl.BlockSpec((1, SEQ, 2), lambda i: (i, 0, 0)),
            pl.BlockSpec((1, 2 * PAD, SEQ), lambda i: (i, 0, 0)), wide, wide],
        out_specs=(pair, pair, pair),
        out_shape=(out, out, out),
        cost_estimate=pl.CostEstimate(flops=12 * 7 * 2 * PAD * SEQ * HEAD, bytes_accessed=16 << 20, transcendentals=0),
        compiler_params=pltpu.CompilerParams(vmem_limit_bytes=24 * 1024 * 1024),
        name="attend_back",
    )(k, v, gm, rows, columns, prob, centroid, count)


def shards(
    tokens,
    segment_ids,
    cluster_ids,
    cotangent,
    first_gain,
    first_shift,
    w_query,
    b_query,
    w_key,
    w_value,
    b_value,
    w_out,
    b_out,
    second_gain,
    second_shift,
    w_up,
    b_up,
    w_down,
    b_down,
):
    groups = high_groups()
    tops = 1 << sum(bits for _, bits in groups)
    bf = jnp.bfloat16
    part = D // (8 * tops)
    wide = D // (2 * tops)
    whole = [1 << bits for _, bits in reversed(groups)]

    attn = jnp.stack([w.astype(bf) for w in (w_query, w_key, w_value, w_out)])
    up, down = (w_up.astype(bf), w_down.T.astype(bf))
    unit_in, _ = moments(tokens.astype(jnp.float32))
    normed_in = (unit_in * first_gain + first_shift).astype(bf)
    id_rows = cluster_ids.reshape(HEADS // 2, 2, SEQ)
    id_columns = id_rows.transpose(0, 2, 1)
    seg = segment_ids.astype(jnp.float32)
    seg_row, seg_col = (seg[None, :], seg[:, None])
    cot_t = cotangent.T
    for group in groups:
        got = exchanged(attn, group)
        normed_in, id_columns, seg_col, *got = tied(normed_in, id_columns, seg_col, *got)
        attn = lined_up(attn, got, group, 1)
    attn = attn.reshape(4, tops, part, D)
    first, second = (attn[:2], attn[2:])
    first_got, second_got = (swapped(first, "dp", 1), swapped(second, "hid", 1))
    for group in groups[:-1]:
        up = lined_up(up, exchanged(up, group), group, 0)
        down = lined_up(down, exchanged(down, group), group, 0)
    up_got, down_got = (exchanged(up, groups[-1]), exchanged(down, groups[-1]))
    cot_t, first_got, second_got, *up_got = tied(cot_t, first_got, second_got, *up_got)
    first = joined(first, first_got, own_bit("dp", 0), 2)
    second = joined(second, second_got, own_bit("hid", 0), 2)
    first_got, second_got = (swapped(first, "hid", 1), swapped(second, "dp", 1))
    first_got, second_got, *down_got = tied(first_got, second_got, *down_got)
    half = tops // 2
    up = lined_up(up, up_got, groups[-1], 0).reshape(tops, wide, D)
    up_one, up_two = (up[:half], up[half:])
    up_one_got, up_two_got = (swapped(up_one, "dp", 1), swapped(up_two, "hid", 1))
    down = lined_up(down, down_got, groups[-1], 0).reshape(tops, wide, D)
    down_one, down_two = (down[:half], down[half:])
    down_one_got, down_two_got = (swapped(down_one, "dp", 1), swapped(down_two, "hid", 1))
    first = joined(first, first_got, own_bit("hid", 0), 3)
    second = joined(second, second_got, own_bit("dp", 0), 2)
    first_got, second_got = (swapped(first, "mp", 1), swapped(second, "mp", 1))
    first_got, second_got, up_one_got, up_two_got = tied(first_got, second_got, up_one_got, up_two_got)
    first = joined(first, first_got, own_bit("mp", 0), 4)
    second = joined(second, second_got, own_bit("mp", 0), 4)
    query_full, key_full = first.reshape(2, D, D)
    value_full, out_full = second.reshape(2, D, D)

    query = (matmul(normed_in, query_full) + b_query).astype(bf)
    up_one, up_two = (joined(up_one, up_one_got, own_bit("dp", 0), 1), jnp.stack([up_two, up_two_got]))
    up_one_got, up_two_got = (swapped(up_one, "hid", 1), swapped(up_two, "dp", 1))
    key_rows = matmul(normed_in, key_full).astype(bf)
    value_rows = (matmul(normed_in, value_full) + b_value).astype(bf)
    value_rows, down_one_got, down_two_got = tied(value_rows, down_one_got, down_two_got)
    down_one, down_two = (joined(down_one, down_one_got, own_bit("dp", 0), 1), jnp.stack([down_two, down_two_got]))
    down_one_got, down_two_got = (swapped(down_one, "hid", 1), swapped(down_two, "dp", 1))
    mixed, probability, centroid, counts = attend(
        query, key_rows, value_rows, id_rows, id_columns, seg_row, seg_col
    )
    mixed, up_one_got, up_two_got = tied(mixed, up_one_got, up_two_got)
    up_two = joined(up_two, up_two_got, own_bit("dp", 0), 2)
    ups = jnp.stack([jnp.concatenate([up_one, up_two[0]]), jnp.concatenate([up_one_got, up_two[1]])])
    ups = ups.reshape(2, D, D)
    ups_next = swapped(ups, "mp", 1)
    residual, x, x_t = middle(mixed, tokens, out_full, b_out, second_gain, second_shift)
    x, x_t, down_one_got, down_two_got = tied(x, x_t, down_one_got, down_two_got)
    down_two = joined(down_two, down_two_got, own_bit("dp", 0), 2)
    down_mate = jnp.concatenate([down_one_got, down_two[1]]).reshape(1, D, D)
    down_across = swapped(down_mate, "mp", 1)
    down = jnp.concatenate([down_one, down_two[0]]).reshape(1, D, D)
    down_next = swapped(down, "mp", 1)
    me = lax.axis_index(("hid", "mp"))
    biases = lambda blocks: jnp.stack([lax.dynamic_slice_in_dim(b_up, block * D, D) for block in blocks])
    split = lambda piece: piece.reshape(tops, 2, wide, D)
    branch, grad_mid, up_send, down_send, up_own, down_own, far_bias = ff_blocks(
        x, cotangent, x_t, cot_t, (ups_next, down_across, ups, down_mate), (1, 0, 1, 0), biases((me ^ 3, me ^ 2)), residual
    )
    up_far = added(up_own, swapped(up_send, "mp", 1))
    down_far, down_sent = sum_halves([split(down_own), split(swapped(down_send, "mp", 1))], "dp", 0, 1)
    branch, grad_mid, up_far, down_sent = tied(branch, grad_mid, up_far, down_sent)
    up_far_got = swapped(up_far, "hid", 1)
    down_far_got = swapped(down_sent, "dp", 1)
    output, grad_mid, up_send, down_send, up_own, down_own, near_bias = ff_blocks(
        x, cotangent, x_t, cot_t, (ups_next, down_next, ups, down), (0, 0, 0, 0), biases((me ^ 1, me)), branch, grad_mid, b_down[None]
    )
    grad_mid, up_send, down_send, up_far_got, down_far_got = tied(grad_mid, up_send, down_send, up_far_got, down_far_got)
    up_near_got, down_near_got = (swapped(up_send, "mp", 1), swapped(down_send, "mp", 1))
    bias_up = jnp.zeros((4, D), jnp.float32)
    for block, bias in ((me ^ 3, far_bias[:1]), (me ^ 2, far_bias[1:]), (me ^ 1, near_bias[:1]), (me, near_bias[1:])):
        bias_up = lax.dynamic_update_slice(bias_up, bias, (block, 0))
    down_far = added(down_far, down_far_got)
    grad_mid, down_far = tied(grad_mid, down_far)
    down_got = swapped(down_far, "hid", 1)

    grad_resid, grad_mixed, out_grad, turn_lines = turn(grad_mid, residual, cotangent, mixed, out_full, second_gain)
    grad_mixed, up_near_got, down_near_got = tied(grad_mixed, up_near_got, down_near_got)
    down_near, down_sent = sum_halves([split(down_own), split(down_near_got)], "dp", 0, 1)
    up_near, up_sent = sum_halves([split(up_own), split(up_near_got), split(up_far_got)], "dp", 0, 1)
    grad_mixed, down_sent, up_sent = tied(grad_mixed, down_sent, up_sent)
    down_near_got = swapped(down_sent, "dp", 1)
    up_got = swapped(up_sent, "dp", 1)

    grad_query, grad_key, grad_value = attend_back(
        key_rows, value_rows, grad_mixed, id_rows, id_columns, probability, centroid, counts
    )
    grad_value, down_got, down_near_got = tied(grad_value, down_got, down_near_got)
    down_sum = rounded_sum([down_near, down_near_got, down_got]).reshape(*whole, wide, D)

    query_grad = matmul_tn(normed_in, grad_query).astype(bf)
    key_grad = matmul_tn(normed_in, grad_key).astype(bf)
    value_grad = matmul_tn(normed_in, grad_value).astype(bf)
    both = jnp.stack([query_grad, key_grad, value_grad, out_grad]).reshape(4, tops, 2, 2, 2, part, D)
    both, sent = halves(both, "mp", 0, 4)
    got = swapped(sent, "mp", 1)
    got, up_got = tied(got, up_got)
    ff_parts = dealt(jnp.stack([added(up_near, up_got).reshape(*whole, wide, D), down_sum]), groups[-1], 1)
    both = added(both, got)
    one, one_sent = halves(both[:2], "dp", 0, 2)
    two, two_sent = halves(both[2:], "hid", 0, 3)
    grad_resid, one_sent, two_sent, ff_parts[0] = tied(grad_resid, one_sent, two_sent, ff_parts[0])
    one_got, two_got = (swapped(one_sent, "dp", 1), swapped(two_sent, "hid", 1))
    tokens_grad, last_lines = last(
        grad_query, grad_key, grad_value, query_full, key_full, value_full, tokens, grad_resid, first_gain
    )
    small = jnp.concatenate([last_lines[:4], turn_lines[:4], bias_up])
    small, one_got, two_got, *ff_parts = tied(small, one_got, two_got, *ff_parts)
    small = small + swapped(small, "mp", 1)
    small = small + swapped(small, "dp", 1)
    one, one_sent = halves(added(one, one_got), "hid", 0, 2)
    two, two_sent = halves(added(two, two_got), "dp", 0, 2)
    got, two_got = (swapped(packed(one_sent, small), "hid", 1), swapped(two_sent, "dp", 1))
    one_got, small_got = unpacked(got, one_sent)
    small = small + small_got
    both = jnp.stack([added(one, one_got), added(two, two_got)]).reshape(4, *whole, part, D)
    for group in reversed(groups):
        shift, bits = group
        mine = (lax.axis_index("dp") >> shift) & ((1 << bits) - 1)
        take = lambda k: lax.dynamic_index_in_dim(both, k, 1, keepdims=False)
        got = [swapped(packed(take(mine ^ d), small), "dp", d << shift) for d in range(1, 1 << bits)]
        pieces = [unpacked(g, take(mine)) for g in got]
        sums = summed([take(mine)] + [piece for piece, _ in pieces])
        small = summed([small] + [piece for _, piece in pieces])
        both = sums.astype(bf)
    for group in reversed(groups[:-1]):
        ff_parts = dealt(rounded_sum(ff_parts), group, 1)
    up_grad, down_grad = summed(ff_parts)
    down_grad = down_grad.T
    query_sum, key_sum, value_sum, out_sum = sums
    return (
        output,
        tokens_grad,
        small[0],
        small[1],
        query_sum,
        small[2],
        key_sum,
        value_sum,
        small[3],
        out_sum,
        small[4],
        small[5],
        small[6],
        up_grad,
        small[8:].reshape(-1),
        down_grad,
        small[7],
    )


def solution(mesh):
    return jax.shard_map(
        shards,
        mesh=mesh,
        in_specs=(
            P(("dp", "hid", "mp"), None),
            P(("dp", "hid", "mp")),
            P(None, ("dp", "hid", "mp")),
            P(("dp", "hid", "mp"), None),
            P(),
            P(),
            P(("dp", "hid", "mp"), None),
            P(),
            P(("dp", "hid", "mp"), None),
            P(("dp", "hid", "mp"), None),
            P(),
            P(("dp", "hid", "mp"), None),
            P(),
            P(),
            P(),
            P("dp", ("hid", "mp")),
            P(),
            P(("hid", "mp"), "dp"),
            P(),
        ),
        out_specs=(
            P(("dp", "hid", "mp"), None),
            P(("dp", "hid", "mp"), None),
            P(),
            P(),
            P(("dp", "hid", "mp"), None),
            P(),
            P(("dp", "hid", "mp"), None),
            P(("dp", "hid", "mp"), None),
            P(),
            P(("dp", "hid", "mp"), None),
            P(),
            P(),
            P(),
            P("dp", ("hid", "mp")),
            P(),
            P(("hid", "mp"), "dp"),
            P(),
        ),
        check_vma=False,
    )
```

```python
import functools

import jax
import jax.numpy as jnp
from jax import lax
from jax.experimental import pallas as pl
from jax.experimental.pallas import tpu as pltpu
from jax.sharding import PartitionSpec as P

D = 768
HEADS = 12
HEAD = 64
CLUSTERS = 100
SEQ = 1024
PAD = 128


def matmul(left, right):
    return jnp.dot(left, right, preferred_element_type=jnp.float32)


def matmul_nt(left, right):
    return lax.dot_general(left, right, (((1,), (1,)), ((), ())), preferred_element_type=jnp.float32)


def matmul_tn(left, right):
    return lax.dot_general(left, right, (((0,), (0,)), ((), ())), preferred_element_type=jnp.float32)


def swapped(array, axis, mask):
    count = lax.axis_size(axis)
    return lax.ppermute(array, axis, [(i, i ^ mask) for i in range(count)])


def own_bit(axis, bit):
    return (lax.axis_index(axis) >> bit) & 1


def joined(own, other, mine, place):
    own, other = (jnp.expand_dims(own, place), jnp.expand_dims(other, place))
    shape = own.shape[:place] + (2,) + own.shape[place + 1 :]
    return jnp.where(lax.broadcasted_iota(jnp.int32, shape, place) == mine, own, other)


def halves(array, axis, bit, place):
    mine = own_bit(axis, bit)
    take = lambda k: lax.dynamic_index_in_dim(array, k, place, keepdims=False)
    return (take(mine), take(1 - mine))


def high_groups():
    count = lax.axis_size("dp").bit_length() - 1
    return [(b, min(2, count - b)) for b in range(1, count, 2)]


def exchanged(piece, group):
    shift, bits = group
    return [swapped(piece, "dp", d << shift) for d in range(1, 1 << bits)]


def lined_up(own, others, group, place):
    shift, bits = group
    mine = (lax.axis_index("dp") >> shift) & ((1 << bits) - 1)
    pieces = [jnp.expand_dims(p, place) for p in [own, *others]]
    shape = pieces[0].shape[:place] + (1 << bits,) + pieces[0].shape[place + 1 :]
    apart = lax.broadcasted_iota(jnp.int32, shape, place) ^ mine
    out = jnp.broadcast_to(pieces[-1], shape)
    for d in reversed(range(len(pieces) - 1)):
        out = jnp.where(apart == d, pieces[d], out)
    return out


def dealt(array, group, place):
    shift, bits = group
    mine = (lax.axis_index("dp") >> shift) & ((1 << bits) - 1)
    take = lambda k: lax.dynamic_index_in_dim(array, k, place, keepdims=False)
    return [take(mine)] + [swapped(take(mine ^ d), "dp", d << shift) for d in range(1, 1 << bits)]


def summed(pieces):
    return sum(p.astype(jnp.float32) for p in pieces)


def moments(values):
    middle = jnp.mean(values, axis=-1, keepdims=True)
    centered = values - middle
    spread = jnp.mean(centered * centered, axis=-1, keepdims=True)
    return (centered * lax.rsqrt(spread + 1e-05), lax.rsqrt(spread + 1e-05))


def norm_pull(grad, gain, unit, scale):
    scaled = grad * gain
    first = jnp.mean(scaled, axis=-1, keepdims=True)
    second = jnp.mean(scaled * unit, axis=-1, keepdims=True)
    return scale * (scaled - first - unit * second)


def gate_and_slope(v):
    size = jnp.abs(v)
    bell = jnp.exp(-0.5 * v * v)
    t = 1.0 / (1.0 + 0.23164189 * size)
    series = 0.7107068705 + t * (-0.7265760135 + t * 0.5307027145)
    tail = t * (0.127414796 + t * (-0.142248368 + t * series)) * bell
    phi = jnp.where(v < 0, tail, 1.0 - tail)
    return (v * phi, phi + v * (0.3989422804014327 * bell))


def ff_kernel(first, rows, places, *refs):
    x_in, cot_in, xt_in, cott_in, *weights, bu, branch_in = refs[:10]
    refs = refs[10:]
    if not first:
        mid_in, b_down = refs[:2]
        refs = refs[2:]
    branch_out, mid_out, *grads = refs[:6]
    dbu, x, cot, xt, cott, wu, wd, branch, mid, branch_old, mid_old, dw, sems = refs[6:]
    nt = (((1,), (1,)), ((), ()))
    parts = [pl.ds(r * rows, rows) for r in range(x.shape[0] // rows)]
    used = [0]

    def started(source, target):
        used[0] += 1
        made = pltpu.make_async_copy(source, target, sems.at[used[0] - 1])
        made.start()
        return made

    def finish(made):
        for one in made:
            one.wait()

    def fetch_weight(k, target):
        ref, place = (weights[k], places[k])
        return started(ref.at[place], target.at[k // 2])

    early = [fetch_weight(0, wu), started(x_in, x), fetch_weight(1, wd), started(cot_in, cot)]
    finish(early)
    late = [started(cott_in, cott), started(xt_in, xt), fetch_weight(2, wu), fetch_weight(3, wd)]
    late.append(started(branch_in, branch_old))
    if not first:
        late.append(started(mid_in, mid_old))
    outs = []
    for block in (0, 1):
        hs, gs = ([], [])
        total = jnp.zeros((1, dbu.shape[1]), jnp.float32)
        for at in parts:
            pre = matmul(x[at, :], wu[block]) + bu[block : block + 1, :]
            grad_hidden = matmul(cot[at, :], wd[block])
            h, slope = gate_and_slope(pre)
            h = h.astype(jnp.bfloat16)
            g = (grad_hidden * slope).astype(jnp.bfloat16)
            total += jnp.sum(g.astype(jnp.float32), axis=0, keepdims=True)
            forth = lax.dot_general(h, wd[block], nt, preferred_element_type=jnp.float32)
            back = lax.dot_general(g, wu[block], nt, preferred_element_type=jnp.float32)
            if block:
                forth += branch[at, :] + branch_old[at, :]
                back += mid[at, :]
                if not first:
                    forth += b_down[...]
                    back += mid_old[at, :]
            if block and not first:
                x[at, :] = forth.astype(jnp.bfloat16)
            else:
                branch[at, :] = forth
            mid[at, :] = back
            hs.append(h)
            gs.append(g)
        dbu[block : block + 1, :] = total
        if block == 0:
            finish(late)
        else:
            outs += [started(branch if first else x, branch_out), started(mid, mid_out)]
        dw[block, 1] = matmul(cott[...], jnp.concatenate(hs, axis=0)).astype(jnp.bfloat16)
        outs.append(started(dw.at[block, 1], grads[2 * block + 1]))
        dw[block, 0] = matmul(xt[...], jnp.concatenate(gs, axis=0)).astype(jnp.bfloat16)
        outs.append(started(dw.at[block, 0], grads[2 * block]))
    finish(outs)


def ff_blocks(x, cot, xt, cott, weights, places, bu, residual, *sums):
    f32, bf = (jnp.float32, jnp.bfloat16)
    count, wide = (x.shape[0], bu.shape[1])
    spec = pl.BlockSpec(memory_space=pltpu.VMEM)
    far = pl.BlockSpec(memory_space=pl.ANY)
    return pl.pallas_call(
        functools.partial(ff_kernel, not sums, 256, places),
        out_shape=(
            pltpu.HBM((count, D), bf if sums else f32),
            pltpu.HBM((count, D), f32),
            pltpu.HBM((D, wide), bf),
            pltpu.HBM((D, wide), bf),
            pltpu.HBM((D, wide), bf),
            pltpu.HBM((D, wide), bf),
            jax.ShapeDtypeStruct((2, wide), f32),
        ),
        in_specs=[far] * 8 + [spec, far] + [far, spec][: len(sums)],
        out_specs=(far,) * 6 + (spec,),
        scratch_shapes=[
            pltpu.VMEM((count, D), bf),
            pltpu.VMEM((count, D), bf),
            pltpu.VMEM((D, count), bf),
            pltpu.VMEM((D, count), bf),
            pltpu.VMEM((2, D, wide), bf),
            pltpu.VMEM((2, D, wide), bf),
            pltpu.VMEM((count, D), f32),
            pltpu.VMEM((count, D), f32),
            pltpu.VMEM((count, D), f32),
            pltpu.VMEM((count, D), f32),
            pltpu.VMEM((2, 2, D, wide), bf),
            pltpu.SemaphoreType.DMA((16,)),
        ],
        compiler_params=pltpu.CompilerParams(vmem_limit_bytes=60 * 1024 * 1024),
        cost_estimate=pl.CostEstimate(
            flops=24 * count * D * wide, bytes_accessed=8 * D * wide, transcendentals=4 * count * wide
        ),
        name="ff_blocks",
    )(x, cot, xt, cott, *weights, bu, residual, *sums)


STEP = 256
ROWS = pl.BlockSpec((STEP, D), lambda i: (i, 0))
WHOLE = pl.BlockSpec((D, D), lambda i: (0, 0))
LINE = pl.BlockSpec((1, D), lambda i: (0, 0))
LINES = pl.BlockSpec((8, D), lambda i: (0, 0))


def by_rows(kernel, name, in_specs, out_specs, out_shape, scratch, flops, moved):
    return pl.pallas_call(
        kernel,
        grid=(SEQ // STEP,),
        in_specs=in_specs,
        out_specs=out_specs,
        out_shape=out_shape,
        scratch_shapes=scratch,
        compiler_params=pltpu.CompilerParams(vmem_limit_bytes=60 * 1024 * 1024),
        cost_estimate=pl.CostEstimate(flops=flops, bytes_accessed=moved, transcendentals=SEQ),
        name=name,
    )


def middle_kernel(mixed, tokens, out_full, b_out, gain, shift, residual, x, x_t):
    value = tokens[...].astype(jnp.float32) + (matmul(mixed[...], out_full[...]) + b_out[...])
    residual[...] = value
    unit, _ = moments(value)
    normed = (unit * gain[...] + shift[...]).astype(jnp.bfloat16)
    x[...] = normed
    x_t[...] = normed.T


def middle(mixed, tokens, out_full, b_out, gain, shift):
    f32, bf = (jnp.float32, jnp.bfloat16)
    return by_rows(
        middle_kernel,
        "middle",
        [ROWS, ROWS, WHOLE, LINE, LINE, LINE],
        (ROWS, ROWS, pl.BlockSpec((D, STEP), lambda i: (0, i))),
        (pltpu.HBM((SEQ, D), f32), pltpu.HBM((SEQ, D), bf), pltpu.HBM((D, SEQ), bf)),
        [],
        SEQ,
        SEQ,
    )(mixed, tokens, out_full, b_out[None], gain[None], shift[None])


def add_lines(ref, lines):
    @pl.when(pl.program_id(0) == 0)
    def _():
        ref[...] = jnp.zeros_like(ref)

    sums = [jnp.sum(line.astype(jnp.float32), axis=0, keepdims=True) for line in lines]
    ref[: len(lines), :] += jnp.concatenate(sums, axis=0)


def turn_kernel(grad_mid, residual, cot, mixed, out_full, gain, grad_resid, grad_mixed, out_grad, lines, held):
    value = residual[...]
    grad = grad_mid[...]
    unit, scale = moments(value)
    pulled = cot[...].astype(jnp.float32) + norm_pull(grad, gain[...], unit, scale)
    grad_resid[...] = pulled
    low = pulled.astype(jnp.bfloat16)
    grad_mixed[...] = matmul_nt(low, out_full[...]).astype(jnp.bfloat16)
    add_lines(lines, [low, grad * unit, grad, cot[...]])

    @pl.when(pl.program_id(0) == 0)
    def _():
        held[...] = jnp.zeros_like(held)

    held[...] += matmul_tn(mixed[...], low)

    @pl.when(pl.program_id(0) == pl.num_programs(0) - 1)
    def _():
        out_grad[...] = held[...].astype(jnp.bfloat16)


def turn(grad_mid, residual, cot, mixed, out_full, gain):
    f32, bf = (jnp.float32, jnp.bfloat16)
    low = jax.ShapeDtypeStruct((SEQ, D), bf)
    return by_rows(
        turn_kernel,
        "turn",
        [ROWS, ROWS, ROWS, ROWS, WHOLE, LINE],
        (ROWS, ROWS, WHOLE, LINES),
        (pltpu.HBM((SEQ, D), f32), low, pltpu.HBM((D, D), bf), jax.ShapeDtypeStruct((8, D), f32)),
        [pltpu.VMEM((D, D), f32)],
        SEQ,
        SEQ,
    )(grad_mid, residual, cot, mixed, out_full, gain[None])


def last_kernel(gq, gk, gv, wq, wk, wv, tokens, grad_resid, gain, tokens_grad, lines):
    grad = matmul_nt(gq[...], wq[...]) + matmul_nt(gk[...], wk[...]) + matmul_nt(gv[...], wv[...])
    unit, scale = moments(tokens[...].astype(jnp.float32))
    tokens_grad[...] = (grad_resid[...] + norm_pull(grad, gain[...], unit, scale)).astype(jnp.bfloat16)
    add_lines(lines, [grad * unit, grad, gq[...], gv[...]])


def last(gq, gk, gv, wq, wk, wv, tokens, grad_resid, gain):
    return by_rows(
        last_kernel,
        "last",
        [ROWS, ROWS, ROWS, WHOLE, WHOLE, WHOLE, ROWS, ROWS, LINE],
        (ROWS, LINES),
        (jax.ShapeDtypeStruct((SEQ, D), jnp.bfloat16), jax.ShapeDtypeStruct((8, D), jnp.float32)),
        [],
        SEQ,
        SEQ,
    )(gq, gk, gv, wq, wk, wv, tokens, grad_resid, gain[None])


def tied(*arrays):
    return lax.optimization_barrier(arrays)


def packed(sent, small):
    high = small.astype(jnp.bfloat16)
    low = (small - high.astype(jnp.float32)).astype(jnp.bfloat16)
    return jnp.concatenate([sent.reshape(-1, D), high, low])


def unpacked(got, like):
    rows = like.size // D
    high, low = jnp.split(got[rows:].astype(jnp.float32), 2)
    return (got[:rows].reshape(like.shape), high + low)


def added(own, got):
    return (own.astype(jnp.float32) + got.astype(jnp.float32)).astype(jnp.bfloat16)


def dot(a, b, ca=1, cb=0):
    return lax.dot_general(a, b, (((ca,), (cb,)), ((), ())), preferred_element_type=jnp.float32)


def rounded_sum(pieces):
    return summed(pieces).astype(jnp.bfloat16)


def sum_halves(pieces, axis, bit, place):
    both = [halves(piece, axis, bit, place) for piece in pieces]
    return (rounded_sum([kept for kept, _ in both]), rounded_sum([sent for _, sent in both]))


def own_half(wide):
    rows = lax.broadcasted_iota(jnp.int32, wide.shape, 0) // PAD
    columns = lax.broadcasted_iota(jnp.int32, wide.shape, 1) // HEAD
    return jnp.where(rows == columns, wide, 0.0)


def pair_rows(ids):
    at = lax.broadcasted_iota(jnp.int32, (PAD, SEQ), 0)
    return jnp.concatenate([jnp.where(ids[k : k + 1, :] == at, 1.0, 0.0) for k in (0, 1)], axis=0).astype(jnp.bfloat16)


def pair_columns(ids):
    at = lax.broadcasted_iota(jnp.int32, (SEQ, PAD), 1)
    return jnp.concatenate([jnp.where(ids[:, k : k + 1] == at, 1.0, 0.0) for k in (0, 1)], axis=1).astype(jnp.bfloat16)


def attend_kernel(q, k, v, rows, columns, seg_row, seg_col, mixed, prob, centroid, count):
    bf = jnp.bfloat16
    hot = pair_rows(rows[0])
    lanes = lax.broadcasted_iota(jnp.int32, (SEQ, PAD), 1)
    marks = jnp.where(lanes == 0, seg_col[...], jnp.where(lanes == 1, 1.0, 0.0)).astype(bf)
    sums = dot(hot, jnp.concatenate([q[...], marks], axis=1))
    owner, counts = (sums[:, 128:129], sums[:, 129:130])
    counts = jnp.maximum(counts, 1.0)
    middle = own_half(sums[:, :128] / counts).astype(bf)
    scores = 0.125 * dot(middle, k[...], 1, 1)
    allowed = jnp.abs(owner - counts * seg_row[...]) < 0.5
    masked = jnp.where(allowed, scores, -1e30)
    highest = jnp.max(masked, axis=1, keepdims=True)
    exponent = jnp.where(allowed, jnp.exp(masked - highest), 0.0)
    total = jnp.sum(exponent, axis=1, keepdims=True)
    p = exponent * (1.0 / jnp.maximum(total, 1e-30))
    context = own_half(dot(p.astype(bf), v[...])).astype(bf)
    mixed[...] = dot(pair_columns(columns[0]), context).astype(bf)
    prob[0] = p
    centroid[0] = middle
    count[0] = jnp.broadcast_to(counts, (2 * PAD, 128))


def attend(q, k, v, rows, columns, seg_row, seg_col):
    bf = jnp.bfloat16
    pair = pl.BlockSpec((SEQ, 128), lambda i: (0, i))
    return pl.pallas_call(
        attend_kernel,
        grid=(HEADS // 2,),
        in_specs=[pair, pair, pair,
            pl.BlockSpec((1, 2, SEQ), lambda i: (i, 0, 0)),
            pl.BlockSpec((1, SEQ, 2), lambda i: (i, 0, 0)),
            pl.BlockSpec((1, SEQ), lambda i: (0, 0)),
            pl.BlockSpec((SEQ, 1), lambda i: (0, 0))],
        out_specs=(pair, pl.BlockSpec((1, 2 * PAD, SEQ), lambda i: (i, 0, 0)), pl.BlockSpec((1, 2 * PAD, 128), lambda i: (i, 0, 0)), pl.BlockSpec((1, 2 * PAD, 128), lambda i: (i, 0, 0))),
        out_shape=(pltpu.HBM((SEQ, D), bf), pltpu.HBM((HEADS // 2, 2 * PAD, SEQ), jnp.float32), pltpu.HBM((HEADS // 2, 2 * PAD, 128), bf), pltpu.HBM((HEADS // 2, 2 * PAD, 128), jnp.float32)),
        cost_estimate=pl.CostEstimate(flops=12 * 5 * 2 * PAD * SEQ * HEAD, bytes_accessed=14 << 20, transcendentals=HEADS * PAD * SEQ),
        compiler_params=pltpu.CompilerParams(vmem_limit_bytes=24 * 1024 * 1024),
        name="attend",
    )(q, k, v, rows, columns, seg_row, seg_col)


def attend_back_kernel(k, v, gm, rows, columns, prob, centroid, count, gq, gk, gv):
    bf = jnp.bfloat16
    hot = pair_rows(rows[0])
    p = prob[0]
    grad_context = own_half(dot(hot, gm[...])).astype(bf)
    gv[...] = dot(p.astype(bf), grad_context, 0, 0).astype(bf)
    grad_prob = dot(grad_context, v[...], 1, 1)
    grad_scores = (p * (grad_prob - jnp.sum(p * grad_prob, axis=1, keepdims=True))).astype(bf)
    grad_centroid = own_half(0.125 * dot(grad_scores, k[...]) / count[0]).astype(bf)
    gk[...] = (0.125 * dot(grad_scores, centroid[0], 0, 0)).astype(bf)
    gq[...] = dot(pair_columns(columns[0]), grad_centroid).astype(bf)


def attend_back(k, v, gm, rows, columns, prob, centroid, count):
    bf = jnp.bfloat16
    pair = pl.BlockSpec((SEQ, 128), lambda i: (0, i))
    wide = pl.BlockSpec((1, 2 * PAD, 128), lambda i: (i, 0, 0))
    out = pltpu.HBM((SEQ, D), bf)
    return pl.pallas_call(
        attend_back_kernel,
        grid=(HEADS // 2,),
        in_specs=[pair, pair, pair,
            pl.BlockSpec((1, 2, SEQ), lambda i: (i, 0, 0)),
            pl.BlockSpec((1, SEQ, 2), lambda i: (i, 0, 0)),
            pl.BlockSpec((1, 2 * PAD, SEQ), lambda i: (i, 0, 0)), wide, wide],
        out_specs=(pair, pair, pair),
        out_shape=(out, out, out),
        cost_estimate=pl.CostEstimate(flops=SEQ, bytes_accessed=SEQ, transcendentals=0),
        compiler_params=pltpu.CompilerParams(vmem_limit_bytes=60 * 1024 * 1024),
        name="attend_back",
    )(k, v, gm, rows, columns, prob, centroid, count)


def shards(
    tokens,
    segment_ids,
    cluster_ids,
    cotangent,
    first_gain,
    first_shift,
    w_query,
    b_query,
    w_key,
    w_value,
    b_value,
    w_out,
    b_out,
    second_gain,
    second_shift,
    w_up,
    b_up,
    w_down,
    b_down,
):
    groups = high_groups()
    tops = 1 << sum(bits for _, bits in groups)
    bf = jnp.bfloat16
    part = D // (8 * tops)
    wide = D // (2 * tops)
    whole = [1 << bits for _, bits in reversed(groups)]

    attn = jnp.stack([w.astype(bf) for w in (w_query, w_key, w_value, w_out)])
    up, down = (w_up.astype(bf), w_down.T.astype(bf))
    unit_in, _ = moments(tokens.astype(jnp.float32))
    normed_in = (unit_in * first_gain + first_shift).astype(bf)
    id_rows = cluster_ids.reshape(HEADS // 2, 2, SEQ)
    id_columns = id_rows.transpose(0, 2, 1)
    seg = segment_ids.astype(jnp.float32)
    seg_row, seg_col = (seg[None, :], seg[:, None])
    cot_t = cotangent.T
    for group in groups:
        got = exchanged(attn, group)
        normed_in, id_columns, seg_col, *got = tied(normed_in, id_columns, seg_col, *got)
        attn = lined_up(attn, got, group, 1)
    attn = attn.reshape(4, tops, part, D)
    first, second = (attn[:2], attn[2:])
    first_got, second_got = (swapped(first, "dp", 1), swapped(second, "hid", 1))
    for group in groups[:-1]:
        up = lined_up(up, exchanged(up, group), group, 0)
        down = lined_up(down, exchanged(down, group), group, 0)
    up_got, down_got = (exchanged(up, groups[-1]), exchanged(down, groups[-1]))
    cot_t, first_got, second_got, *up_got = tied(cot_t, first_got, second_got, *up_got)
    first = joined(first, first_got, own_bit("dp", 0), 2)
    second = joined(second, second_got, own_bit("hid", 0), 2)
    first_got, second_got = (swapped(first, "hid", 1), swapped(second, "dp", 1))
    first_got, second_got, *down_got = tied(first_got, second_got, *down_got)
    half = tops // 2
    up = lined_up(up, up_got, groups[-1], 0).reshape(tops, wide, D)
    up_one, up_two = (up[:half], up[half:])
    up_one_got, up_two_got = (swapped(up_one, "dp", 1), swapped(up_two, "hid", 1))
    down = lined_up(down, down_got, groups[-1], 0).reshape(tops, wide, D)
    down_one, down_two = (down[:half], down[half:])
    down_one_got, down_two_got = (swapped(down_one, "dp", 1), swapped(down_two, "hid", 1))
    first = joined(first, first_got, own_bit("hid", 0), 3)
    second = joined(second, second_got, own_bit("dp", 0), 2)
    first_got, second_got = (swapped(first, "mp", 1), swapped(second, "mp", 1))
    first = joined(first, first_got, own_bit("mp", 0), 4)
    second = joined(second, second_got, own_bit("mp", 0), 4)
    query_full, key_full = first.reshape(2, D, D)
    value_full, out_full = second.reshape(2, D, D)

    value_rows = (matmul(normed_in, value_full) + b_value).astype(bf)
    value_rows, normed, up_one_got, up_two_got = tied(value_rows, normed_in, up_one_got, up_two_got)
    up_one, up_two = (joined(up_one, up_one_got, own_bit("dp", 0), 1), jnp.stack([up_two, up_two_got]))
    up_one_got, up_two_got = (swapped(up_one, "hid", 1), swapped(up_two, "dp", 1))
    key_rows = matmul(normed, key_full).astype(bf)
    query = (matmul(normed, query_full) + b_query).astype(bf)
    key_rows, down_one_got, down_two_got = tied(key_rows, down_one_got, down_two_got)
    down_one, down_two = (joined(down_one, down_one_got, own_bit("dp", 0), 1), jnp.stack([down_two, down_two_got]))
    down_one_got, down_two_got = (swapped(down_one, "hid", 1), swapped(down_two, "dp", 1))
    mixed, probability, centroid, counts = attend(
        query, key_rows, value_rows, id_rows, id_columns, seg_row, seg_col
    )
    mixed, up_one_got, up_two_got = tied(mixed, up_one_got, up_two_got)
    up_two = joined(up_two, up_two_got, own_bit("dp", 0), 2)
    ups = jnp.stack([jnp.concatenate([up_one, up_two[0]]), jnp.concatenate([up_one_got, up_two[1]])])
    ups = ups.reshape(2, D, D)
    ups_next = swapped(ups, "mp", 1)
    residual, x, x_t = middle(mixed, tokens, out_full, b_out, second_gain, second_shift)
    x, x_t, down_one_got, down_two_got = tied(x, x_t, down_one_got, down_two_got)
    down_two = joined(down_two, down_two_got, own_bit("dp", 0), 2)
    down_mate = jnp.concatenate([down_one_got, down_two[1]]).reshape(1, D, D)
    down_across = swapped(down_mate, "mp", 1)
    down = jnp.concatenate([down_one, down_two[0]]).reshape(1, D, D)
    down_next = swapped(down, "mp", 1)
    me = lax.axis_index(("hid", "mp"))
    biases = lambda blocks: jnp.stack([lax.dynamic_slice_in_dim(b_up, block * D, D) for block in blocks])
    split = lambda piece: piece.reshape(tops, 2, wide, D)
    branch, grad_mid, up_send, down_send, up_own, down_own, far_bias = ff_blocks(
        x, cotangent, x_t, cot_t, (ups_next, down_across, ups, down_mate), (1, 0, 1, 0), biases((me ^ 3, me ^ 2)), residual
    )
    up_far = added(up_own, swapped(up_send, "mp", 1))
    down_far, down_sent = sum_halves([split(down_own), split(swapped(down_send, "mp", 1))], "dp", 0, 1)
    branch, grad_mid, up_far, down_sent = tied(branch, grad_mid, up_far, down_sent)
    up_far_got = swapped(up_far, "hid", 1)
    down_far_got = swapped(down_sent, "dp", 1)
    output, grad_mid, up_send, down_send, up_own, down_own, near_bias = ff_blocks(
        x, cotangent, x_t, cot_t, (ups_next, down_next, ups, down), (0, 0, 0, 0), biases((me ^ 1, me)), branch, grad_mid, b_down[None]
    )
    grad_mid, up_send, down_send, up_far_got, down_far_got = tied(grad_mid, up_send, down_send, up_far_got, down_far_got)
    up_near_got, down_near_got = (swapped(up_send, "mp", 1), swapped(down_send, "mp", 1))
    bias_up = jnp.zeros((4, D), jnp.float32)
    for block, bias in ((me ^ 3, far_bias[:1]), (me ^ 2, far_bias[1:]), (me ^ 1, near_bias[:1]), (me, near_bias[1:])):
        bias_up = lax.dynamic_update_slice(bias_up, bias, (block, 0))
    down_far = added(down_far, down_far_got)
    grad_mid, down_far = tied(grad_mid, down_far)
    down_got = swapped(down_far, "hid", 1)

    grad_resid, grad_mixed, out_grad, turn_lines = turn(grad_mid, residual, cotangent, mixed, out_full, second_gain)
    grad_mixed, up_near_got, down_near_got = tied(grad_mixed, up_near_got, down_near_got)
    down_near, down_sent = sum_halves([split(down_own), split(down_near_got)], "dp", 0, 1)
    up_near, up_sent = sum_halves([split(up_own), split(up_near_got), split(up_far_got)], "dp", 0, 1)
    grad_mixed, down_sent, up_sent = tied(grad_mixed, down_sent, up_sent)
    down_near_got = swapped(down_sent, "dp", 1)
    up_got = swapped(up_sent, "dp", 1)

    grad_query, grad_key, grad_value = attend_back(
        key_rows, value_rows, grad_mixed, id_rows, id_columns, probability, centroid, counts
    )
    grad_value, down_got, down_near_got = tied(grad_value, down_got, down_near_got)
    down_sum = rounded_sum([down_near, down_near_got, down_got]).reshape(*whole, wide, D)

    query_grad = matmul_tn(normed_in, grad_query).astype(bf)
    key_grad = matmul_tn(normed_in, grad_key).astype(bf)
    value_grad = matmul_tn(normed_in, grad_value).astype(bf)
    query_grad, key_grad, value_grad, up_got = tied(query_grad, key_grad, value_grad, up_got)
    both = jnp.stack([query_grad, key_grad, value_grad, out_grad]).reshape(4, tops, 2, 2, 2, part, D)
    both, sent = halves(both, "mp", 0, 4)
    got = swapped(sent, "mp", 1)
    ff_parts = dealt(jnp.stack([added(up_near, up_got).reshape(*whole, wide, D), down_sum]), groups[-1], 1)
    both = added(both, got)
    one, one_sent = halves(both[:2], "dp", 0, 2)
    two, two_sent = halves(both[2:], "hid", 0, 3)
    grad_resid, one_sent, two_sent, ff_parts[0] = tied(grad_resid, one_sent, two_sent, ff_parts[0])
    one_got, two_got = (swapped(one_sent, "dp", 1), swapped(two_sent, "hid", 1))
    tokens_grad, last_lines = last(
        grad_query, grad_key, grad_value, query_full, key_full, value_full, tokens, grad_resid, first_gain
    )
    small = jnp.concatenate([last_lines[:4], turn_lines[:4], bias_up])
    small, one_got, two_got, *ff_parts = tied(small, one_got, two_got, *ff_parts)
    small = small + swapped(small, "mp", 1)
    small = small + swapped(small, "dp", 1)
    one, one_sent = halves(added(one, one_got), "hid", 0, 2)
    two, two_sent = halves(added(two, two_got), "dp", 0, 2)
    got, two_got = (swapped(packed(one_sent, small), "hid", 1), swapped(two_sent, "dp", 1))
    one_got, small_got = unpacked(got, one_sent)
    small = small + small_got
    both = jnp.stack([added(one, one_got), added(two, two_got)]).reshape(4, *whole, part, D)
    for group in reversed(groups):
        shift, bits = group
        mine = (lax.axis_index("dp") >> shift) & ((1 << bits) - 1)
        take = lambda k: lax.dynamic_index_in_dim(both, k, 1, keepdims=False)
        got = [swapped(packed(take(mine ^ d), small), "dp", d << shift) for d in range(1, 1 << bits)]
        pieces = [unpacked(g, take(mine)) for g in got]
        sums = summed([take(mine)] + [piece for piece, _ in pieces])
        small = summed([small] + [piece for _, piece in pieces])
        both = sums.astype(bf)
    for group in reversed(groups[:-1]):
        ff_parts = dealt(rounded_sum(ff_parts), group, 1)
    up_grad, down_grad = summed(ff_parts)
    down_grad = down_grad.T
    query_sum, key_sum, value_sum, out_sum = sums
    return (
        output,
        tokens_grad,
        small[0],
        small[1],
        query_sum,
        small[2],
        key_sum,
        value_sum,
        small[3],
        out_sum,
        small[4],
        small[5],
        small[6],
        up_grad,
        small[8:].reshape(-1),
        down_grad,
        small[7],
    )


def solution(mesh):
    return jax.shard_map(
        shards,
        mesh=mesh,
        in_specs=(
            P(("dp", "hid", "mp"), None),
            P(("dp", "hid", "mp")),
            P(None, ("dp", "hid", "mp")),
            P(("dp", "hid", "mp"), None),
            P(),
            P(),
            P(("dp", "hid", "mp"), None),
            P(),
            P(("dp", "hid", "mp"), None),
            P(("dp", "hid", "mp"), None),
            P(),
            P(("dp", "hid", "mp"), None),
            P(),
            P(),
            P(),
            P("dp", ("hid", "mp")),
            P(),
            P(("hid", "mp"), "dp"),
            P(),
        ),
        out_specs=(
            P(("dp", "hid", "mp"), None),
            P(("dp", "hid", "mp"), None),
            P(),
            P(),
            P(("dp", "hid", "mp"), None),
            P(),
            P(("dp", "hid", "mp"), None),
            P(("dp", "hid", "mp"), None),
            P(),
            P(("dp", "hid", "mp"), None),
            P(),
            P(),
            P(),
            P("dp", ("hid", "mp")),
            P(),
            P(("hid", "mp"), "dp"),
            P(),
        ),
        check_vma=False,
    )
```

```python
import functools

import jax
import jax.numpy as jnp
from jax import lax
from jax.experimental import pallas as pl
from jax.experimental.pallas import tpu as pltpu
from jax.sharding import PartitionSpec as P

D = 768
HEADS = 12
HEAD = 64
CLUSTERS = 100
SEQ = 1024
PAD = 128


def matmul(left, right):
    return jnp.dot(left, right, preferred_element_type=jnp.float32)


def matmul_nt(left, right):
    return lax.dot_general(left, right, (((1,), (1,)), ((), ())), preferred_element_type=jnp.float32)


def matmul_tn(left, right):
    return lax.dot_general(left, right, (((0,), (0,)), ((), ())), preferred_element_type=jnp.float32)


def swapped(array, axis, mask):
    count = lax.axis_size(axis)
    return lax.ppermute(array, axis, [(i, i ^ mask) for i in range(count)])


def own_bit(axis, bit):
    return (lax.axis_index(axis) >> bit) & 1


def joined(own, other, mine, place):
    own, other = (jnp.expand_dims(own, place), jnp.expand_dims(other, place))
    shape = own.shape[:place] + (2,) + own.shape[place + 1 :]
    return jnp.where(lax.broadcasted_iota(jnp.int32, shape, place) == mine, own, other)


def halves(array, axis, bit, place):
    mine = own_bit(axis, bit)
    take = lambda k: lax.dynamic_index_in_dim(array, k, place, keepdims=False)
    return (take(mine), take(1 - mine))


def high_groups():
    count = lax.axis_size("dp").bit_length() - 1
    return [(b, min(2, count - b)) for b in range(1, count, 2)]


def exchanged(piece, group):
    shift, bits = group
    return [swapped(piece, "dp", d << shift) for d in range(1, 1 << bits)]


def lined_up(own, others, group, place):
    shift, bits = group
    mine = (lax.axis_index("dp") >> shift) & ((1 << bits) - 1)
    pieces = [jnp.expand_dims(p, place) for p in [own, *others]]
    shape = pieces[0].shape[:place] + (1 << bits,) + pieces[0].shape[place + 1 :]
    apart = lax.broadcasted_iota(jnp.int32, shape, place) ^ mine
    out = jnp.broadcast_to(pieces[-1], shape)
    for d in reversed(range(len(pieces) - 1)):
        out = jnp.where(apart == d, pieces[d], out)
    return out


def dealt(array, group, place):
    shift, bits = group
    mine = (lax.axis_index("dp") >> shift) & ((1 << bits) - 1)
    take = lambda k: lax.dynamic_index_in_dim(array, k, place, keepdims=False)
    return [take(mine)] + [swapped(take(mine ^ d), "dp", d << shift) for d in range(1, 1 << bits)]


def summed(pieces):
    return sum(p.astype(jnp.float32) for p in pieces)


def moments(values):
    middle = jnp.mean(values, axis=-1, keepdims=True)
    centered = values - middle
    spread = jnp.mean(centered * centered, axis=-1, keepdims=True)
    return (centered * lax.rsqrt(spread + 1e-05), lax.rsqrt(spread + 1e-05))


def norm_pull(grad, gain, unit, scale):
    scaled = grad * gain
    first = jnp.mean(scaled, axis=-1, keepdims=True)
    second = jnp.mean(scaled * unit, axis=-1, keepdims=True)
    return scale * (scaled - first - unit * second)


def gate_and_slope(v):
    size = jnp.abs(v)
    bell = jnp.exp(-0.5 * v * v)
    t = 1.0 / (1.0 + 0.23164189 * size)
    series = 0.7107068705 + t * (-0.7265760135 + t * 0.5307027145)
    tail = t * (0.127414796 + t * (-0.142248368 + t * series)) * bell
    phi = jnp.where(v < 0, tail, 1.0 - tail)
    return (v * phi, phi + v * (0.3989422804014327 * bell))


def ff_kernel(first, rows, places, *refs):
    x_in, cot_in, xt_in, cott_in, *weights, bu, branch_in = refs[:14]
    refs = refs[14:]
    if not first:
        mid_in, b_down = refs[:2]
        refs = refs[2:]
    branch_out, mid_out, *grads = refs[:6]
    dbu, x, cot, xt, cott, wu, wd, branch, mid, branch_old, mid_old, dw, sems = refs[6:]
    nt = (((1,), (1,)), ((), ()))
    parts = [pl.ds(r * rows, rows) for r in range(x.shape[0] // rows)]
    used = [0]

    def started(source, target):
        used[0] += 1
        made = pltpu.make_async_copy(source, target, sems.at[used[0] - 1])
        made.start()
        return made

    def finish(made):
        for one in made:
            one.wait()

    def fetch_weight(k, target):
        return [
            started(weights[2 * k + j].at[places[2 * k + j]], target.at[k // 2, pl.ds(j * (D // 2), D // 2)])
            for j in (0, 1)
        ]

    early = fetch_weight(0, wu) + [started(x_in, x)] + fetch_weight(1, wd) + [started(cot_in, cot)]
    finish(early)
    late = [started(cott_in, cott), started(xt_in, xt)] + fetch_weight(2, wu) + fetch_weight(3, wd)
    late.append(started(branch_in, branch_old))
    if not first:
        late.append(started(mid_in, mid_old))
    outs = []
    for block in (0, 1):
        hs, gs = ([], [])
        total = jnp.zeros((1, dbu.shape[1]), jnp.float32)
        for at in parts:
            pre = matmul(x[at, :], wu[block]) + bu[block : block + 1, :]
            grad_hidden = matmul(cot[at, :], wd[block])
            h, slope = gate_and_slope(pre)
            h = h.astype(jnp.bfloat16)
            g = (grad_hidden * slope).astype(jnp.bfloat16)
            total += jnp.sum(g.astype(jnp.float32), axis=0, keepdims=True)
            forth = lax.dot_general(h, wd[block], nt, preferred_element_type=jnp.float32)
            back = lax.dot_general(g, wu[block], nt, preferred_element_type=jnp.float32)
            if block:
                forth += branch[at, :] + branch_old[at, :]
                back += mid[at, :]
                if not first:
                    forth += b_down[...]
                    back += mid_old[at, :]
            if block and not first:
                x[at, :] = forth.astype(jnp.bfloat16)
            else:
                branch[at, :] = forth
            mid[at, :] = back
            hs.append(h)
            gs.append(g)
        dbu[block : block + 1, :] = total
        if block == 0:
            finish(late)
        else:
            outs += [started(branch if first else x, branch_out), started(mid, mid_out)]
        dw[block, 1] = matmul(cott[...], jnp.concatenate(hs, axis=0)).astype(jnp.bfloat16)
        outs.append(started(dw.at[block, 1], grads[2 * block + 1]))
        dw[block, 0] = matmul(xt[...], jnp.concatenate(gs, axis=0)).astype(jnp.bfloat16)
        outs.append(started(dw.at[block, 0], grads[2 * block]))
    finish(outs)


def ff_blocks(x, cot, xt, cott, halved, bu, residual, *sums):
    f32, bf = (jnp.float32, jnp.bfloat16)
    count, wide = (x.shape[0], bu.shape[1])
    weights, places = zip(*[half for weight in halved for half in weight])
    spec = pl.BlockSpec(memory_space=pltpu.VMEM)
    far = pl.BlockSpec(memory_space=pl.ANY)
    return pl.pallas_call(
        functools.partial(ff_kernel, not sums, 256, places),
        out_shape=(
            pltpu.HBM((count, D), bf if sums else f32),
            pltpu.HBM((count, D), f32),
            pltpu.HBM((D, wide), bf),
            pltpu.HBM((D, wide), bf),
            pltpu.HBM((D, wide), bf),
            pltpu.HBM((D, wide), bf),
            jax.ShapeDtypeStruct((2, wide), f32),
        ),
        in_specs=[far] * 12 + [spec, far] + [far, spec][: len(sums)],
        out_specs=(far,) * 6 + (spec,),
        scratch_shapes=[
            pltpu.VMEM((count, D), bf),
            pltpu.VMEM((count, D), bf),
            pltpu.VMEM((D, count), bf),
            pltpu.VMEM((D, count), bf),
            pltpu.VMEM((2, D, wide), bf),
            pltpu.VMEM((2, D, wide), bf),
            pltpu.VMEM((count, D), f32),
            pltpu.VMEM((count, D), f32),
            pltpu.VMEM((count, D), f32),
            pltpu.VMEM((count, D), f32),
            pltpu.VMEM((2, 2, D, wide), bf),
            pltpu.SemaphoreType.DMA((24,)),
        ],
        compiler_params=pltpu.CompilerParams(vmem_limit_bytes=60 * 1024 * 1024),
        cost_estimate=pl.CostEstimate(
            flops=24 * count * D * wide, bytes_accessed=8 * D * wide, transcendentals=4 * count * wide
        ),
        name="ff_blocks",
    )(x, cot, xt, cott, *weights, bu, residual, *sums)


STEP = 256
ROWS = pl.BlockSpec((STEP, D), lambda i: (i, 0))
WHOLE = pl.BlockSpec((D, D), lambda i: (0, 0))
LINE = pl.BlockSpec((1, D), lambda i: (0, 0))
LINES = pl.BlockSpec((8, D), lambda i: (0, 0))


def by_rows(kernel, name, in_specs, out_specs, out_shape, scratch, flops, moved):
    return pl.pallas_call(
        kernel,
        grid=(SEQ // STEP,),
        in_specs=in_specs,
        out_specs=out_specs,
        out_shape=out_shape,
        scratch_shapes=scratch,
        compiler_params=pltpu.CompilerParams(vmem_limit_bytes=60 * 1024 * 1024),
        cost_estimate=pl.CostEstimate(flops=flops, bytes_accessed=moved, transcendentals=SEQ),
        name=name,
    )


def middle_kernel(mixed, tokens, out_full, b_out, gain, shift, residual, x, x_t):
    value = tokens[...].astype(jnp.float32) + (matmul(mixed[...], out_full[...]) + b_out[...])
    residual[...] = value
    unit, _ = moments(value)
    normed = (unit * gain[...] + shift[...]).astype(jnp.bfloat16)
    x[...] = normed
    x_t[...] = normed.T


def middle(mixed, tokens, out_full, b_out, gain, shift):
    f32, bf = (jnp.float32, jnp.bfloat16)
    return by_rows(
        middle_kernel,
        "middle",
        [ROWS, ROWS, WHOLE, LINE, LINE, LINE],
        (ROWS, ROWS, pl.BlockSpec((D, STEP), lambda i: (0, i))),
        (pltpu.HBM((SEQ, D), f32), pltpu.HBM((SEQ, D), bf), pltpu.HBM((D, SEQ), bf)),
        [],
        SEQ,
        SEQ,
    )(mixed, tokens, out_full, b_out[None], gain[None], shift[None])


def add_lines(ref, lines):
    @pl.when(pl.program_id(0) == 0)
    def _():
        ref[...] = jnp.zeros_like(ref)

    sums = [jnp.sum(line.astype(jnp.float32), axis=0, keepdims=True) for line in lines]
    ref[: len(lines), :] += jnp.concatenate(sums, axis=0)


def turn_kernel(grad_mid, residual, cot, mixed, out_full, gain, grad_resid, grad_mixed, out_grad, lines, held):
    value = residual[...]
    grad = grad_mid[...]
    unit, scale = moments(value)
    pulled = cot[...].astype(jnp.float32) + norm_pull(grad, gain[...], unit, scale)
    grad_resid[...] = pulled
    low = pulled.astype(jnp.bfloat16)
    grad_mixed[...] = matmul_nt(low, out_full[...]).astype(jnp.bfloat16)
    add_lines(lines, [low, grad * unit, grad, cot[...]])

    @pl.when(pl.program_id(0) == 0)
    def _():
        held[...] = jnp.zeros_like(held)

    held[...] += matmul_tn(mixed[...], low)

    @pl.when(pl.program_id(0) == pl.num_programs(0) - 1)
    def _():
        out_grad[...] = held[...].astype(jnp.bfloat16)


def turn(grad_mid, residual, cot, mixed, out_full, gain):
    f32, bf = (jnp.float32, jnp.bfloat16)
    low = jax.ShapeDtypeStruct((SEQ, D), bf)
    return by_rows(
        turn_kernel,
        "turn",
        [ROWS, ROWS, ROWS, ROWS, WHOLE, LINE],
        (ROWS, ROWS, WHOLE, LINES),
        (pltpu.HBM((SEQ, D), f32), low, pltpu.HBM((D, D), bf), jax.ShapeDtypeStruct((8, D), f32)),
        [pltpu.VMEM((D, D), f32)],
        SEQ,
        SEQ,
    )(grad_mid, residual, cot, mixed, out_full, gain[None])


def last_kernel(gq, gk, gv, wq, wk, wv, tokens, grad_resid, gain, tokens_grad, lines):
    grad = matmul_nt(gq[...], wq[...]) + matmul_nt(gk[...], wk[...]) + matmul_nt(gv[...], wv[...])
    unit, scale = moments(tokens[...].astype(jnp.float32))
    tokens_grad[...] = (grad_resid[...] + norm_pull(grad, gain[...], unit, scale)).astype(jnp.bfloat16)
    add_lines(lines, [grad * unit, grad, gq[...], gv[...]])


def last(gq, gk, gv, wq, wk, wv, tokens, grad_resid, gain):
    return by_rows(
        last_kernel,
        "last",
        [ROWS, ROWS, ROWS, WHOLE, WHOLE, WHOLE, ROWS, ROWS, LINE],
        (ROWS, LINES),
        (jax.ShapeDtypeStruct((SEQ, D), jnp.bfloat16), jax.ShapeDtypeStruct((8, D), jnp.float32)),
        [],
        SEQ,
        SEQ,
    )(gq, gk, gv, wq, wk, wv, tokens, grad_resid, gain[None])


def tied(*arrays):
    return lax.optimization_barrier(arrays)


def packed(sent, small):
    high = small.astype(jnp.bfloat16)
    low = (small - high.astype(jnp.float32)).astype(jnp.bfloat16)
    return jnp.concatenate([sent.reshape(-1, D), high, low])


def unpacked(got, like):
    rows = like.size // D
    high, low = jnp.split(got[rows:].astype(jnp.float32), 2)
    return (got[:rows].reshape(like.shape), high + low)


def added(own, got):
    return (own.astype(jnp.float32) + got.astype(jnp.float32)).astype(jnp.bfloat16)


def dot(a, b, ca=1, cb=0):
    return lax.dot_general(a, b, (((ca,), (cb,)), ((), ())), preferred_element_type=jnp.float32)


def rounded_sum(pieces):
    return summed(pieces).astype(jnp.bfloat16)


def sum_halves(pieces, axis, bit, place):
    both = [halves(piece, axis, bit, place) for piece in pieces]
    return (rounded_sum([kept for kept, _ in both]), rounded_sum([sent for _, sent in both]))


def own_half(wide):
    rows = lax.broadcasted_iota(jnp.int32, wide.shape, 0) // PAD
    columns = lax.broadcasted_iota(jnp.int32, wide.shape, 1) // HEAD
    return jnp.where(rows == columns, wide, 0.0)


def pair_rows(ids):
    at = lax.broadcasted_iota(jnp.int32, (PAD, SEQ), 0)
    return jnp.concatenate([jnp.where(ids[k : k + 1, :] == at, 1.0, 0.0) for k in (0, 1)], axis=0).astype(jnp.bfloat16)


def pair_columns(ids):
    at = lax.broadcasted_iota(jnp.int32, (SEQ, PAD), 1)
    return jnp.concatenate([jnp.where(ids[:, k : k + 1] == at, 1.0, 0.0) for k in (0, 1)], axis=1).astype(jnp.bfloat16)


def attend_kernel(q, k, v, rows, columns, seg_row, seg_col, mixed, prob, centroid, count):
    bf = jnp.bfloat16
    hot = pair_rows(rows[0])
    lanes = lax.broadcasted_iota(jnp.int32, (SEQ, PAD), 1)
    marks = jnp.where(lanes == 0, seg_col[...], jnp.where(lanes == 1, 1.0, 0.0)).astype(bf)
    sums = dot(hot, jnp.concatenate([q[...], marks], axis=1))
    owner, counts = (sums[:, 128:129], sums[:, 129:130])
    counts = jnp.maximum(counts, 1.0)
    middle = own_half(sums[:, :128] / counts).astype(bf)
    scores = 0.125 * dot(middle, k[...], 1, 1)
    allowed = jnp.abs(owner - counts * seg_row[...]) < 0.5
    masked = jnp.where(allowed, scores, -1e30)
    highest = jnp.max(masked, axis=1, keepdims=True)
    exponent = jnp.where(allowed, jnp.exp(masked - highest), 0.0)
    total = jnp.sum(exponent, axis=1, keepdims=True)
    p = exponent * (1.0 / jnp.maximum(total, 1e-30))
    context = own_half(dot(p.astype(bf), v[...])).astype(bf)
    mixed[...] = dot(pair_columns(columns[0]), context).astype(bf)
    prob[0] = p
    centroid[0] = middle
    count[0] = jnp.broadcast_to(counts, (2 * PAD, 128))


def attend(q, k, v, rows, columns, seg_row, seg_col):
    bf = jnp.bfloat16
    pair = pl.BlockSpec((SEQ, 128), lambda i: (0, i))
    return pl.pallas_call(
        attend_kernel,
        grid=(HEADS // 2,),
        in_specs=[pair, pair, pair,
            pl.BlockSpec((1, 2, SEQ), lambda i: (i, 0, 0)),
            pl.BlockSpec((1, SEQ, 2), lambda i: (i, 0, 0)),
            pl.BlockSpec((1, SEQ), lambda i: (0, 0)),
            pl.BlockSpec((SEQ, 1), lambda i: (0, 0))],
        out_specs=(pair, pl.BlockSpec((1, 2 * PAD, SEQ), lambda i: (i, 0, 0)), pl.BlockSpec((1, 2 * PAD, 128), lambda i: (i, 0, 0)), pl.BlockSpec((1, 2 * PAD, 128), lambda i: (i, 0, 0))),
        out_shape=(pltpu.HBM((SEQ, D), bf), pltpu.HBM((HEADS // 2, 2 * PAD, SEQ), jnp.float32), pltpu.HBM((HEADS // 2, 2 * PAD, 128), bf), pltpu.HBM((HEADS // 2, 2 * PAD, 128), jnp.float32)),
        cost_estimate=pl.CostEstimate(flops=12 * 5 * 2 * PAD * SEQ * HEAD, bytes_accessed=14 << 20, transcendentals=HEADS * PAD * SEQ),
        compiler_params=pltpu.CompilerParams(vmem_limit_bytes=24 * 1024 * 1024),
        name="attend",
    )(q, k, v, rows, columns, seg_row, seg_col)


def attend_back_kernel(k, v, gm, rows, columns, prob, centroid, count, gq, gk, gv):
    bf = jnp.bfloat16
    hot = pair_rows(rows[0])
    p = prob[0]
    grad_context = own_half(dot(hot, gm[...])).astype(bf)
    gv[...] = dot(p.astype(bf), grad_context, 0, 0).astype(bf)
    grad_prob = dot(grad_context, v[...], 1, 1)
    grad_scores = (p * (grad_prob - jnp.sum(p * grad_prob, axis=1, keepdims=True))).astype(bf)
    grad_centroid = own_half(0.125 * dot(grad_scores, k[...]) / count[0]).astype(bf)
    gk[...] = (0.125 * dot(grad_scores, centroid[0], 0, 0)).astype(bf)
    gq[...] = dot(pair_columns(columns[0]), grad_centroid).astype(bf)


def attend_back(k, v, gm, rows, columns, prob, centroid, count):
    bf = jnp.bfloat16
    pair = pl.BlockSpec((SEQ, 128), lambda i: (0, i))
    wide = pl.BlockSpec((1, 2 * PAD, 128), lambda i: (i, 0, 0))
    out = pltpu.HBM((SEQ, D), bf)
    return pl.pallas_call(
        attend_back_kernel,
        grid=(HEADS // 2,),
        in_specs=[pair, pair, pair,
            pl.BlockSpec((1, 2, SEQ), lambda i: (i, 0, 0)),
            pl.BlockSpec((1, SEQ, 2), lambda i: (i, 0, 0)),
            pl.BlockSpec((1, 2 * PAD, SEQ), lambda i: (i, 0, 0)), wide, wide],
        out_specs=(pair, pair, pair),
        out_shape=(out, out, out),
        cost_estimate=pl.CostEstimate(flops=SEQ, bytes_accessed=SEQ, transcendentals=0),
        compiler_params=pltpu.CompilerParams(vmem_limit_bytes=60 * 1024 * 1024),
        name="attend_back",
    )(k, v, gm, rows, columns, prob, centroid, count)


def shards(
    tokens,
    segment_ids,
    cluster_ids,
    cotangent,
    first_gain,
    first_shift,
    w_query,
    b_query,
    w_key,
    w_value,
    b_value,
    w_out,
    b_out,
    second_gain,
    second_shift,
    w_up,
    b_up,
    w_down,
    b_down,
):
    groups = high_groups()
    tops = 1 << sum(bits for _, bits in groups)
    bf = jnp.bfloat16
    part = D // (8 * tops)
    wide = D // (2 * tops)
    whole = [1 << bits for _, bits in reversed(groups)]

    attn = jnp.stack([w.astype(bf) for w in (w_query, w_key, w_value, w_out)])
    up, down = (w_up.astype(bf), w_down.T.astype(bf))
    unit_in, _ = moments(tokens.astype(jnp.float32))
    normed_in = (unit_in * first_gain + first_shift).astype(bf)
    id_rows = cluster_ids.reshape(HEADS // 2, 2, SEQ)
    id_columns = id_rows.transpose(0, 2, 1)
    seg = segment_ids.astype(jnp.float32)
    seg_row, seg_col = (seg[None, :], seg[:, None])
    cot_t = cotangent.T
    for group in groups:
        got = exchanged(attn, group)
        normed_in, id_columns, seg_col, *got = tied(normed_in, id_columns, seg_col, *got)
        attn = lined_up(attn, got, group, 1)
    attn = attn.reshape(4, tops, part, D)
    first, second = (attn[:2], attn[2:])
    first_got, second_got = (swapped(first, "dp", 1), swapped(second, "hid", 1))
    for group in groups[:-1]:
        up = lined_up(up, exchanged(up, group), group, 0)
        down = lined_up(down, exchanged(down, group), group, 0)
    up_got, down_got = (exchanged(up, groups[-1]), exchanged(down, groups[-1]))
    cot_t, first_got, second_got, *up_got = tied(cot_t, first_got, second_got, *up_got)
    first = joined(first, first_got, own_bit("dp", 0), 2)
    second = joined(second, second_got, own_bit("hid", 0), 2)
    first_got, second_got = (swapped(first, "hid", 1), swapped(second, "dp", 1))
    first_got, second_got, *down_got = tied(first_got, second_got, *down_got)
    half = tops // 2
    up = lined_up(up, up_got, groups[-1], 0).reshape(tops, wide, D)
    up_one, up_two = (up[:half], up[half:])
    up_one_got, up_two_got = (swapped(up_one, "dp", 1), swapped(up_two, "hid", 1))
    down = lined_up(down, down_got, groups[-1], 0).reshape(tops, wide, D)
    down_one, down_two = (down[:half], down[half:])
    down_one_got, down_two_got = (swapped(down_one, "dp", 1), swapped(down_two, "hid", 1))
    first = joined(first, first_got, own_bit("hid", 0), 3)
    second = joined(second, second_got, own_bit("dp", 0), 2)
    first_got, second_got = (swapped(first, "mp", 1), swapped(second, "mp", 1))
    first = joined(first, first_got, own_bit("mp", 0), 4)
    second = joined(second, second_got, own_bit("mp", 0), 4)
    query_full, key_full = first.reshape(2, D, D)
    value_full, out_full = second.reshape(2, D, D)

    value_rows = (matmul(normed_in, value_full) + b_value).astype(bf)
    value_rows, normed, up_one_got, up_two_got = tied(value_rows, normed_in, up_one_got, up_two_got)
    up_one, up_two = (joined(up_one, up_one_got, own_bit("dp", 0), 1), jnp.stack([up_two, up_two_got]))
    up_one_got, up_two_got = (swapped(up_one, "hid", 1), swapped(up_two, "dp", 1))
    key_rows = matmul(normed, key_full).astype(bf)
    query = (matmul(normed, query_full) + b_query).astype(bf)
    key_rows, down_one_got, down_two_got = tied(key_rows, down_one_got, down_two_got)
    down_one, down_two = (joined(down_one, down_one_got, own_bit("dp", 0), 1), jnp.stack([down_two, down_two_got]))
    down_one_got, down_two_got = (swapped(down_one, "hid", 1), swapped(down_two, "dp", 1))
    mixed, probability, centroid, counts = attend(
        query, key_rows, value_rows, id_rows, id_columns, seg_row, seg_col
    )
    mixed, up_one_got, up_two_got = tied(mixed, up_one_got, up_two_got)
    up_two = joined(up_two, up_two_got, own_bit("dp", 0), 2)
    rows = lambda piece: piece.reshape(-1, D // 2, D)
    up_one, up_mate, up_two = (rows(up_one), rows(up_one_got), rows(up_two))
    up_one_next, up_mate_next, up_two_next = [swapped(piece, "mp", 1) for piece in (up_one, up_mate, up_two)]
    residual, x, x_t = middle(mixed, tokens, out_full, b_out, second_gain, second_shift)
    x, x_t, down_one_got, down_two_got = tied(x, x_t, down_one_got, down_two_got)
    down_two = joined(down_two, down_two_got, own_bit("dp", 0), 2)
    down_one, down_mate, down_two = (rows(down_one), rows(down_one_got), rows(down_two))
    down_mate_next, down_two_next, down_one_next = [swapped(piece, "mp", 1) for piece in (down_mate, down_two, down_one)]
    pick = lambda one, two, place: ((one, 0), (two, place))
    me = lax.axis_index(("hid", "mp"))
    biases = lambda blocks: jnp.stack([lax.dynamic_slice_in_dim(b_up, block * D, D) for block in blocks])
    split = lambda piece: piece.reshape(tops, 2, wide, D)
    branch, grad_mid, up_send, down_send, up_own, down_own, far_bias = ff_blocks(
        x,
        cotangent,
        x_t,
        cot_t,
        [
            pick(up_mate_next, up_two_next, 1),
            pick(down_mate_next, down_two_next, 1),
            pick(up_mate, up_two, 1),
            pick(down_mate, down_two, 1),
        ],
        biases((me ^ 3, me ^ 2)),
        residual,
    )
    up_far = added(up_own, swapped(up_send, "mp", 1))
    down_far, down_sent = sum_halves([split(down_own), split(swapped(down_send, "mp", 1))], "dp", 0, 1)
    branch, grad_mid, up_far, down_sent = tied(branch, grad_mid, up_far, down_sent)
    up_far_got = swapped(up_far, "hid", 1)
    down_far_got = swapped(down_sent, "dp", 1)
    output, grad_mid, up_send, down_send, up_own, down_own, near_bias = ff_blocks(
        x,
        cotangent,
        x_t,
        cot_t,
        [
            pick(up_one_next, up_two_next, 0),
            pick(down_one_next, down_two_next, 0),
            pick(up_one, up_two, 0),
            pick(down_one, down_two, 0),
        ],
        biases((me ^ 1, me)),
        branch,
        grad_mid,
        b_down[None],
    )
    grad_mid, up_send, down_send, up_far_got, down_far_got = tied(grad_mid, up_send, down_send, up_far_got, down_far_got)
    up_near_got, down_near_got = (swapped(up_send, "mp", 1), swapped(down_send, "mp", 1))
    bias_up = jnp.zeros((4, D), jnp.float32)
    for block, bias in ((me ^ 3, far_bias[:1]), (me ^ 2, far_bias[1:]), (me ^ 1, near_bias[:1]), (me, near_bias[1:])):
        bias_up = lax.dynamic_update_slice(bias_up, bias, (block, 0))
    down_far = added(down_far, down_far_got)
    grad_mid, down_far = tied(grad_mid, down_far)
    down_got = swapped(down_far, "hid", 1)

    grad_resid, grad_mixed, out_grad, turn_lines = turn(grad_mid, residual, cotangent, mixed, out_full, second_gain)
    grad_mixed, up_near_got, down_near_got = tied(grad_mixed, up_near_got, down_near_got)
    down_near, down_sent = sum_halves([split(down_own), split(down_near_got)], "dp", 0, 1)
    up_near, up_sent = sum_halves([split(up_own), split(up_near_got), split(up_far_got)], "dp", 0, 1)
    grad_mixed, down_sent, up_sent = tied(grad_mixed, down_sent, up_sent)
    down_near_got = swapped(down_sent, "dp", 1)
    up_got = swapped(up_sent, "dp", 1)

    grad_query, grad_key, grad_value = attend_back(
        key_rows, value_rows, grad_mixed, id_rows, id_columns, probability, centroid, counts
    )
    grad_value, down_got, down_near_got = tied(grad_value, down_got, down_near_got)
    down_sum = rounded_sum([down_near, down_near_got, down_got]).reshape(*whole, wide, D)

    query_grad = matmul_tn(normed_in, grad_query).astype(bf)
    key_grad = matmul_tn(normed_in, grad_key).astype(bf)
    value_grad = matmul_tn(normed_in, grad_value).astype(bf)
    query_grad, key_grad, value_grad, up_got = tied(query_grad, key_grad, value_grad, up_got)
    both = jnp.stack([query_grad, key_grad, value_grad, out_grad]).reshape(4, tops, 2, 2, 2, part, D)
    both, sent = halves(both, "mp", 0, 4)
    got = swapped(sent, "mp", 1)
    ff_parts = dealt(jnp.stack([added(up_near, up_got).reshape(*whole, wide, D), down_sum]), groups[-1], 1)
    both = added(both, got)
    one, one_sent = halves(both[:2], "dp", 0, 2)
    two, two_sent = halves(both[2:], "hid", 0, 3)
    grad_resid, one_sent, two_sent, ff_parts[0] = tied(grad_resid, one_sent, two_sent, ff_parts[0])
    one_got, two_got = (swapped(one_sent, "dp", 1), swapped(two_sent, "hid", 1))
    tokens_grad, last_lines = last(
        grad_query, grad_key, grad_value, query_full, key_full, value_full, tokens, grad_resid, first_gain
    )
    small = jnp.concatenate([last_lines[:4], turn_lines[:4], bias_up])
    small, one_got, two_got, *ff_parts = tied(small, one_got, two_got, *ff_parts)
    small = small + swapped(small, "mp", 1)
    small = small + swapped(small, "dp", 1)
    one, one_sent = halves(added(one, one_got), "hid", 0, 2)
    two, two_sent = halves(added(two, two_got), "dp", 0, 2)
    got, two_got = (swapped(packed(one_sent, small), "hid", 1), swapped(two_sent, "dp", 1))
    one_got, small_got = unpacked(got, one_sent)
    small = small + small_got
    both = jnp.stack([added(one, one_got), added(two, two_got)]).reshape(4, *whole, part, D)
    for group in reversed(groups):
        shift, bits = group
        mine = (lax.axis_index("dp") >> shift) & ((1 << bits) - 1)
        take = lambda k: lax.dynamic_index_in_dim(both, k, 1, keepdims=False)
        got = [swapped(packed(take(mine ^ d), small), "dp", d << shift) for d in range(1, 1 << bits)]
        pieces = [unpacked(g, take(mine)) for g in got]
        sums = summed([take(mine)] + [piece for piece, _ in pieces])
        small = summed([small] + [piece for _, piece in pieces])
        both = sums.astype(bf)
    for group in reversed(groups[:-1]):
        ff_parts = dealt(rounded_sum(ff_parts), group, 1)
    up_grad, down_grad = summed(ff_parts)
    down_grad = down_grad.T
    query_sum, key_sum, value_sum, out_sum = sums
    return (
        output,
        tokens_grad,
        small[0],
        small[1],
        query_sum,
        small[2],
        key_sum,
        value_sum,
        small[3],
        out_sum,
        small[4],
        small[5],
        small[6],
        up_grad,
        small[8:].reshape(-1),
        down_grad,
        small[7],
    )


def solution(mesh):
    return jax.shard_map(
        shards,
        mesh=mesh,
        in_specs=(
            P(("dp", "hid", "mp"), None),
            P(("dp", "hid", "mp")),
            P(None, ("dp", "hid", "mp")),
            P(("dp", "hid", "mp"), None),
            P(),
            P(),
            P(("dp", "hid", "mp"), None),
            P(),
            P(("dp", "hid", "mp"), None),
            P(("dp", "hid", "mp"), None),
            P(),
            P(("dp", "hid", "mp"), None),
            P(),
            P(),
            P(),
            P("dp", ("hid", "mp")),
            P(),
            P(("hid", "mp"), "dp"),
            P(),
        ),
        out_specs=(
            P(("dp", "hid", "mp"), None),
            P(("dp", "hid", "mp"), None),
            P(),
            P(),
            P(("dp", "hid", "mp"), None),
            P(),
            P(("dp", "hid", "mp"), None),
            P(("dp", "hid", "mp"), None),
            P(),
            P(("dp", "hid", "mp"), None),
            P(),
            P(),
            P(),
            P("dp", ("hid", "mp")),
            P(),
            P(("hid", "mp"), "dp"),
            P(),
        ),
        check_vma=False,
    )
```

```python
import functools

import jax
import jax.numpy as jnp
from jax import lax
from jax.experimental import pallas as pl
from jax.experimental.pallas import tpu as pltpu
from jax.sharding import PartitionSpec as P

D = 768
HEADS = 12
HEAD = 64
CLUSTERS = 100
SEQ = 1024
PAD = 128


def matmul(left, right):
    return jnp.dot(left, right, preferred_element_type=jnp.float32)


def matmul_nt(left, right):
    return lax.dot_general(left, right, (((1,), (1,)), ((), ())), preferred_element_type=jnp.float32)


def matmul_tn(left, right):
    return lax.dot_general(left, right, (((0,), (0,)), ((), ())), preferred_element_type=jnp.float32)


def swapped(array, axis, mask):
    count = lax.axis_size(axis)
    return lax.ppermute(array, axis, [(i, i ^ mask) for i in range(count)])


def own_bit(axis, bit):
    return (lax.axis_index(axis) >> bit) & 1


def joined(own, other, mine, place):
    own, other = (jnp.expand_dims(own, place), jnp.expand_dims(other, place))
    shape = own.shape[:place] + (2,) + own.shape[place + 1 :]
    return jnp.where(lax.broadcasted_iota(jnp.int32, shape, place) == mine, own, other)


def halves(array, axis, bit, place):
    mine = own_bit(axis, bit)
    take = lambda k: lax.dynamic_index_in_dim(array, k, place, keepdims=False)
    return (take(mine), take(1 - mine))


def high_groups():
    count = lax.axis_size("dp").bit_length() - 1
    return [(b, min(2, count - b)) for b in range(1, count, 2)]


def exchanged(piece, group):
    shift, bits = group
    return [swapped(piece, "dp", d << shift) for d in range(1, 1 << bits)]


def lined_up(own, others, group, place):
    shift, bits = group
    mine = (lax.axis_index("dp") >> shift) & ((1 << bits) - 1)
    pieces = [jnp.expand_dims(p, place) for p in [own, *others]]
    shape = pieces[0].shape[:place] + (1 << bits,) + pieces[0].shape[place + 1 :]
    apart = lax.broadcasted_iota(jnp.int32, shape, place) ^ mine
    out = jnp.broadcast_to(pieces[-1], shape)
    for d in reversed(range(len(pieces) - 1)):
        out = jnp.where(apart == d, pieces[d], out)
    return out


def dealt(array, group, place):
    shift, bits = group
    mine = (lax.axis_index("dp") >> shift) & ((1 << bits) - 1)
    take = lambda k: lax.dynamic_index_in_dim(array, k, place, keepdims=False)
    return [take(mine)] + [swapped(take(mine ^ d), "dp", d << shift) for d in range(1, 1 << bits)]


def summed(pieces):
    return sum(p.astype(jnp.float32) for p in pieces)


def moments(values):
    middle = jnp.mean(values, axis=-1, keepdims=True)
    centered = values - middle
    spread = jnp.mean(centered * centered, axis=-1, keepdims=True)
    return (centered * lax.rsqrt(spread + 1e-05), lax.rsqrt(spread + 1e-05))


def norm_pull(grad, gain, unit, scale):
    scaled = grad * gain
    first = jnp.mean(scaled, axis=-1, keepdims=True)
    second = jnp.mean(scaled * unit, axis=-1, keepdims=True)
    return scale * (scaled - first - unit * second)


def gate_and_slope(v):
    size = jnp.abs(v)
    bell = jnp.exp(-0.5 * v * v)
    t = 1.0 / (1.0 + 0.23164189 * size)
    series = 0.7107068705 + t * (-0.7265760135 + t * 0.5307027145)
    tail = t * (0.127414796 + t * (-0.142248368 + t * series)) * bell
    phi = jnp.where(v < 0, tail, 1.0 - tail)
    return (v * phi, phi + v * (0.3989422804014327 * bell))


def ff_kernel(first, rows, places, *refs):
    x_in, cot_in, xt_in, cott_in, *weights, bu, branch_in = refs[:14]
    refs = refs[14:]
    if not first:
        mid_in, b_down = refs[:2]
        refs = refs[2:]
    branch_out, mid_out, *grads = refs[:6]
    dbu, x, cot, xt, cott, wu, wd, branch, mid, branch_old, mid_old, dw, sems = refs[6:]
    nt = (((1,), (1,)), ((), ()))
    parts = [pl.ds(r * rows, rows) for r in range(x.shape[0] // rows)]
    used = [0]

    def started(source, target):
        used[0] += 1
        made = pltpu.make_async_copy(source, target, sems.at[used[0] - 1])
        made.start()
        return made

    def finish(made):
        for one in made:
            one.wait()

    def fetch_weight(k, target):
        return [
            started(weights[2 * k + j].at[places[2 * k + j]], target.at[k // 2, pl.ds(j * (D // 2), D // 2)])
            for j in (0, 1)
        ]

    early = fetch_weight(0, wu) + [started(x_in, x)] + fetch_weight(1, wd) + [started(cot_in, cot)]
    finish(early)
    late = [started(cott_in, cott), started(xt_in, xt)] + fetch_weight(2, wu) + fetch_weight(3, wd)
    late.append(started(branch_in, branch_old))
    if not first:
        late.append(started(mid_in, mid_old))
    outs = []
    for block in (0, 1):
        hs, gs = ([], [])
        total = jnp.zeros((1, dbu.shape[1]), jnp.float32)
        for at in parts:
            pre = matmul(x[at, :], wu[block]) + bu[block : block + 1, :]
            grad_hidden = matmul(cot[at, :], wd[block])
            h, slope = gate_and_slope(pre)
            h = h.astype(jnp.bfloat16)
            g = (grad_hidden * slope).astype(jnp.bfloat16)
            total += jnp.sum(g.astype(jnp.float32), axis=0, keepdims=True)
            forth = lax.dot_general(h, wd[block], nt, preferred_element_type=jnp.float32)
            back = lax.dot_general(g, wu[block], nt, preferred_element_type=jnp.float32)
            if block:
                forth += branch[at, :] + branch_old[at, :]
                back += mid[at, :]
                if not first:
                    forth += b_down[3:4, :]
                    back += mid_old[at, :]
            if block and not first:
                x[at, :] = forth.astype(jnp.bfloat16)
            else:
                branch[at, :] = forth
            mid[at, :] = back
            hs.append(h)
            gs.append(g)
        dbu[block : block + 1, :] = total
        if block == 0:
            finish(late)
        else:
            outs += [started(branch if first else x, branch_out), started(mid, mid_out)]
        dw[block, 1] = matmul(cott[...], jnp.concatenate(hs, axis=0)).astype(jnp.bfloat16)
        outs.append(started(dw.at[block, 1], grads[2 * block + 1]))
        dw[block, 0] = matmul(xt[...], jnp.concatenate(gs, axis=0)).astype(jnp.bfloat16)
        outs.append(started(dw.at[block, 0], grads[2 * block]))
    finish(outs)


def ff_blocks(x, cot, xt, cott, halved, bu, residual, *sums):
    f32, bf = (jnp.float32, jnp.bfloat16)
    count, wide = (x.shape[0], bu.shape[1])
    weights, places = zip(*[half for weight in halved for half in weight])
    spec = pl.BlockSpec(memory_space=pltpu.VMEM)
    far = pl.BlockSpec(memory_space=pl.ANY)
    return pl.pallas_call(
        functools.partial(ff_kernel, not sums, 256, places),
        out_shape=(
            pltpu.HBM((count, D), bf if sums else f32),
            pltpu.HBM((count, D), f32),
            pltpu.HBM((D, wide), bf),
            pltpu.HBM((D, wide), bf),
            pltpu.HBM((D, wide), bf),
            pltpu.HBM((D, wide), bf),
            jax.ShapeDtypeStruct((2, wide), f32),
        ),
        in_specs=[far] * 12 + [spec, far] + [far, spec][: len(sums)],
        out_specs=(far,) * 6 + (spec,),
        scratch_shapes=[
            pltpu.VMEM((count, D), bf),
            pltpu.VMEM((count, D), bf),
            pltpu.VMEM((D, count), bf),
            pltpu.VMEM((D, count), bf),
            pltpu.VMEM((2, D, wide), bf),
            pltpu.VMEM((2, D, wide), bf),
            pltpu.VMEM((count, D), f32),
            pltpu.VMEM((count, D), f32),
            pltpu.VMEM((count, D), f32),
            pltpu.VMEM((count, D), f32),
            pltpu.VMEM((2, 2, D, wide), bf),
            pltpu.SemaphoreType.DMA((24,)),
        ],
        compiler_params=pltpu.CompilerParams(vmem_limit_bytes=60 * 1024 * 1024),
        cost_estimate=pl.CostEstimate(
            flops=24 * count * D * wide, bytes_accessed=8 * D * wide, transcendentals=4 * count * wide
        ),
        name="ff_blocks",
    )(x, cot, xt, cott, *weights, bu, residual, *sums)


STEP = 256
ROWS = pl.BlockSpec((STEP, D), lambda i: (i, 0))
WHOLE = pl.BlockSpec((D, D), lambda i: (0, 0))
LINES = pl.BlockSpec((8, D), lambda i: (0, 0))


def by_rows(kernel, name, in_specs, out_specs, out_shape, scratch, flops, moved):
    return pl.pallas_call(
        kernel,
        grid=(SEQ // STEP,),
        in_specs=in_specs,
        out_specs=out_specs,
        out_shape=out_shape,
        scratch_shapes=scratch,
        compiler_params=pltpu.CompilerParams(vmem_limit_bytes=60 * 1024 * 1024),
        cost_estimate=pl.CostEstimate(flops=flops, bytes_accessed=moved, transcendentals=SEQ),
        name=name,
    )


def middle_kernel(mixed, tokens, out_full, vectors, residual, x, x_t):
    b_out, gain, shift = (vectors.at[k : k + 1] for k in (0, 1, 2))
    value = tokens[...].astype(jnp.float32) + (matmul(mixed[...], out_full[...]) + b_out[...])
    residual[...] = value
    unit, _ = moments(value)
    normed = (unit * gain[...] + shift[...]).astype(jnp.bfloat16)
    x[...] = normed
    x_t[...] = normed.T


def middle(mixed, tokens, out_full, vectors):
    f32, bf = (jnp.float32, jnp.bfloat16)
    return by_rows(
        middle_kernel,
        "middle",
        [ROWS, ROWS, WHOLE, LINES],
        (ROWS, ROWS, pl.BlockSpec((D, STEP), lambda i: (0, i))),
        (pltpu.HBM((SEQ, D), f32), pltpu.HBM((SEQ, D), bf), pltpu.HBM((D, SEQ), bf)),
        [],
        SEQ,
        SEQ,
    )(mixed, tokens, out_full, vectors)


def add_lines(ref, lines):
    @pl.when(pl.program_id(0) == 0)
    def _():
        ref[...] = jnp.zeros_like(ref)

    sums = [jnp.sum(line.astype(jnp.float32), axis=0, keepdims=True) for line in lines]
    ref[: len(lines), :] += jnp.concatenate(sums, axis=0)


def turn_kernel(grad_mid, residual, cot, mixed, out_full, vectors, grad_resid, grad_mixed, out_grad, lines, held):
    value = residual[...]
    grad = grad_mid[...]
    unit, scale = moments(value)
    pulled = cot[...].astype(jnp.float32) + norm_pull(grad, vectors[1:2, :], unit, scale)
    grad_resid[...] = pulled
    low = pulled.astype(jnp.bfloat16)
    grad_mixed[...] = matmul_nt(low, out_full[...]).astype(jnp.bfloat16)
    add_lines(lines, [low, grad * unit, grad, cot[...]])

    @pl.when(pl.program_id(0) == 0)
    def _():
        held[...] = jnp.zeros_like(held)

    held[...] += matmul_tn(mixed[...], low)

    @pl.when(pl.program_id(0) == pl.num_programs(0) - 1)
    def _():
        out_grad[...] = held[...].astype(jnp.bfloat16)


def turn(grad_mid, residual, cot, mixed, out_full, vectors):
    f32, bf = (jnp.float32, jnp.bfloat16)
    low = jax.ShapeDtypeStruct((SEQ, D), bf)
    return by_rows(
        turn_kernel,
        "turn",
        [ROWS, ROWS, ROWS, ROWS, WHOLE, LINES],
        (ROWS, ROWS, WHOLE, LINES),
        (pltpu.HBM((SEQ, D), f32), low, pltpu.HBM((D, D), bf), jax.ShapeDtypeStruct((8, D), f32)),
        [pltpu.VMEM((D, D), f32)],
        SEQ,
        SEQ,
    )(grad_mid, residual, cot, mixed, out_full, vectors)


def last_kernel(gq, gk, gv, wq, wk, wv, tokens, grad_resid, vectors, tokens_grad, lines):
    grad = matmul_nt(gq[...], wq[...]) + matmul_nt(gk[...], wk[...]) + matmul_nt(gv[...], wv[...])
    unit, scale = moments(tokens[...].astype(jnp.float32))
    tokens_grad[...] = (grad_resid[...] + norm_pull(grad, vectors[4:5, :], unit, scale)).astype(jnp.bfloat16)
    add_lines(lines, [grad * unit, grad, gq[...], gv[...]])


def last(gq, gk, gv, wq, wk, wv, tokens, grad_resid, vectors):
    return by_rows(
        last_kernel,
        "last",
        [ROWS, ROWS, ROWS, WHOLE, WHOLE, WHOLE, ROWS, ROWS, LINES],
        (ROWS, LINES),
        (jax.ShapeDtypeStruct((SEQ, D), jnp.bfloat16), jax.ShapeDtypeStruct((8, D), jnp.float32)),
        [],
        SEQ,
        SEQ,
    )(gq, gk, gv, wq, wk, wv, tokens, grad_resid, vectors)


def tied(*arrays):
    return lax.optimization_barrier(arrays)


def packed(sent, small):
    high = small.astype(jnp.bfloat16)
    low = (small - high.astype(jnp.float32)).astype(jnp.bfloat16)
    return jnp.concatenate([sent.reshape(-1, D), high, low])


def unpacked(got, like):
    rows = like.size // D
    high, low = jnp.split(got[rows:].astype(jnp.float32), 2)
    return (got[:rows].reshape(like.shape), high + low)


def added(own, got):
    return (own.astype(jnp.float32) + got.astype(jnp.float32)).astype(jnp.bfloat16)


def dot(a, b, ca=1, cb=0):
    return lax.dot_general(a, b, (((ca,), (cb,)), ((), ())), preferred_element_type=jnp.float32)


def rounded_sum(pieces):
    return summed(pieces).astype(jnp.bfloat16)


def sum_halves(pieces, axis, bit, place):
    both = [halves(piece, axis, bit, place) for piece in pieces]
    return (rounded_sum([kept for kept, _ in both]), rounded_sum([sent for _, sent in both]))


def own_half(wide):
    rows = lax.broadcasted_iota(jnp.int32, wide.shape, 0) // PAD
    columns = lax.broadcasted_iota(jnp.int32, wide.shape, 1) // HEAD
    return jnp.where(rows == columns, wide, 0.0)


def pair_rows(ids):
    at = lax.broadcasted_iota(jnp.int32, (PAD, SEQ), 0)
    return jnp.concatenate([jnp.where(ids[k : k + 1, :] == at, 1.0, 0.0) for k in (0, 1)], axis=0).astype(jnp.bfloat16)


def pair_columns(ids):
    at = lax.broadcasted_iota(jnp.int32, (SEQ, PAD), 1)
    return jnp.concatenate([jnp.where(ids[:, k : k + 1] == at, 1.0, 0.0) for k in (0, 1)], axis=1).astype(jnp.bfloat16)


def attend_kernel(q, k, v, rows, columns, seg_row, seg_col, mixed, prob, centroid, count):
    bf = jnp.bfloat16
    hot = pair_rows(rows[0])
    lanes = lax.broadcasted_iota(jnp.int32, (SEQ, PAD), 1)
    marks = jnp.where(lanes == 0, seg_col[...], jnp.where(lanes == 1, 1.0, 0.0)).astype(bf)
    sums = dot(hot, jnp.concatenate([q[...], marks], axis=1))
    owner, counts = (sums[:, 128:129], sums[:, 129:130])
    counts = jnp.maximum(counts, 1.0)
    middle = own_half(sums[:, :128] / counts).astype(bf)
    scores = 0.125 * dot(middle, k[...], 1, 1)
    allowed = jnp.abs(owner - counts * seg_row[...]) < 0.5
    masked = jnp.where(allowed, scores, -1e30)
    highest = jnp.max(masked, axis=1, keepdims=True)
    exponent = jnp.where(allowed, jnp.exp(masked - highest), 0.0)
    total = jnp.sum(exponent, axis=1, keepdims=True)
    p = exponent * (1.0 / jnp.maximum(total, 1e-30))
    context = own_half(dot(p.astype(bf), v[...])).astype(bf)
    mixed[...] = dot(pair_columns(columns[0]), context).astype(bf)
    prob[0] = p
    centroid[0] = middle
    count[0] = jnp.broadcast_to(counts, (2 * PAD, 128))


def attend(q, k, v, rows, columns, seg_row, seg_col):
    bf = jnp.bfloat16
    pair = pl.BlockSpec((SEQ, 128), lambda i: (0, i))
    return pl.pallas_call(
        attend_kernel,
        grid=(HEADS // 2,),
        in_specs=[pair, pair, pair,
            pl.BlockSpec((1, 2, SEQ), lambda i: (i, 0, 0)),
            pl.BlockSpec((1, SEQ, 2), lambda i: (i, 0, 0)),
            pl.BlockSpec((1, SEQ), lambda i: (0, 0)),
            pl.BlockSpec((SEQ, 1), lambda i: (0, 0))],
        out_specs=(pair, pl.BlockSpec((1, 2 * PAD, SEQ), lambda i: (i, 0, 0)), pl.BlockSpec((1, 2 * PAD, 128), lambda i: (i, 0, 0)), pl.BlockSpec((1, 2 * PAD, 128), lambda i: (i, 0, 0))),
        out_shape=(pltpu.HBM((SEQ, D), bf), pltpu.HBM((HEADS // 2, 2 * PAD, SEQ), jnp.float32), pltpu.HBM((HEADS // 2, 2 * PAD, 128), bf), pltpu.HBM((HEADS // 2, 2 * PAD, 128), jnp.float32)),
        cost_estimate=pl.CostEstimate(flops=12 * 5 * 2 * PAD * SEQ * HEAD, bytes_accessed=14 << 20, transcendentals=HEADS * PAD * SEQ),
        compiler_params=pltpu.CompilerParams(vmem_limit_bytes=24 * 1024 * 1024),
        name="attend",
    )(q, k, v, rows, columns, seg_row, seg_col)


def attend_back_kernel(k, v, gm, rows, columns, prob, centroid, count, gq, gk, gv):
    bf = jnp.bfloat16
    hot = pair_rows(rows[0])
    p = prob[0]
    grad_context = own_half(dot(hot, gm[...])).astype(bf)
    gv[...] = dot(p.astype(bf), grad_context, 0, 0).astype(bf)
    grad_prob = dot(grad_context, v[...], 1, 1)
    grad_scores = (p * (grad_prob - jnp.sum(p * grad_prob, axis=1, keepdims=True))).astype(bf)
    grad_centroid = own_half(0.125 * dot(grad_scores, k[...]) / count[0]).astype(bf)
    gk[...] = (0.125 * dot(grad_scores, centroid[0], 0, 0)).astype(bf)
    gq[...] = dot(pair_columns(columns[0]), grad_centroid).astype(bf)


def attend_back(k, v, gm, rows, columns, prob, centroid, count):
    bf = jnp.bfloat16
    pair = pl.BlockSpec((SEQ, 128), lambda i: (0, i))
    wide = pl.BlockSpec((1, 2 * PAD, 128), lambda i: (i, 0, 0))
    out = pltpu.HBM((SEQ, D), bf)
    return pl.pallas_call(
        attend_back_kernel,
        grid=(HEADS // 2,),
        in_specs=[pair, pair, pair,
            pl.BlockSpec((1, 2, SEQ), lambda i: (i, 0, 0)),
            pl.BlockSpec((1, SEQ, 2), lambda i: (i, 0, 0)),
            pl.BlockSpec((1, 2 * PAD, SEQ), lambda i: (i, 0, 0)), wide, wide],
        out_specs=(pair, pair, pair),
        out_shape=(out, out, out),
        cost_estimate=pl.CostEstimate(flops=SEQ, bytes_accessed=SEQ, transcendentals=0),
        compiler_params=pltpu.CompilerParams(vmem_limit_bytes=60 * 1024 * 1024),
        name="attend_back",
    )(k, v, gm, rows, columns, prob, centroid, count)


def shards(
    tokens,
    segment_ids,
    cluster_ids,
    cotangent,
    first_gain,
    first_shift,
    w_query,
    b_query,
    w_key,
    w_value,
    b_value,
    w_out,
    b_out,
    second_gain,
    second_shift,
    w_up,
    b_up,
    w_down,
    b_down,
):
    groups = high_groups()
    tops = 1 << sum(bits for _, bits in groups)
    bf = jnp.bfloat16
    part = D // (8 * tops)
    wide = D // (2 * tops)
    whole = [1 << bits for _, bits in reversed(groups)]

    attn = jnp.stack([w.astype(bf) for w in (w_query, w_key, w_value, w_out)])
    up, down = (w_up.astype(bf), w_down.T.astype(bf))
    unit_in, _ = moments(tokens.astype(jnp.float32))
    normed_in = (unit_in * first_gain + first_shift).astype(bf)
    id_rows = cluster_ids.reshape(HEADS // 2, 2, SEQ)
    id_columns = id_rows.transpose(0, 2, 1)
    seg = segment_ids.astype(jnp.float32)
    seg_row, seg_col = (seg[None, :], seg[:, None])
    cot_t = cotangent.T
    vectors = jnp.stack([b_out, second_gain, second_shift, b_down, first_gain, first_gain, first_gain, first_gain])
    me = lax.axis_index(("hid", "mp"))
    biases = lambda blocks: jnp.stack([lax.dynamic_slice_in_dim(b_up, block * D, D) for block in blocks])
    far_up, near_up = (biases((me ^ 3, me ^ 2)), biases((me ^ 1, me)))
    for group in groups:
        got = exchanged(attn, group)
        normed_in, id_columns, seg_col, vectors, far_up, near_up, *got = tied(
            normed_in, id_columns, seg_col, vectors, far_up, near_up, *got
        )
        attn = lined_up(attn, got, group, 1)
    attn = attn.reshape(4, tops, part, D)
    first, second = (attn[:2], attn[2:])
    first_got, second_got = (swapped(first, "dp", 1), swapped(second, "hid", 1))
    for group in groups[:-1]:
        up = lined_up(up, exchanged(up, group), group, 0)
        down = lined_up(down, exchanged(down, group), group, 0)
    up_got, down_got = (exchanged(up, groups[-1]), exchanged(down, groups[-1]))
    cot_t, first_got, second_got, *up_got = tied(cot_t, first_got, second_got, *up_got)
    first = joined(first, first_got, own_bit("dp", 0), 2)
    second = joined(second, second_got, own_bit("hid", 0), 2)
    first_got, second_got = (swapped(first, "hid", 1), swapped(second, "dp", 1))
    first_got, second_got, *down_got = tied(first_got, second_got, *down_got)
    half = tops // 2
    up = lined_up(up, up_got, groups[-1], 0).reshape(tops, wide, D)
    up_one, up_two = (up[:half], up[half:])
    up_one_got, up_two_got = (swapped(up_one, "dp", 1), swapped(up_two, "hid", 1))
    down = lined_up(down, down_got, groups[-1], 0).reshape(tops, wide, D)
    down_one, down_two = (down[:half], down[half:])
    down_one_got, down_two_got = (swapped(down_one, "dp", 1), swapped(down_two, "hid", 1))
    first = joined(first, first_got, own_bit("hid", 0), 3)
    second = joined(second, second_got, own_bit("dp", 0), 2)
    first_got, second_got = (swapped(first, "mp", 1), swapped(second, "mp", 1))
    first = joined(first, first_got, own_bit("mp", 0), 4)
    second = joined(second, second_got, own_bit("mp", 0), 4)
    query_full, key_full = first.reshape(2, D, D)
    value_full, out_full = second.reshape(2, D, D)

    value_rows = (matmul(normed_in, value_full) + b_value).astype(bf)
    value_rows, normed, up_one_got, up_two_got = tied(value_rows, normed_in, up_one_got, up_two_got)
    up_one, up_two = (joined(up_one, up_one_got, own_bit("dp", 0), 1), jnp.stack([up_two, up_two_got]))
    up_one_got, up_two_got = (swapped(up_one, "hid", 1), swapped(up_two, "dp", 1))
    key_rows = matmul(normed, key_full).astype(bf)
    query = (matmul(normed, query_full) + b_query).astype(bf)
    key_rows, down_one_got, down_two_got = tied(key_rows, down_one_got, down_two_got)
    down_one, down_two = (joined(down_one, down_one_got, own_bit("dp", 0), 1), jnp.stack([down_two, down_two_got]))
    down_one_got, down_two_got = (swapped(down_one, "hid", 1), swapped(down_two, "dp", 1))
    mixed, probability, centroid, counts = attend(
        query, key_rows, value_rows, id_rows, id_columns, seg_row, seg_col
    )
    mixed, up_one_got, up_two_got = tied(mixed, up_one_got, up_two_got)
    up_two = joined(up_two, up_two_got, own_bit("dp", 0), 2)
    rows = lambda piece: piece.reshape(-1, D // 2, D)
    up_one, up_mate, up_two = (rows(up_one), rows(up_one_got), rows(up_two))
    up_one_next, up_mate_next, up_two_next = [swapped(piece, "mp", 1) for piece in (up_one, up_mate, up_two)]
    residual, x, x_t = middle(mixed, tokens, out_full, vectors)
    x, x_t, down_one_got, down_two_got = tied(x, x_t, down_one_got, down_two_got)
    down_two = joined(down_two, down_two_got, own_bit("dp", 0), 2)
    down_one, down_mate, down_two = (rows(down_one), rows(down_one_got), rows(down_two))
    down_mate_next, down_two_next, down_one_next = [swapped(piece, "mp", 1) for piece in (down_mate, down_two, down_one)]
    pick = lambda one, two, place: ((one, 0), (two, place))
    split = lambda piece: piece.reshape(tops, 2, wide, D)
    branch, grad_mid, up_send, down_send, up_own, down_own, far_bias = ff_blocks(
        x,
        cotangent,
        x_t,
        cot_t,
        [
            pick(up_mate_next, up_two_next, 1),
            pick(down_mate_next, down_two_next, 1),
            pick(up_mate, up_two, 1),
            pick(down_mate, down_two, 1),
        ],
        far_up,
        residual,
    )
    up_far = added(up_own, swapped(up_send, "mp", 1))
    down_far, down_sent = sum_halves([split(down_own), split(swapped(down_send, "mp", 1))], "dp", 0, 1)
    branch, grad_mid, up_far, down_sent = tied(branch, grad_mid, up_far, down_sent)
    up_far_got = swapped(up_far, "hid", 1)
    down_far_got = swapped(down_sent, "dp", 1)
    output, grad_mid, up_send, down_send, up_own, down_own, near_bias = ff_blocks(
        x,
        cotangent,
        x_t,
        cot_t,
        [
            pick(up_one_next, up_two_next, 0),
            pick(down_one_next, down_two_next, 0),
            pick(up_one, up_two, 0),
            pick(down_one, down_two, 0),
        ],
        near_up,
        branch,
        grad_mid,
        vectors,
    )
    grad_mid, up_send, down_send, up_far_got, down_far_got = tied(grad_mid, up_send, down_send, up_far_got, down_far_got)
    up_near_got, down_near_got = (swapped(up_send, "mp", 1), swapped(down_send, "mp", 1))
    bias_up = jnp.zeros((4, D), jnp.float32)
    for block, bias in ((me ^ 3, far_bias[:1]), (me ^ 2, far_bias[1:]), (me ^ 1, near_bias[:1]), (me, near_bias[1:])):
        bias_up = lax.dynamic_update_slice(bias_up, bias, (block, 0))
    down_far = added(down_far, down_far_got)
    grad_mid, down_far = tied(grad_mid, down_far)
    down_got = swapped(down_far, "hid", 1)

    grad_resid, grad_mixed, out_grad, turn_lines = turn(grad_mid, residual, cotangent, mixed, out_full, vectors)
    grad_mixed, up_near_got, down_near_got = tied(grad_mixed, up_near_got, down_near_got)
    down_near, down_sent = sum_halves([split(down_own), split(down_near_got)], "dp", 0, 1)
    up_near, up_sent = sum_halves([split(up_own), split(up_near_got), split(up_far_got)], "dp", 0, 1)
    grad_mixed, down_sent, up_sent = tied(grad_mixed, down_sent, up_sent)
    down_near_got = swapped(down_sent, "dp", 1)
    up_got = swapped(up_sent, "dp", 1)

    grad_query, grad_key, grad_value = attend_back(
        key_rows, value_rows, grad_mixed, id_rows, id_columns, probability, centroid, counts
    )
    grad_value, down_got, down_near_got = tied(grad_value, down_got, down_near_got)
    down_sum = rounded_sum([down_near, down_near_got, down_got]).reshape(*whole, wide, D)

    query_grad = matmul_tn(normed_in, grad_query).astype(bf)
    key_grad = matmul_tn(normed_in, grad_key).astype(bf)
    value_grad = matmul_tn(normed_in, grad_value).astype(bf)
    both = jnp.stack([query_grad, key_grad, value_grad, out_grad]).reshape(4, tops, 2, 2, 2, part, D)
    both, sent = halves(both, "mp", 0, 4)
    both, sent, up_got = tied(both, sent, up_got)
    got = swapped(sent, "mp", 1)
    ff_parts = dealt(jnp.stack([added(up_near, up_got).reshape(*whole, wide, D), down_sum]), groups[-1], 1)
    both = added(both, got)
    one, one_sent = halves(both[:2], "dp", 0, 2)
    two, two_sent = halves(both[2:], "hid", 0, 3)
    grad_resid, one_sent, two_sent, ff_parts[0] = tied(grad_resid, one_sent, two_sent, ff_parts[0])
    one_got, two_got = (swapped(one_sent, "dp", 1), swapped(two_sent, "hid", 1))
    tokens_grad, last_lines = last(
        grad_query, grad_key, grad_value, query_full, key_full, value_full, tokens, grad_resid, vectors
    )
    small = jnp.concatenate([last_lines[:4], turn_lines[:4], bias_up])
    small, one_got, two_got, *ff_parts = tied(small, one_got, two_got, *ff_parts)
    small = small + swapped(small, "mp", 1)
    small = small + swapped(small, "dp", 1)
    one, one_sent = halves(added(one, one_got), "hid", 0, 2)
    two, two_sent = halves(added(two, two_got), "dp", 0, 2)
    got, two_got = (swapped(packed(one_sent, small), "hid", 1), swapped(two_sent, "dp", 1))
    one_got, small_got = unpacked(got, one_sent)
    small = small + small_got
    both = jnp.stack([added(one, one_got), added(two, two_got)]).reshape(4, *whole, part, D)
    for group in reversed(groups):
        shift, bits = group
        mine = (lax.axis_index("dp") >> shift) & ((1 << bits) - 1)
        take = lambda k: lax.dynamic_index_in_dim(both, k, 1, keepdims=False)
        got = [swapped(packed(take(mine ^ d), small), "dp", d << shift) for d in range(1, 1 << bits)]
        pieces = [unpacked(g, take(mine)) for g in got]
        sums = summed([take(mine)] + [piece for piece, _ in pieces])
        small = summed([small] + [piece for _, piece in pieces])
        both = sums.astype(bf)
    for group in reversed(groups[:-1]):
        ff_parts = dealt(rounded_sum(ff_parts), group, 1)
    up_grad, down_grad = summed(ff_parts)
    down_grad = down_grad.T
    query_sum, key_sum, value_sum, out_sum = sums
    return (
        output,
        tokens_grad,
        small[0],
        small[1],
        query_sum,
        small[2],
        key_sum,
        value_sum,
        small[3],
        out_sum,
        small[4],
        small[5],
        small[6],
        up_grad,
        small[8:].reshape(-1),
        down_grad,
        small[7],
    )


def solution(mesh):
    return jax.shard_map(
        shards,
        mesh=mesh,
        in_specs=(
            P(("dp", "hid", "mp"), None),
            P(("dp", "hid", "mp")),
            P(None, ("dp", "hid", "mp")),
            P(("dp", "hid", "mp"), None),
            P(),
            P(),
            P(("dp", "hid", "mp"), None),
            P(),
            P(("dp", "hid", "mp"), None),
            P(("dp", "hid", "mp"), None),
            P(),
            P(("dp", "hid", "mp"), None),
            P(),
            P(),
            P(),
            P("dp", ("hid", "mp")),
            P(),
            P(("hid", "mp"), "dp"),
            P(),
        ),
        out_specs=(
            P(("dp", "hid", "mp"), None),
            P(("dp", "hid", "mp"), None),
            P(),
            P(),
            P(("dp", "hid", "mp"), None),
            P(),
            P(("dp", "hid", "mp"), None),
            P(("dp", "hid", "mp"), None),
            P(),
            P(("dp", "hid", "mp"), None),
            P(),
            P(),
            P(),
            P("dp", ("hid", "mp")),
            P(),
            P(("hid", "mp"), "dp"),
            P(),
        ),
        check_vma=False,
    )
```
